256 devices in a mesh: seq: 32 (over x, z), head: 8 (over y, core).
Axes of the slice: x: 4, y: 4, z: 8, core: 2. Of those that a mesh axis runs over, the one named last changes fastest.
Arguments:
- queries: bfloat16 [4096, 8192], P('seq', 'head'), may hold values from -250 to 250
- key_vectors: bfloat16 [4096, 1024], P('seq', 'head'), may hold values from -250 to 250
- value_vectors: bfloat16 [4096, 1024], P('seq', 'head'), may hold values from -20 to 20
- positions: int32 [4096], P('seq'), may hold values from 0 to 2047, as said below
- query_map: float32 [64, 128, 128], P('head'), may hold values from -0.5 to 0.5
- key_map: float32 [8, 128, 128], P('head'), may hold values from -0.5 to 0.5
Outputs:
- grad_queries: float32 [4096, 8192], P('seq', 'head')
- grad_keys: float32 [4096, 1024], P('seq', 'head')
- grad_values: float32 [4096, 1024], P('seq', 'head')
- query_map_grad: float32 [64, 128, 128], P('head')
- key_map_grad: float32 [8, 128, 128], P('head')
The draws below stay inside these ranges and needn't reach their ends.
Inputs may be any that keep to these rules, and one draw needn't show every extreme that they name: positions[0] is 0, and each later position is either 0 (a document begins) or one more than the position before it; the slab holds at most 4 documents, and one of them is exactly 2048 tokens long.
All inputs are finite; a program needn't handle non-finite values.
Results may differ from the reference program's by a relative error of at most 0.0025.
Values may be sent and summed in bfloat16 or wider, within the bound.
No kernel may reach another device: no remote copies, remote signals or barrier semaphores. Data moves between devices by JAX's collectives and lax.ppermute only.
A program may use at most 64 MiB of HBM per device.

```python
import math
import jax
import jax.numpy as jnp
from jax import lax

HD = 128
GROUP = 8
FH = 128
TOK_DEV = 128
KV = 8
HEADS = 64
TOKENS = 4096


def attention_draw(key):
    base_key = jax.random.fold_in(key, 101)
    q_key, k_key = jax.random.split(base_key, 2)
    queries = jnp.clip(jax.random.normal(q_key, (TOKENS, KV, GROUP, HD), jnp.float32), -6.0, 6.0)
    key_rows = jnp.clip(jax.random.normal(k_key, (TOKENS, KV, HD), jnp.float32), -6.0, 6.0)
    queries = jnp.clip(queries, -250.0, 250.0).reshape(TOKENS, HEADS * HD)
    key_rows = jnp.clip(key_rows, -250.0, 250.0).reshape(TOKENS, KV * HD)
    return (queries, key_rows)


def draw_queries(key, part):
    return attention_draw(key)[0].astype(jnp.bfloat16)


def draw_key_vectors(key, part):
    return attention_draw(key)[1].astype(jnp.bfloat16)


def draw_value_vectors(key, part):
    noise_key, scale_key = jax.random.split(jax.random.fold_in(key, 23))
    noise = jnp.clip(jax.random.normal(noise_key, (TOKENS, KV, HD), jnp.float32), -6.0, 6.0)
    scales = jnp.exp(jax.random.uniform(scale_key, (KV,), jnp.float32, 0.0, math.log(3.0)))
    return (noise * scales[None, :, None]).reshape(TOKENS, KV * HD).astype(jnp.bfloat16)


def draw_positions(key, part):
    first_key, inner_key = jax.random.split(jax.random.fold_in(key, 5))
    half_len = TOKENS // 2
    first_cut = jax.random.randint(first_key, (), 1, half_len)
    inner_cut = jax.random.randint(inner_key, (), 1, jnp.maximum(first_cut, 2))
    cut_points = jnp.stack([inner_cut, first_cut, first_cut + half_len]).astype(jnp.int32)
    row_index = jnp.arange(TOKENS, dtype=jnp.int32)
    reached = cut_points[None, :] <= row_index[:, None]
    starts = jnp.max(jnp.where(reached, cut_points[None, :], 0), axis=1)
    return (row_index - starts).astype(jnp.int32)


def steps_of(own_key, extent, cuts, least, high):
    def one(dim, parts):
        heights = jax.random.uniform(jax.random.fold_in(jax.random.fold_in(own_key, 6), dim), (parts,), jnp.float32, least / len(cuts), high / len(cuts))
        return jnp.repeat(jnp.exp(heights), extent[dim] // parts).reshape((-1,) + (1,) * (len(extent) - dim - 1))

    gain = one(*cuts[0])
    for cut in cuts[1:]:
        gain = gain * one(*cut)
    return gain


def gaussian(own_key, shape, deviation, reach, cuts=(), held_as=jnp.bfloat16):
    values = jax.random.normal(own_key, shape, jnp.float32) * deviation
    if len(cuts) > 0:
        values = steps_of(own_key, shape, cuts, -0.22, 0.18) * values
    return jnp.clip(values, min=-reach, max=reach).astype(held_as)


def setup_inputs(seed: int = 0) -> dict:
    splits = jax.random.split(jax.random.key(seed), 7)
    queries = draw_queries(jax.random.fold_in(splits[6], 71), 0)
    key_vectors = draw_key_vectors(jax.random.fold_in(splits[6], 71), 0)
    value_vectors = draw_value_vectors(jax.random.fold_in(splits[6], 71), 0)
    positions = draw_positions(jax.random.fold_in(splits[6], 71), 0)
    query_map = gaussian(splits[4], (HEADS, HD, FH), HD ** -0.5, 0.5, ((0, 8),), jnp.float32)
    key_map = gaussian(splits[5], (KV, HD, FH), HD ** -0.5, 0.5, ((0, 8),), jnp.float32)
    return dict(queries=queries, key_vectors=key_vectors, value_vectors=value_vectors, positions=positions, query_map=query_map, key_map=key_map)


HIGHEST = lax.Precision.HIGHEST
NEGATIVE = -1e+30

def feature_map(logits):
    return jnp.concatenate([jax.nn.softmax(logits, axis=-1), jax.nn.softmax(-logits, axis=-1)], axis=-1)

def teacher_attention(queries, key_vectors, value_vectors, starts):
    q_heads = queries.astype(jnp.float32).reshape(TOKENS, KV, GROUP, HD)
    k_heads = key_vectors.astype(jnp.float32).reshape(TOKENS, KV, HD)
    v_heads = value_vectors.astype(jnp.float32).reshape(TOKENS, KV, HD)
    block_len = min(512, TOKENS)
    blocks = TOKENS // block_len
    scaling = 1.0 / math.sqrt(HD)

    def one_block(q_block):
        q_first = (q_block * block_len).astype(jnp.int32)
        q_part = lax.dynamic_slice_in_dim(q_heads, q_first, block_len, 0)
        s_part = lax.dynamic_slice_in_dim(starts, q_first, block_len, 0)
        q_index = q_first + jnp.arange(block_len, dtype=jnp.int32)

        def key_step(running, k_block):
            k_first = (k_block * block_len).astype(jnp.int32)

            def update(current):
                run_max, row_sum, summed = current
                k_part = lax.dynamic_slice_in_dim(k_heads, k_first, block_len, 0)
                v_part = lax.dynamic_slice_in_dim(v_heads, k_first, block_len, 0)
                k_index = k_first + jnp.arange(block_len, dtype=jnp.int32)
                visible = (k_index[None, :] <= q_index[:, None]) & (k_index[None, :] >= s_part[:, None])
                scores = jnp.einsum('tkgd,nkd->kgtn', q_part, k_part, precision=HIGHEST) * scaling
                scores = jnp.where(visible, scores, NEGATIVE)
                new_max = jnp.maximum(run_max, lax.optimization_barrier(jnp.max(scores, axis=-1)))
                weights = jnp.where(visible, jnp.exp(scores - new_max[..., None]), 0.0)
                fading = jnp.exp(run_max - new_max)
                row_sum = row_sum * fading + lax.optimization_barrier(jnp.sum(weights, axis=-1))
                rounded = lax.optimization_barrier(weights.astype(jnp.bfloat16)).astype(jnp.float32)
                summed = summed * fading[..., None] + jnp.einsum('kgtn,nkd->kgtd', rounded, v_part, precision=HIGHEST)
                return (new_max, row_sum, summed)
            return (lax.cond(k_first <= q_first + block_len - 1, update, lambda current: current, running), None)
        initial = (jnp.full((KV, GROUP, block_len), NEGATIVE, jnp.float32), jnp.zeros((KV, GROUP, block_len), jnp.float32), jnp.zeros((KV, GROUP, block_len, HD), jnp.float32))
        finals, unused = lax.scan(key_step, initial, jnp.arange(blocks, dtype=jnp.int32))
        return finals[2] / finals[1][..., None]
    outputs = lax.map(one_block, jnp.arange(blocks, dtype=jnp.int32))
    return jnp.transpose(outputs, (0, 3, 1, 2, 4)).reshape(TOKENS, KV, GROUP, HD)

def student(query_float, key_float, value_float, q_weights, k_weights, starts):
    q_logits = jnp.einsum('tkgd,kgdf->tkgf', query_float.reshape(TOKENS, KV, GROUP, HD), q_weights.reshape(KV, GROUP, HD, FH), precision=HIGHEST)
    query_phi = feature_map(q_logits)
    k_logits = jnp.einsum('tkd,kdf->tkf', key_float.reshape(TOKENS, KV, HD), k_weights, precision=HIGHEST)
    key_phi = feature_map(k_logits)
    v_heads = value_float.reshape(TOKENS, KV, HD)
    spans = TOKENS // TOK_DEV
    feat_width = 2 * FH
    inputs = (query_phi.reshape(spans, TOK_DEV, KV, GROUP, feat_width), key_phi.reshape(spans, TOK_DEV, KV, feat_width), v_heads.reshape(spans, TOK_DEV, KV, HD), starts.reshape(spans, TOK_DEV), jnp.arange(spans, dtype=jnp.int32) * TOK_DEV)

    def span_step(running, pieces):
        state_sum, norm_sums = running
        q_phi, k_phi, v_rows, s_rows, row_base = pieces
        row_index = row_base + jnp.arange(TOK_DEV, dtype=jnp.int32)
        visible = ((row_index[None, :] <= row_index[:, None]) & (row_index[None, :] >= s_rows[:, None])).astype(jnp.float32)
        crossing = (s_rows < row_base).astype(jnp.float32)
        inner = jnp.einsum('ikgf,jkf->kgij', q_phi, k_phi, precision=HIGHEST) * visible
        numer = jnp.einsum('kgij,jkd->ikgd', inner, v_rows, precision=HIGHEST)
        numer = numer + crossing[:, None, None, None] * jnp.einsum('ikgf,kfd->ikgd', q_phi, state_sum, precision=HIGHEST)
        denom = jnp.einsum('kgij->ikg', inner) + crossing[:, None, None] * jnp.einsum('ikgf,kf->ikg', q_phi, norm_sums, precision=HIGHEST)
        outputs = numer / denom[..., None]
        last_start = s_rows[-1]
        keeping = (s_rows == last_start).astype(jnp.float32)
        carried = (last_start < row_base).astype(jnp.float32)
        kept_phi = k_phi * keeping[:, None, None]
        state_sum = carried * state_sum + jnp.einsum('jkf,jkd->kfd', kept_phi, v_rows, precision=HIGHEST)
        norm_sums = carried * norm_sums + lax.optimization_barrier(jnp.sum(kept_phi, axis=0))
        return ((state_sum, norm_sums), outputs)
    initial = (jnp.zeros((KV, feat_width, HD), jnp.float32), jnp.zeros((KV, feat_width), jnp.float32))
    finals, outputs = lax.scan(span_step, initial, inputs)
    return outputs.reshape(TOKENS, KV, GROUP, HD)

def reference(queries, key_vectors, value_vectors, positions, query_map, key_map):
    starts = jnp.arange(TOKENS, dtype=jnp.int32) - positions.astype(jnp.int32)
    teacher = teacher_attention(queries, key_vectors, value_vectors, starts)

    def energy(query_float, key_float, value_float, q_weights, k_weights):
        outputs = student(query_float, key_float, value_float, q_weights, k_weights, starts)
        return 0.5 * jnp.sum((outputs - teacher) ** 2)
    grads = jax.grad(energy, argnums=(0, 1, 2, 3, 4))(queries.astype(jnp.float32), key_vectors.astype(jnp.float32), value_vectors.astype(jnp.float32), query_map, key_map)
    grad_norm = jnp.sqrt(jnp.sum(grads[3] * grads[3]) + jnp.sum(grads[4] * grads[4]))
    clip_limit = 0.25 * math.sqrt((HEADS + KV) * HD * FH)
    factor = jnp.minimum(1.0, clip_limit / (grad_norm + 1e-06))
    return (grads[0], grads[1], grads[2], factor * grads[3], factor * grads[4])
```

```python
import functools
import math

import jax
import jax.numpy as jnp
from jax import lax
from jax.experimental import pallas as pl
from jax.experimental.pallas import tpu as pltpu
from jax.sharding import PartitionSpec as P

F32 = jnp.float32
BF16 = jnp.bfloat16
NEGATIVE = -1e30
EPSILON = 1e-06
T = 128
WINDOW = 16
KEYS = (WINDOW + 1) * T
PER_STEP = 2
ROWS = PER_STEP * T
PIECE = 48
STATE_ROW, KMAP_ROW, NORM_ROW, INFO_ROW = 32, 40, 44, 46


def nn(a, b):
    return lax.dot_general(a, b, (((1,), (0,)), ((), ())), preferred_element_type=F32)


def nt(a, b):
    return lax.dot_general(a, b, (((1,), (1,)), ((), ())), preferred_element_type=F32)


def tn(a, b):
    return lax.dot_general(a, b, (((0,), (0,)), ((), ())), preferred_element_type=F32)


def split2(x):
    high = x.astype(BF16)
    return high, (x - high.astype(F32)).astype(BF16)


def split3(x):
    high = x.astype(BF16)
    rest = x - high.astype(F32)
    middle = rest.astype(BF16)
    return high, middle, (rest - middle.astype(F32)).astype(BF16)


def product(form, a, b):
    return form(a[0], b[0]) + (form(a[0], b[1]) + form(a[1], b[0]))


def exact_left(form, a, parts):
    total = form(a, parts[-1])
    for part in parts[-2::-1]:
        total = total + form(a, part)
    return total


def exact_right(form, parts, b):
    return form(parts[0], b) + form(parts[1], b)


def feature_map(logits):
    upper = jnp.exp(logits - jnp.max(logits, axis=-1, keepdims=True))
    lower = jnp.exp(jnp.min(logits, axis=-1, keepdims=True) - logits)
    upper = upper * (1.0 / jnp.sum(upper, axis=-1, keepdims=True))
    lower = lower * (1.0 / jnp.sum(lower, axis=-1, keepdims=True))
    return upper, lower


def feature_back(phi, grad):
    upper, lower = phi[:, :T], phi[:, T:]
    up, low = grad[:, :T], grad[:, T:]
    up = upper * (up - jnp.sum(upper * up, axis=-1, keepdims=True))
    low = lower * (low - jnp.sum(lower * low, axis=-1, keepdims=True))
    return up - low


def column_of(row):
    i = lax.broadcasted_iota(jnp.int32, (T, T), 0)
    j = lax.broadcasted_iota(jnp.int32, (T, T), 1)
    return jnp.sum(jnp.where(i == j, row, 0.0), axis=1, keepdims=True)


def main_kernel(
    places,
    pos_ref,
    q_ref,
    qmap_ref,
    kmap_ref,
    *rest,
):
    count = len(places)
    blocks = rest[:count]
    gq_ref, payload_ref, phi_ref, gkphi_ref, gv_ref = rest[count : count + 5]
    k_s, v_s, phi_s, bias_s, s_s, n_s, back_s, backn_s = rest[count + 5 :]
    step = pl.program_id(0)
    last = pl.num_programs(0) - 1
    pos = column_of(pos_ref[...].astype(F32))
    row = lax.broadcasted_iota(jnp.int32, (T, 1), 0).astype(F32)
    start = row - pos
    crossing = (start < 0.0).astype(F32)
    entry = -pos_ref[0:1, 0:1].astype(F32)

    @pl.when(step == 0)
    def _():
        for ref, held in zip(blocks, places):
            for slot, block in enumerate(held):
                at = (WINDOW - block) * T
                k_s[at : at + T, :] = ref[slot * 2 * T : slot * 2 * T + T, :]
                v_s[at : at + T, :] = ref[slot * 2 * T + T : slot * 2 * T + 2 * T, :]
        key = lax.broadcasted_iota(jnp.int32, (T, KEYS), 1).astype(F32) - float(WINDOW * T)
        bias_s[...] = jnp.where((key <= row) & (key >= start), 0.0, NEGATIVE)
        map_parts = split3(kmap_ref[0])
        s_s[...] = jnp.zeros_like(s_s)
        n_s[...] = jnp.zeros_like(n_s)
        back_s[...] = jnp.zeros_like(back_s)
        backn_s[...] = jnp.zeros_like(backn_s)
        gkphi_ref[...] = jnp.zeros_like(gkphi_ref)
        gv_ref[...] = jnp.zeros_like(gv_ref)

        def features(at):
            logits = exact_left(nn, k_s[pl.ds(at, T), :], map_parts)
            return jnp.concatenate(feature_map(logits), axis=1)

        def lap(block, carry):
            at = pl.multiple_of(block * T, T)
            key_row = row + (at - WINDOW * T).astype(F32)
            phi = jnp.where(key_row >= entry, features(at), 0.0)
            phi_s[pl.ds(at, T), :] = phi
            s_s[...] += exact_right(tn, split2(phi), v_s[pl.ds(at, T), :])
            n_s[...] += jnp.sum(phi, axis=0, keepdims=True)
            return carry

        lax.fori_loop(0, WINDOW, lap, 0)
        own = features(WINDOW * T)
        phi_s[WINDOW * T :, :] = own
        phi_ref[...] = own

    both = lambda x: jnp.concatenate([x] * PER_STEP, axis=0)
    cross = both(crossing)
    own_v = v_s[WINDOW * T :, :]
    own_phi = split2(phi_s[WINDOW * T :, :])
    state = split2(s_s[...])
    norms = n_s[...]
    bias = bias_s[...]
    seen = both((bias[:, WINDOW * T :] == 0.0).astype(F32))

    heads = [q_ref[:, i * T : (i + 1) * T] for i in range(PER_STEP)]
    queries = jnp.concatenate(heads, axis=0)
    scores = nt(queries, k_s[...]) * (1.0 / math.sqrt(T)) + both(bias)
    weights = jnp.exp(scores - jnp.max(scores, axis=-1, keepdims=True))
    total = jnp.sum(weights, axis=-1, keepdims=True)
    teacher = nn(weights.astype(BF16), v_s[...]) / total
    logits = jnp.concatenate(
        [exact_left(nn, heads[i], split3(qmap_ref[i])) for i in range(PER_STEP)], axis=0
    )
    phi = jnp.concatenate(feature_map(logits), axis=1)
    phi_parts = split2(phi)
    inner = product(nt, phi_parts, own_phi) * seen
    inner_parts = split2(inner)
    numer = exact_right(nn, inner_parts, own_v) + cross * product(nn, phi_parts, state)
    denom = jnp.sum(inner, axis=-1, keepdims=True) + cross * jnp.sum(
        phi * norms, axis=-1, keepdims=True
    )
    outputs = numer / denom
    error = outputs - teacher
    grad_numer = error / denom
    grad_denom = -jnp.sum(error * outputs, axis=-1, keepdims=True) / denom
    numer_parts = split2(grad_numer)
    far_numer = cross * grad_numer
    far_parts = split2(far_numer)
    far_denom = cross * grad_denom
    mixing = (exact_right(nt, numer_parts, own_v) + grad_denom) * seen
    mixing_parts = split2(mixing)
    grad_phi = (
        product(nn, mixing_parts, own_phi) + product(nt, far_parts, state) + far_denom * norms
    )
    back_s[...] += product(tn, phi_parts, far_parts)
    backn_s[...] += jnp.sum(phi * far_denom, axis=0, keepdims=True)
    gkphi_ref[...] += product(tn, mixing_parts, phi_parts)
    gv_ref[...] += product(tn, inner_parts, numer_parts)
    dlogit = feature_back(phi, grad_phi)
    for i in range(PER_STEP):
        part = split2(dlogit[i * T : (i + 1) * T, :])
        gq_ref[:, i * T : (i + 1) * T] = product(nt, part, split2(qmap_ref[i]))
        grad_map = exact_left(tn, heads[i], part)
        for quarter in range(4):
            payload_ref[step * (4 * PER_STEP) + 4 * i + quarter, 0:STATE_ROW, :] = grad_map[
                quarter * 32 : quarter * 32 + 32, :
            ]

    @pl.when(step == last)
    def _():
        back = back_s[...]
        back_parts = split2(back)
        backn = backn_s[...]
        for piece in range(32):
            payload_ref[piece, STATE_ROW : STATE_ROW + 8, :] = back[piece * 8 : piece * 8 + 8, :]

        def lap(block, total):
            at = pl.multiple_of(block * T, T)
            grad = exact_left(nt, v_s[pl.ds(at, T), :], back_parts) + backn
            part = split2(feature_back(phi_s[pl.ds(at, T), :], grad))
            return total + exact_left(tn, k_s[pl.ds(at, T), :], part)

        own = split2(feature_back(phi_s[WINDOW * T :, :], gkphi_ref[...]))
        grad_map = lax.fori_loop(0, WINDOW, lap, exact_left(tn, k_s[WINDOW * T :, :], own))
        tail = jnp.concatenate(
            [
                backn[:, :T],
                backn[:, T:],
                jnp.broadcast_to(pos_ref[0:1, 0:1].astype(F32), (1, T)),
                jnp.zeros((1, T), F32),
            ],
            axis=0,
        )
        for piece in range(32):
            payload_ref[piece, KMAP_ROW:PIECE, :] = jnp.concatenate(
                [grad_map[piece * 4 : piece * 4 + 4, :], tail], axis=0
            )


def middle_kernel(me_ref, got_ref, out_ref, norms_ref):
    pieces = got_ref.shape[0]
    total = got_ref[0]
    for i in range(1, pieces):
        total = total + got_ref[i]
    squares = jnp.sum(total[0:STATE_ROW, :] * total[0:STATE_ROW, :]) + jnp.sum(
        total[KMAP_ROW:NORM_ROW, :] * total[KMAP_ROW:NORM_ROW, :]
    )
    tail = jnp.concatenate(
        [total[KMAP_ROW:INFO_ROW, :], jnp.full((2, T), squares, F32)], axis=0
    )
    for j in range(pieces):
        out_ref[j, 0:STATE_ROW, :] = total[0:STATE_ROW, :]
        out_ref[j, KMAP_ROW:PIECE, :] = tail
    sender = lax.broadcasted_iota(jnp.int32, (pieces, T), 0)
    target = lax.broadcasted_iota(jnp.int32, (pieces, T), 1)
    first = (sender * T).astype(F32) - got_ref[:, INFO_ROW, :]
    links = (sender > target) & (first <= (target * T + (T - 1)).astype(F32))
    reach = links.astype(F32)[:, :pieces].astype(BF16)
    for i in range(8):
        high, middle, low = split3(got_ref[:, STATE_ROW + i, :])
        out_ref[:, STATE_ROW + i, :] = tn(reach, high) + (tn(reach, middle) + tn(reach, low))
    me = me_ref[0]
    mine = (sender > me) & (first <= (me * T + (T - 1)).astype(F32))
    for half in range(2):
        norms_ref[0:1, half * T : half * T + T] = jnp.sum(
            jnp.where(mine, got_ref[:, NORM_ROW + half, :], 0.0), axis=0, keepdims=True
        )


def last_kernel(pos_ref, got_ref, norms_ref, kv_ref, kmap_ref, phi_ref, gkphi_ref, gv_ref, gk_ref, gvo_ref):
    pos = column_of(pos_ref[...].astype(F32))
    row = lax.broadcasted_iota(jnp.int32, (T, 1), 0).astype(F32)
    start = row - pos
    last_start = float(T - 1) - pos_ref[0:1, T - 1 : T].astype(F32)
    keeping = (start == last_start).astype(F32)
    pieces = got_ref.shape[0]
    back = split2(
        jnp.concatenate([got_ref[r, STATE_ROW : STATE_ROW + 8, :] for r in range(pieces)], axis=0)
    )
    phi = phi_ref[...]
    own_v = kv_ref[T:, :]
    grad = gkphi_ref[...] + keeping * (exact_left(nt, own_v, back) + norms_ref[...])
    gvo_ref[...] = gv_ref[...] + keeping * product(nn, split2(phi), back)
    gk_ref[...] = product(nt, split2(feature_back(phi, grad)), split2(kmap_ref[0]))


def vmem(count):
    return [pl.BlockSpec(memory_space=pltpu.VMEM)] * count


def window_of(kv):
    n = lax.axis_size("seq")

    def shift(x, k):
        return lax.ppermute(x, "seq", [(i, (i + k) % n) for i in range(n)])

    r8 = shift(kv, 8)
    r16 = shift(r8, 8)
    ahead = jnp.concatenate([kv, r8], axis=0)
    behind = jnp.concatenate([r8, r16], axis=0)
    f1, b1 = shift(ahead, 1), shift(behind, -1)
    f2, b2 = shift(f1, 1), shift(b1, -1)
    f3, b3 = shift(f2, 1), shift(b2, -1)
    f4, b4 = shift(f3[: 2 * T], 1), shift(b3[2 * T :], -1)
    arrays = [kv, r8, r16, f1, b1, f2, b2, f3, b3, f4, b4]
    places = [(0,), (8,), (16,), (1, 9), (7, 15), (2, 10), (6, 14), (3, 11), (5, 13), (4,), (12,)]
    return arrays, places


def on_device(queries, key_vectors, value_vectors, positions, query_map, key_map):
    group = query_map.shape[0]
    pieces = lax.axis_size("seq")
    me = lax.axis_index("seq").astype(jnp.int32).reshape(1)
    pos = positions.reshape(1, T)
    kv = jnp.concatenate([key_vectors, value_vectors], axis=0)
    arrays, places = window_of(kv)
    sds = jax.ShapeDtypeStruct
    whole = lambda *shape: pl.BlockSpec(shape, lambda h: (0,) * len(shape))
    grad_queries, payload, phi, gkphi, gv = pl.pallas_call(
        functools.partial(main_kernel, places),
        grid=(group // PER_STEP,),
        in_specs=[
            whole(1, T),
            pl.BlockSpec((T, ROWS), lambda h: (0, h)),
            pl.BlockSpec((PER_STEP, T, T), lambda h: (h, 0, 0)),
            whole(1, T, T),
        ]
        + [whole(*a.shape) for a in arrays],
        out_specs=[
            pl.BlockSpec((T, ROWS), lambda h: (0, h)),
            whole(pieces, PIECE, T),
            whole(T, 2 * T),
            whole(T, 2 * T),
            whole(T, T),
        ],
        out_shape=[
            sds((T, group * T), F32),
            sds((pieces, PIECE, T), F32),
            sds((T, 2 * T), F32),
            sds((T, 2 * T), F32),
            sds((T, T), F32),
        ],
        scratch_shapes=[
            pltpu.VMEM((KEYS, T), BF16),
            pltpu.VMEM((KEYS, T), BF16),
            pltpu.VMEM((KEYS, 2 * T), F32),
            pltpu.VMEM((T, KEYS), F32),
            pltpu.VMEM((2 * T, T), F32),
            pltpu.VMEM((1, 2 * T), F32),
            pltpu.VMEM((2 * T, T), F32),
            pltpu.VMEM((1, 2 * T), F32),
        ],
        compiler_params=pltpu.CompilerParams(vmem_limit_bytes=48 << 20),
        name="attention_transfer",
    )(pos, queries, query_map, key_map, *arrays)

    gathered = lax.all_to_all(payload, "seq", 0, 0)
    reduced, norms = pl.pallas_call(
        middle_kernel,
        in_specs=[pl.BlockSpec(memory_space=pltpu.SMEM)] + vmem(1),
        out_specs=vmem(2),
        out_shape=[sds((pieces, PIECE, T), F32), sds((1, 2 * T), F32)],
        compiler_params=pltpu.CompilerParams(vmem_limit_bytes=32 << 20),
        name="sum_pieces",
    )(me, gathered)
    back = lax.all_to_all(reduced, "seq", 0, 0)
    squares = jnp.sum(back[:, INFO_ROW, 0])
    heads = lax.axis_size("head")
    squared = jnp.sum(lax.all_to_all(jnp.broadcast_to(squares, (heads, 8, T)), "head", 0, 0)[:, 0, 0])
    grad_keys, grad_values = pl.pallas_call(
        last_kernel,
        in_specs=vmem(8),
        out_specs=vmem(2),
        out_shape=[sds((T, T), F32), sds((T, T), F32)],
        compiler_params=pltpu.CompilerParams(vmem_limit_bytes=32 << 20),
        name="key_gradients",
    )(pos, back, norms, kv, key_map, phi, gkphi, gv)
    clip_limit = 0.25 * math.sqrt((group + 1) * heads * T * T)
    factor = jnp.minimum(1.0, clip_limit / (jnp.sqrt(squared) + EPSILON))
    query_map_grad = factor * back[:, :STATE_ROW, :].reshape(group, T, T)
    key_map_grad = factor * back[:, KMAP_ROW:NORM_ROW, :].reshape(1, T, T)
    return (grad_queries, grad_keys, grad_values, query_map_grad, key_map_grad)


def solution(mesh):
    placed = (
        P("seq", "head"),
        P("seq", "head"),
        P("seq", "head"),
        P("seq"),
        P("head", None, None),
        P("head", None, None),
    )
    return jax.shard_map(
        on_device,
        mesh=mesh,
        in_specs=placed,
        out_specs=(
            P("seq", "head"),
            P("seq", "head"),
            P("seq", "head"),
            P("head", None, None),
            P("head", None, None),
        ),
        check_vma=False,
    )
```

```python
import functools
import math

import jax
import jax.numpy as jnp
from jax import lax
from jax.experimental import pallas as pl
from jax.experimental.pallas import tpu as pltpu
from jax.sharding import PartitionSpec as P

F32 = jnp.float32
BF16 = jnp.bfloat16
NEGATIVE = -1e30
EPSILON = 1e-06
T = 128
WINDOW = 16
KEYS = (WINDOW + 1) * T
CHUNK = 1024
PIECE = 48
STATE_ROW, KMAP_ROW, NORM_ROW, INFO_ROW = 32, 40, 44, 46


def nn(a, b):
    return lax.dot_general(a, b, (((1,), (0,)), ((), ())), preferred_element_type=F32)


def nt(a, b):
    return lax.dot_general(a, b, (((1,), (1,)), ((), ())), preferred_element_type=F32)


def tn(a, b):
    return lax.dot_general(a, b, (((0,), (0,)), ((), ())), preferred_element_type=F32)


def split2(x):
    high = x.astype(BF16)
    return high, (x - high.astype(F32)).astype(BF16)


def split3(x):
    high = x.astype(BF16)
    rest = x - high.astype(F32)
    middle = rest.astype(BF16)
    return high, middle, (rest - middle.astype(F32)).astype(BF16)


def product(form, a, b):
    return form(a[0], b[0]) + (form(a[0], b[1]) + form(a[1], b[0]))


def exact_left(form, a, parts):
    total = form(a, parts[-1])
    for part in parts[-2::-1]:
        total = total + form(a, part)
    return total


def exact_right(form, parts, b):
    return form(parts[0], b) + form(parts[1], b)


def feature_map(logits):
    upper = jnp.exp(logits - jnp.max(logits, axis=-1, keepdims=True))
    lower = jnp.exp(jnp.min(logits, axis=-1, keepdims=True) - logits)
    upper = upper * (1.0 / jnp.sum(upper, axis=-1, keepdims=True))
    lower = lower * (1.0 / jnp.sum(lower, axis=-1, keepdims=True))
    return upper, lower


def feature_back(phi, grad):
    upper, lower = phi[:, :T], phi[:, T:]
    up, low = grad[:, :T], grad[:, T:]
    up = upper * (up - jnp.sum(upper * up, axis=-1, keepdims=True))
    low = lower * (low - jnp.sum(lower * low, axis=-1, keepdims=True))
    return up - low


def column_of(row):
    i = lax.broadcasted_iota(jnp.int32, (T, T), 0)
    j = lax.broadcasted_iota(jnp.int32, (T, T), 1)
    return jnp.sum(jnp.where(i == j, row, 0.0), axis=1, keepdims=True)


def stacked(ref):
    return jnp.concatenate([ref[:, h * T : h * T + T] for h in range(ref.shape[1] // T)], axis=0)


def every_head(x, heads):
    return jnp.concatenate([x] * heads, axis=0)


def positions_of(pos_ref):
    row = lax.broadcasted_iota(jnp.int32, (T, 1), 0).astype(F32)
    return row, row - column_of(pos_ref[...].astype(F32))


def local_kernel(pos_ref, q_ref, k_ref, qmap_ref, kmap_ref, phi_ref, inner_ref, own_ref):
    heads = qmap_ref.shape[0]
    row, start = positions_of(pos_ref)
    key = lax.broadcasted_iota(jnp.int32, (T, T), 1).astype(F32)
    seen = every_head(((key <= row) & (key >= start)).astype(F32), heads)
    own = jnp.concatenate(
        feature_map(exact_left(nn, k_ref[...], split3(kmap_ref[0]))), axis=1
    )
    own_ref[...] = own
    logits = jnp.concatenate(
        [exact_left(nn, q_ref[:, h * T : h * T + T], split3(qmap_ref[h])) for h in range(heads)],
        axis=0,
    )
    phi = jnp.concatenate(feature_map(logits), axis=1)
    phi_ref[...] = phi
    inner_ref[...] = product(nt, split2(phi), split2(own)) * seen


def main_kernel(places, pos_ref, q_ref, kmap_ref, phi_ref, inner_ref, own_ref, *rest):
    count = len(places)
    blocks = rest[:count]
    payload_ref, dlogit_ref, gn_ref, gkphi_ref = rest[count : count + 4]
    k_s, v_s, phi_s = rest[count + 4 :]
    heads = q_ref.shape[1] // T
    row, start = positions_of(pos_ref)
    entry = -pos_ref[0:1, 0:1].astype(F32)
    for ref, held in zip(blocks, places):
        for slot, block in enumerate(held):
            at = (WINDOW - block) * T
            k_s[at : at + T, :] = ref[slot * 2 * T : slot * 2 * T + T, :]
            v_s[at : at + T, :] = ref[slot * 2 * T + T : slot * 2 * T + 2 * T, :]

    map_parts = split3(kmap_ref[0])
    state = jnp.zeros((2 * T, T), F32)
    norms = jnp.zeros((1, 2 * T), F32)
    for at in range(0, WINDOW * T, CHUNK):
        key_row = lax.broadcasted_iota(jnp.int32, (CHUNK, 1), 0) + (at - WINDOW * T)
        features = jnp.concatenate(
            feature_map(exact_left(nn, k_s[at : at + CHUNK, :], map_parts)), axis=1
        )
        features = jnp.where(key_row.astype(F32) >= entry, features, 0.0)
        phi_s[at : at + CHUNK, :] = features
        state = state + exact_right(tn, split2(features), v_s[at : at + CHUNK, :])
        norms = norms + jnp.sum(features, axis=0, keepdims=True)
    state = split2(state)

    key = lax.broadcasted_iota(jnp.int32, (T, KEYS), 1).astype(F32) - float(WINDOW * T)
    visible = (key <= row) & (key >= start)
    bias = every_head(jnp.where(visible, 0.0, NEGATIVE), heads)
    seen = every_head(visible[:, WINDOW * T :].astype(F32), heads)
    cross = every_head((start < 0.0).astype(F32), heads)
    queries = stacked(q_ref)
    scores = nt(queries, k_s[...]) * (1.0 / math.sqrt(T)) + bias
    weights = jnp.exp(scores - jnp.max(scores, axis=-1, keepdims=True))
    total = jnp.sum(weights, axis=-1, keepdims=True)
    teacher = nn(weights.astype(BF16), v_s[...]) / total

    own = own_ref[...]
    own_v = v_s[WINDOW * T :, :]
    own_phi = split2(own)
    phi = phi_ref[...]
    phi_parts = split2(phi)
    inner = inner_ref[...]
    numer = exact_right(nn, split2(inner), own_v) + cross * product(nn, phi_parts, state)
    denom = jnp.sum(inner, axis=-1, keepdims=True) + cross * jnp.sum(
        phi * norms, axis=-1, keepdims=True
    )
    outputs = numer / denom
    error = outputs - teacher

    grad_numer = error / denom
    grad_denom = -jnp.sum(error * outputs, axis=-1, keepdims=True) / denom
    gn_ref[...] = grad_numer
    far_parts = split2(cross * grad_numer)
    far_denom = cross * grad_denom
    mixing_parts = split2((exact_right(nt, split2(grad_numer), own_v) + grad_denom) * seen)
    grad_phi = (
        product(nn, mixing_parts, own_phi) + product(nt, far_parts, state) + far_denom * norms
    )
    back = product(tn, phi_parts, far_parts)
    backn = jnp.sum(phi * far_denom, axis=0, keepdims=True)
    gkphi = product(tn, mixing_parts, phi_parts)
    gkphi_ref[...] = gkphi
    dlogit = feature_back(phi, grad_phi)
    dlogit_ref[...] = dlogit
    dlogit_parts = split2(dlogit)
    for h in range(heads):
        at = slice(h * T, h * T + T)
        grad_map = exact_left(tn, q_ref[:, at], [part[at, :] for part in dlogit_parts])
        for quarter in range(4):
            payload_ref[4 * h + quarter, 0:STATE_ROW, :] = grad_map[
                quarter * 32 : quarter * 32 + 32, :
            ]
    back_parts = split2(back)
    for piece in range(32):
        payload_ref[piece, STATE_ROW : STATE_ROW + 8, :] = back[piece * 8 : piece * 8 + 8, :]

    part = split2(feature_back(own, gkphi))
    grad_map = exact_left(tn, k_s[WINDOW * T :, :], part)
    for at in range(0, WINDOW * T, CHUNK):
        grad = exact_left(nt, v_s[at : at + CHUNK, :], back_parts) + backn
        part = split2(feature_back(phi_s[at : at + CHUNK, :], grad))
        grad_map = grad_map + exact_left(tn, k_s[at : at + CHUNK, :], part)
    tail = jnp.concatenate(
        [
            backn[:, :T],
            backn[:, T:],
            jnp.broadcast_to(pos_ref[0:1, 0:1].astype(F32), (1, T)),
            jnp.zeros((1, T), F32),
        ],
        axis=0,
    )
    for piece in range(32):
        payload_ref[piece, KMAP_ROW:PIECE, :] = jnp.concatenate(
            [grad_map[piece * 4 : piece * 4 + 4, :], tail], axis=0
        )


def query_kernel(dlogit_ref, inner_ref, gn_ref, qmap_ref, gq_ref, gv_ref):
    for h in range(qmap_ref.shape[0]):
        at = slice(h * T, h * T + T)
        gq_ref[:, at] = product(nt, split2(dlogit_ref[at, :]), split2(qmap_ref[h]))
    gv_ref[...] = product(tn, split2(inner_ref[...]), split2(gn_ref[...]))


def middle_kernel(me_ref, got_ref, out_ref, norms_ref):
    pieces = got_ref.shape[0]
    total = got_ref[0]
    for i in range(1, pieces):
        total = total + got_ref[i]
    squares = jnp.sum(total[0:STATE_ROW, :] * total[0:STATE_ROW, :]) + jnp.sum(
        total[KMAP_ROW:NORM_ROW, :] * total[KMAP_ROW:NORM_ROW, :]
    )
    tail = jnp.concatenate(
        [total[KMAP_ROW:INFO_ROW, :], jnp.full((2, T), squares, F32)], axis=0
    )
    for j in range(pieces):
        out_ref[j, 0:STATE_ROW, :] = total[0:STATE_ROW, :]
        out_ref[j, KMAP_ROW:PIECE, :] = tail
    sender = lax.broadcasted_iota(jnp.int32, (pieces, T), 0)
    target = lax.broadcasted_iota(jnp.int32, (pieces, T), 1)
    first = (sender * T).astype(F32) - got_ref[:, INFO_ROW, :]
    links = (sender > target) & (first <= (target * T + (T - 1)).astype(F32))
    reach = links.astype(F32)[:, :pieces].astype(BF16)
    for i in range(8):
        high, middle, low = split3(got_ref[:, STATE_ROW + i, :])
        out_ref[:, STATE_ROW + i, :] = tn(reach, high) + (tn(reach, middle) + tn(reach, low))
    me = me_ref[0]
    mine = (sender > me) & (first <= (me * T + (T - 1)).astype(F32))
    for half in range(2):
        norms_ref[0:1, half * T : half * T + T] = jnp.sum(
            jnp.where(mine, got_ref[:, NORM_ROW + half, :], 0.0), axis=0, keepdims=True
        )


def last_kernel(pos_ref, got_ref, norms_ref, v_ref, kmap_ref, phi_ref, gkphi_ref, gv_ref, gk_ref, gvo_ref):
    _, start = positions_of(pos_ref)
    last_start = float(T - 1) - pos_ref[0:1, T - 1 : T].astype(F32)
    keeping = (start == last_start).astype(F32)
    pieces = got_ref.shape[0]
    back = split2(
        jnp.concatenate([got_ref[r, STATE_ROW : STATE_ROW + 8, :] for r in range(pieces)], axis=0)
    )
    phi = phi_ref[...]
    own_v = v_ref[...]
    grad = gkphi_ref[...] + keeping * (exact_left(nt, own_v, back) + norms_ref[...])
    gvo_ref[...] = gv_ref[...] + keeping * product(nn, split2(phi), back)
    gk_ref[...] = product(nt, split2(feature_back(phi, grad)), split2(kmap_ref[0]))


def squares_kernel(tail_ref, out_ref):
    total = jnp.sum(tail_ref[:, INFO_ROW - KMAP_ROW, :], axis=0, keepdims=True)
    out_ref[...] = jnp.broadcast_to(total.reshape(1, 1, T), out_ref.shape)


def scale_kernel(limit, got_ref, squares_ref, qmap_ref, kmap_ref):
    pieces = got_ref.shape[0]
    squared = jnp.sum(squares_ref[:, 0, :], axis=0, keepdims=True)
    factor = jnp.minimum(1.0, limit / (jnp.sqrt(squared) + EPSILON))
    for piece in range(pieces):
        rows = slice(piece % 4 * 32, piece % 4 * 32 + 32)
        qmap_ref[piece // 4, rows, :] = factor * got_ref[piece, 0:STATE_ROW, :]
        kmap_ref[0, piece * 4 : piece * 4 + 4, :] = factor * got_ref[piece, KMAP_ROW:NORM_ROW, :]


def call(body, name, ins, outs, scratch=(), limit=32):
    return pl.pallas_call(
        body,
        in_specs=[pl.BlockSpec(memory_space=space) for space in ins],
        out_specs=[pl.BlockSpec(memory_space=pltpu.VMEM)] * len(outs),
        out_shape=[jax.ShapeDtypeStruct(shape, F32) for shape in outs],
        scratch_shapes=list(scratch),
        compiler_params=pltpu.CompilerParams(vmem_limit_bytes=limit << 20),
        name=name,
    )


def joined(a, b):
    return lax.pad(a, jnp.zeros((), a.dtype), ((0, b.shape[0], 0), (0, 0, 0))) + lax.pad(
        b, jnp.zeros((), b.dtype), ((a.shape[0], 0, 0), (0, 0, 0))
    )


def window_of(kv):
    n = lax.axis_size("seq")
    size = kv.shape[0]

    def shift(x, k):
        return lax.ppermute(x, "seq", [(i, (i + k) % n) for i in range(n)])

    b1, b4, b7, b8 = (shift(kv, k) for k in (1, 4, 7, 8))
    near = jnp.concatenate([b8, b1, b4, b7], axis=0)
    far = shift(near, 8)
    up, down = slice(size, 3 * size), slice(2 * size, 4 * size)
    n1, n2 = shift(near[up], 1), shift(near[down], -1)
    f1, f2 = shift(far[up], 1), shift(far[down], -1)
    arrays = [kv, near, far, n1, n2, f1, f2]
    places = [(0,), (8, 1, 4, 7), (16, 9, 12, 15), (2, 5), (3, 6), (10, 13), (11, 14)]
    return arrays, places


def on_device(queries, key_vectors, value_vectors, positions, query_map, key_map):
    group = query_map.shape[0]
    pieces = lax.axis_size("seq")
    heads = lax.axis_size("head")
    rows = group * T
    me = lax.axis_index("seq").astype(jnp.int32).reshape(1)
    pos = positions.reshape(1, T)
    kv = joined(key_vectors, value_vectors)
    arrays, places = window_of(kv)
    V = pltpu.VMEM
    phi, inner, own = call(
        local_kernel, "local_features", [V] * 5, [(rows, 2 * T), (rows, T), (T, 2 * T)]
    )(pos, queries, key_vectors, query_map, key_map)
    payload, dlogit, grad_numer, gkphi = call(
        functools.partial(main_kernel, places),
        "attention_transfer",
        [V] * (6 + len(arrays)),
        [(pieces, PIECE, T), (rows, T), (rows, T), (T, 2 * T)],
        [V((KEYS, T), BF16), V((KEYS, T), BF16), V((WINDOW * T, 2 * T), F32)],
        32,
    )(pos, queries, key_map, phi, inner, own, *arrays)
    gathered = lax.all_to_all(payload, "seq", 0, 0)
    grad_queries, near_values = call(
        query_kernel, "query_gradients", [V] * 4, [(T, rows), (T, T)]
    )(dlogit, inner, grad_numer, query_map)
    reduced, norms = call(
        middle_kernel, "sum_pieces", [pltpu.SMEM, V], [(pieces, PIECE, T), (1, 2 * T)]
    )(me, gathered)
    back = lax.all_to_all(reduced, "seq", 0, 0)
    squares = pl.pallas_call(
        squares_kernel,
        grid=(1,),
        in_specs=[pl.BlockSpec((pieces, PIECE - KMAP_ROW, T), lambda i: (0, KMAP_ROW // 8, 0))],
        out_specs=pl.BlockSpec((heads, 8, T), lambda i: (0, 0, 0)),
        out_shape=jax.ShapeDtypeStruct((heads, 8, T), F32),
        name="head_squares",
    )(back)
    squares = lax.all_to_all(squares, "head", 0, 0)
    grad_keys, grad_values = call(last_kernel, "key_gradients", [V] * 8, [(T, T), (T, T)])(
        pos, back, norms, value_vectors, key_map, own, gkphi, near_values
    )
    clip_limit = 0.25 * math.sqrt((group + 1) * heads * T * T)
    query_map_grad, key_map_grad = call(
        functools.partial(scale_kernel, clip_limit),
        "clip_maps",
        [V] * 2,
        [(group, T, T), (1, T, T)],
    )(back, squares)
    return (grad_queries, grad_keys, grad_values, query_map_grad, key_map_grad)


def solution(mesh):
    placed = (
        P("seq", "head"),
        P("seq", "head"),
        P("seq", "head"),
        P("seq"),
        P("head", None, None),
        P("head", None, None),
    )
    return jax.shard_map(
        on_device,
        mesh=mesh,
        in_specs=placed,
        out_specs=(
            P("seq", "head"),
            P("seq", "head"),
            P("seq", "head"),
            P("head", None, None),
            P("head", None, None),
        ),
        check_vma=False,
    )
```

```python
import functools
import math

import jax
import jax.numpy as jnp
from jax import lax
from jax.experimental import pallas as pl
from jax.experimental.pallas import tpu as pltpu
from jax.sharding import PartitionSpec as P

F32 = jnp.float32
BF16 = jnp.bfloat16
NEGATIVE = -1e30
EPSILON = 1e-06
T = 128
WINDOW = 16
KEYS = (WINDOW + 1) * T
CHUNK = 2048
PIECE = 48
STATE_ROW, KMAP_ROW, NORM_ROW, INFO_ROW = 32, 40, 44, 46
REPLY = 56
HIGH_ROW, LOW_ROW, KEY_ROW, SQUARE_ROW = 32, 40, 48, 52


def nn(a, b):
    return lax.dot_general(a, b, (((1,), (0,)), ((), ())), preferred_element_type=F32)


def nt(a, b):
    return lax.dot_general(a, b, (((1,), (1,)), ((), ())), preferred_element_type=F32)


def tn(a, b):
    return lax.dot_general(a, b, (((0,), (0,)), ((), ())), preferred_element_type=F32)


def split2(x):
    high = x.astype(BF16)
    return high, (x - high.astype(F32)).astype(BF16)


def split3(x):
    high = x.astype(BF16)
    rest = x - high.astype(F32)
    middle = rest.astype(BF16)
    return high, middle, (rest - middle.astype(F32)).astype(BF16)


def product(form, a, b):
    return form(a[0], b[0]) + (form(a[0], b[1]) + form(a[1], b[0]))


def exact_left(form, a, parts):
    total = form(a, parts[-1])
    for part in parts[-2::-1]:
        total = total + form(a, part)
    return total


def exact_right(form, parts, b):
    return form(parts[0], b) + form(parts[1], b)


def row_sums(x):
    return exact_right(nn, split2(x), jnp.ones((T, T), BF16))


def feature_map(logits):
    upper = jnp.exp(logits - jnp.max(logits, axis=-1, keepdims=True))
    lower = jnp.exp(jnp.min(logits, axis=-1, keepdims=True) - logits)
    return jnp.concatenate([upper / row_sums(upper), lower / row_sums(lower)], axis=1)


def feature_back(phi, grad):
    upper, lower = phi[:, :T], phi[:, T:]
    up, low = grad[:, :T], grad[:, T:]
    return upper * (up - row_sums(upper * up)) - lower * (low - row_sums(lower * low))


def column_of(row):
    i = lax.broadcasted_iota(jnp.int32, (T, T), 0)
    j = lax.broadcasted_iota(jnp.int32, (T, T), 1)
    return jnp.sum(jnp.where(i == j, row, 0.0), axis=1, keepdims=True)


def stacked(ref):
    return jnp.concatenate([ref[:, h * T : h * T + T] for h in range(ref.shape[1] // T)], axis=0)


def every_head(x, heads):
    return jnp.concatenate([x] * heads, axis=0)


def positions_of(pos_ref):
    row = lax.broadcasted_iota(jnp.int32, (T, 1), 0).astype(F32)
    return row, row - column_of(pos_ref[...].astype(F32))


def local_kernel(pos_ref, q_ref, k_ref, qmap_ref, kmap_ref, phi_ref, inner_ref, own_ref):
    heads = qmap_ref.shape[0]
    row, start = positions_of(pos_ref)
    key = lax.broadcasted_iota(jnp.int32, (T, T), 1).astype(F32)
    seen = every_head(((key <= row) & (key >= start)).astype(F32), heads)
    own = feature_map(exact_left(nn, k_ref[...], split3(kmap_ref[0])))
    own_ref[...] = own
    logits = jnp.concatenate(
        [exact_left(nn, q_ref[:, h * T : h * T + T], split3(qmap_ref[h])) for h in range(heads)],
        axis=0,
    )
    phi = feature_map(logits)
    phi_ref[...] = phi
    inner_ref[...] = product(nt, split2(phi), split2(own)) * seen


def main_kernel(places, pos_ref, q_ref, kmap_ref, phi_ref, inner_ref, own_ref, *rest):
    count = len(places)
    blocks = rest[:count]
    payload_ref, dlogit_ref, gn_ref, gkphi_ref = rest[count : count + 4]
    k_s, v_s, phi_s = rest[count + 4 :]
    heads = q_ref.shape[1] // T
    row, start = positions_of(pos_ref)
    entry = -pos_ref[0:1, 0:1].astype(F32)
    crossing = (start < 0.0).astype(F32)
    lane = lax.broadcasted_iota(jnp.int32, (T, T), 1)
    for ref, held in zip(blocks, places):
        for slot, block in enumerate(held):
            at = (WINDOW - block) * T
            k_s[at : at + T, :T] = ref[slot * 2 * T : slot * 2 * T + T, :]
            v_s[at : at + T, :T] = ref[slot * 2 * T + T : slot * 2 * T + 2 * T, :]
            hidden = jnp.where(row - float(block * T) >= entry, 0.0, NEGATIVE)
            hidden = jnp.where(lane == 0, NEGATIVE, jnp.where(lane == 1, hidden, 0.0))
            k_s[at : at + T, T:] = (hidden if block else jnp.zeros((T, T), F32)).astype(BF16)
    v_s[:, T:] = jnp.ones((KEYS, T), BF16)

    map_parts = split3(kmap_ref[0])
    state = jnp.zeros((2 * T, 2 * T), F32)
    for at in range(0, WINDOW * T, CHUNK):
        key_row = lax.broadcasted_iota(jnp.int32, (CHUNK, 1), 0) + (at - WINDOW * T)
        features = feature_map(exact_left(nn, k_s[at : at + CHUNK, :T], map_parts))
        features = jnp.where(key_row.astype(F32) >= entry, features, 0.0)
        phi_s[at : at + CHUNK, :] = features
        state = state + exact_right(tn, split2(features), v_s[at : at + CHUNK, :])
    norms = jnp.transpose(state[:, T:])[0:1, :]
    state = split2(state)

    own_key = lane.astype(F32)
    visible = (own_key <= row) & (own_key >= start)
    seen = every_head(visible.astype(F32), heads)
    bias = every_head(jnp.where(visible, 0.0, NEGATIVE), heads)
    cross = every_head(jnp.broadcast_to(crossing, (T, T)), heads)
    hider = jnp.where(lane == 0, 1.0 - crossing, jnp.where(lane == 1, 1.0, 0.0)).astype(BF16)
    queries = jnp.concatenate([stacked(q_ref), every_head(hider, heads)], axis=1)
    scores = nt(queries, k_s[...])
    near = scores[:, WINDOW * T :] + bias
    far = scores[:, : WINDOW * T]
    highest = jnp.maximum(
        jnp.max(near, axis=-1, keepdims=True), jnp.max(far, axis=-1, keepdims=True)
    )
    rate = math.log2(math.e) / math.sqrt(T)
    near = jnp.exp2((near - highest) * rate)
    far = jnp.exp2((far - highest) * rate)
    total = jnp.sum(near, axis=-1, keepdims=True) + jnp.sum(far, axis=-1, keepdims=True)
    own_v = v_s[WINDOW * T :, :]
    teacher = nn(near.astype(BF16), own_v[:, :T]) + nn(far.astype(BF16), v_s[: WINDOW * T, :T])
    teacher = teacher / total

    own = own_ref[...]
    own_phi = split2(own)
    phi = phi_ref[...]
    phi_parts = split2(phi)
    near = exact_right(nn, split2(inner_ref[...]), own_v)
    far = product(nn, phi_parts, state)
    inverse = 1.0 / (near[:, T:] + cross * far[:, T:])
    outputs = (near[:, :T] + cross * far[:, :T]) * inverse
    error = outputs - teacher

    grad_numer = error * inverse
    grad_denom = -row_sums(error * outputs) * inverse
    gn_ref[...] = grad_numer
    far_numer = cross * grad_numer
    far_denom = cross * grad_denom
    mixing = (exact_right(nt, split2(grad_numer), own_v[:, :T]) + grad_denom) * seen
    mixing_parts = split2(mixing)
    near = product(nn, mixing_parts, own_phi)
    far = product(nt, split2(far_numer), [part[:, :T] for part in state])
    grad_phi = jnp.concatenate(
        [
            near[:, :T] + far[:, :T] + far_denom * norms[:, :T],
            near[:, T:] + far[:, T:] + far_denom * norms[:, T:],
        ],
        axis=1,
    )
    back = product(tn, phi_parts, split2(jnp.concatenate([far_numer, far_denom], axis=1)))
    backn = jnp.transpose(back[:, T:])[0:1, :]
    gkphi = product(tn, mixing_parts, phi_parts)
    gkphi_ref[...] = gkphi
    dlogit = feature_back(phi, grad_phi)
    dlogit_ref[...] = dlogit
    dlogit_parts = split2(dlogit)
    for h in range(heads):
        at = slice(h * T, h * T + T)
        grad_map = exact_left(tn, q_ref[:, at], [part[at, :] for part in dlogit_parts])
        for quarter in range(4):
            payload_ref[4 * h + quarter, 0:STATE_ROW, :] = grad_map[
                quarter * 32 : quarter * 32 + 32, :
            ]
    for piece in range(32):
        payload_ref[piece, STATE_ROW : STATE_ROW + 8, :] = back[piece * 8 : piece * 8 + 8, :T]

    part = split2(feature_back(own, gkphi))
    grad_map = exact_left(tn, k_s[WINDOW * T :, :T], part)
    back_parts = split2(jnp.concatenate([back[:, :T], back[:, T:] * (1.0 / T)], axis=1))
    for at in range(0, WINDOW * T, CHUNK):
        grad = exact_left(nt, v_s[at : at + CHUNK, :], back_parts)
        part = split2(feature_back(phi_s[at : at + CHUNK, :], grad))
        grad_map = grad_map + exact_left(tn, k_s[at : at + CHUNK, :T], part)
    tail = jnp.concatenate(
        [
            backn[:, :T],
            backn[:, T:],
            jnp.broadcast_to(pos_ref[0:1, 0:1].astype(F32), (1, T)),
            jnp.zeros((1, T), F32),
        ],
        axis=0,
    )
    for piece in range(32):
        payload_ref[piece, KMAP_ROW:PIECE, :] = jnp.concatenate(
            [grad_map[piece * 4 : piece * 4 + 4, :], tail], axis=0
        )


def query_kernel(dlogit_ref, inner_ref, gn_ref, qmap_ref, gq_ref, gv_ref):
    for h in range(qmap_ref.shape[0]):
        at = slice(h * T, h * T + T)
        gq_ref[:, at] = product(nt, split2(dlogit_ref[at, :]), split2(qmap_ref[h]))
    gv_ref[...] = product(tn, split2(inner_ref[...]), split2(gn_ref[...]))


def middle_kernel(me_ref, got_ref, out_ref, norms_ref, state_s):
    pieces = got_ref.shape[0]
    total = got_ref[0]
    for i in range(1, pieces):
        total = total + got_ref[i]
    qmap, kmap = total[0:STATE_ROW, :], total[KMAP_ROW:NORM_ROW, :]
    squares = jnp.sum(qmap * qmap) + jnp.sum(kmap * kmap)
    parts = [part.astype(F32) for part in split3(jnp.full((1, T), squares, F32))]
    tail = jnp.concatenate([kmap] + parts + [jnp.zeros((1, T), F32)], axis=0).astype(BF16)
    qmap = qmap.astype(BF16)
    for j in range(pieces):
        out_ref[j, 0:HIGH_ROW, :] = qmap
        out_ref[j, KEY_ROW:REPLY, :] = tail
    sender = lax.broadcasted_iota(jnp.int32, (pieces, T), 0)
    target = lax.broadcasted_iota(jnp.int32, (pieces, T), 1)
    first = (sender * T).astype(F32) - got_ref[:, INFO_ROW, :]
    links = (sender > target) & (first <= (target * T + (T - 1)).astype(F32))
    reach = links.astype(F32)[:, :pieces].astype(BF16)
    for i in range(8):
        state_s[:, i, :] = exact_left(tn, reach, split3(got_ref[:, STATE_ROW + i, :]))
    high, low = split2(state_s[...])
    out_ref[:, HIGH_ROW:LOW_ROW, :] = high
    out_ref[:, LOW_ROW:KEY_ROW, :] = low
    me = me_ref[0]
    mine = (sender > me) & (first <= (me * T + (T - 1)).astype(F32))
    for half in range(2):
        norms_ref[0:1, half * T : half * T + T] = jnp.sum(
            jnp.where(mine, got_ref[:, NORM_ROW + half, :], 0.0), axis=0, keepdims=True
        )


def last_kernel(pos_ref, got_ref, norms_ref, v_ref, kmap_ref, phi_ref, gkphi_ref, gv_ref, gk_ref, gvo_ref):
    _, start = positions_of(pos_ref)
    last_start = float(T - 1) - pos_ref[0:1, T - 1 : T].astype(F32)
    keeping = (start == last_start).astype(F32)
    pieces = got_ref.shape[0]
    back = [
        jnp.concatenate([got_ref[r, at : at + 8, :] for r in range(pieces)], axis=0)
        for at in (HIGH_ROW, LOW_ROW)
    ]
    phi = phi_ref[...]
    own_v = v_ref[...]
    grad = gkphi_ref[...] + keeping * (exact_left(nt, own_v, back) + norms_ref[...])
    gvo_ref[...] = gv_ref[...] + keeping * product(nn, split2(phi), back)
    gk_ref[...] = product(nt, split2(feature_back(phi, grad)), split2(kmap_ref[0]))


def squares_kernel(tail_ref, out_ref):
    total = jnp.sum(tail_ref[:, KEY_ROW:REPLY, :].astype(F32), axis=0)
    total = jnp.sum(total[SQUARE_ROW - KEY_ROW : SQUARE_ROW - KEY_ROW + 3, :], axis=0)
    out_ref[...] = jnp.broadcast_to(total.reshape(1, 1, T), out_ref.shape)


def scale_kernel(limit, got_ref, squares_ref, qmap_ref, kmap_ref):
    pieces = got_ref.shape[0]
    squared = jnp.sum(squares_ref[:, 0, :], axis=0, keepdims=True)
    factor = jnp.minimum(1.0, limit / (jnp.sqrt(squared) + EPSILON))
    for piece in range(pieces):
        rows = slice(piece % 4 * 32, piece % 4 * 32 + 32)
        qmap_ref[piece // 4, rows, :] = factor * got_ref[piece, 0:HIGH_ROW, :].astype(F32)
        tail = got_ref[piece, KEY_ROW:REPLY, :].astype(F32)
        kmap_ref[0, piece * 4 : piece * 4 + 4, :] = factor * tail[0 : SQUARE_ROW - KEY_ROW, :]


def call(body, name, ins, outs, scratch=(), limit=32):
    return pl.pallas_call(
        body,
        in_specs=[pl.BlockSpec(memory_space=space) for space in ins],
        out_specs=[pl.BlockSpec(memory_space=pltpu.VMEM)] * len(outs),
        out_shape=[
            out if isinstance(out, jax.ShapeDtypeStruct) else jax.ShapeDtypeStruct(out, F32)
            for out in outs
        ],
        scratch_shapes=list(scratch),
        compiler_params=pltpu.CompilerParams(vmem_limit_bytes=limit << 20),
        name=name,
    )


def joined(a, b):
    return lax.pad(a, jnp.zeros((), a.dtype), ((0, b.shape[0], 0), (0, 0, 0))) + lax.pad(
        b, jnp.zeros((), b.dtype), ((a.shape[0], 0, 0), (0, 0, 0))
    )


def window_of(kv):
    n = lax.axis_size("seq")
    size = kv.shape[0]

    def shift(x, k):
        return lax.ppermute(x, "seq", [(i, (i + k) % n) for i in range(n)])

    b1, b4, b7, b8 = (shift(kv, k) for k in (1, 4, 7, 8))
    near = jnp.concatenate([b8, b1, b4, b7], axis=0)
    far = shift(near, 8)
    up, down = slice(size, 3 * size), slice(2 * size, 4 * size)
    n1, n2 = shift(near[up], 1), shift(near[down], -1)
    f1, f2 = shift(far[up], 1), shift(far[down], -1)
    arrays = [kv, near, far, n1, n2, f1, f2]
    places = [(0,), (8, 1, 4, 7), (16, 9, 12, 15), (2, 5), (3, 6), (10, 13), (11, 14)]
    return arrays, places


def on_device(queries, key_vectors, value_vectors, positions, query_map, key_map):
    group = query_map.shape[0]
    pieces = lax.axis_size("seq")
    heads = lax.axis_size("head")
    rows = group * T
    me = lax.axis_index("seq").astype(jnp.int32).reshape(1)
    pos = positions.reshape(1, T)
    kv = joined(key_vectors, value_vectors)
    arrays, places = window_of(kv)
    V = pltpu.VMEM
    phi, inner, own = call(
        local_kernel, "local_features", [V] * 5, [(rows, 2 * T), (rows, T), (T, 2 * T)]
    )(pos, queries, key_vectors, query_map, key_map)
    payload, dlogit, grad_numer, gkphi = call(
        functools.partial(main_kernel, places),
        "attention_transfer",
        [V] * (6 + len(arrays)),
        [(pieces, PIECE, T), (rows, T), (rows, T), (T, 2 * T)],
        [V((KEYS, 2 * T), BF16), V((KEYS, 2 * T), BF16), V((WINDOW * T, 2 * T), F32)],
        32,
    )(pos, queries, key_map, phi, inner, own, *arrays)
    gathered = lax.all_to_all(payload, "seq", 0, 0)
    grad_queries, near_values = call(
        query_kernel, "query_gradients", [V] * 4, [(T, rows), (T, T)]
    )(dlogit, inner, grad_numer, query_map)
    reduced, norms = call(
        middle_kernel,
        "sum_pieces",
        [pltpu.SMEM, V],
        [jax.ShapeDtypeStruct((pieces, REPLY, T), BF16), (1, 2 * T)],
        [V((pieces, 8, T), F32)],
    )(me, gathered)
    back = lax.all_to_all(reduced, "seq", 0, 0)
    squares = call(squares_kernel, "head_squares", [V], [(heads, 8, T)])(back)[0]
    squares = lax.all_to_all(squares, "head", 0, 0)
    grad_keys, grad_values = call(last_kernel, "key_gradients", [V] * 8, [(T, T), (T, T)])(
        pos, back, norms, value_vectors, key_map, own, gkphi, near_values
    )
    clip_limit = 0.25 * math.sqrt((group + 1) * heads * T * T)
    query_map_grad, key_map_grad = call(
        functools.partial(scale_kernel, clip_limit),
        "clip_maps",
        [V] * 2,
        [(group, T, T), (1, T, T)],
    )(back, squares)
    return (grad_queries, grad_keys, grad_values, query_map_grad, key_map_grad)


def solution(mesh):
    placed = (
        P("seq", "head"),
        P("seq", "head"),
        P("seq", "head"),
        P("seq"),
        P("head", None, None),
        P("head", None, None),
    )
    return jax.shard_map(
        on_device,
        mesh=mesh,
        in_specs=placed,
        out_specs=(
            P("seq", "head"),
            P("seq", "head"),
            P("seq", "head"),
            P("head", None, None),
            P("head", None, None),
        ),
        check_vma=False,
    )
```

```python
import functools
import math

import jax
import jax.numpy as jnp
from jax import lax
from jax.experimental import pallas as pl
from jax.experimental.pallas import tpu as pltpu
from jax.sharding import PartitionSpec as P

F32 = jnp.float32
BF16 = jnp.bfloat16
NEGATIVE = -1e30
EPSILON = 1e-06
T = 128
WINDOW = 16
KEYS = (WINDOW + 1) * T
CHUNK = 2048
PIECE = 48
STATE_ROW, KMAP_ROW, NORM_ROW, INFO_ROW = 32, 40, 44, 46
REPLY = 56
HIGH_ROW, LOW_ROW, KEY_ROW, SQUARE_ROW = 32, 40, 48, 52


def nn(a, b):
    return lax.dot_general(a, b, (((1,), (0,)), ((), ())), preferred_element_type=F32)


def nt(a, b):
    return lax.dot_general(a, b, (((1,), (1,)), ((), ())), preferred_element_type=F32)


def tn(a, b):
    return lax.dot_general(a, b, (((0,), (0,)), ((), ())), preferred_element_type=F32)


def split2(x):
    high = x.astype(BF16)
    return high, (x - high.astype(F32)).astype(BF16)


def split3(x):
    high = x.astype(BF16)
    rest = x - high.astype(F32)
    middle = rest.astype(BF16)
    return high, middle, (rest - middle.astype(F32)).astype(BF16)


def product(form, a, b):
    return form(a[0], b[0]) + (form(a[0], b[1]) + form(a[1], b[0]))


def exact_left(form, a, parts):
    total = form(a, parts[-1])
    for part in parts[-2::-1]:
        total = total + form(a, part)
    return total


def exact_right(form, parts, b):
    return form(parts[0], b) + form(parts[1], b)


def row_sums(x):
    return exact_right(nn, split2(x), jnp.ones((T, T), BF16))


def feature_map(logits):
    upper = jnp.exp(logits - jnp.max(logits, axis=-1, keepdims=True))
    lower = jnp.exp(jnp.min(logits, axis=-1, keepdims=True) - logits)
    return jnp.concatenate([upper / row_sums(upper), lower / row_sums(lower)], axis=1)


def feature_back(phi, grad):
    upper, lower = phi[:, :T], phi[:, T:]
    up, low = grad[:, :T], grad[:, T:]
    return upper * (up - row_sums(upper * up)) - lower * (low - row_sums(lower * low))


def column_of(row):
    i = lax.broadcasted_iota(jnp.int32, (T, T), 0)
    j = lax.broadcasted_iota(jnp.int32, (T, T), 1)
    return jnp.sum(jnp.where(i == j, row, 0.0), axis=1, keepdims=True)


def stacked(ref):
    return jnp.concatenate([ref[:, h * T : h * T + T] for h in range(ref.shape[1] // T)], axis=0)


def every_head(x, heads):
    return jnp.concatenate([x] * heads, axis=0)


def positions_of(pos_ref):
    row = lax.broadcasted_iota(jnp.int32, (T, 1), 0).astype(F32)
    return row, row - column_of(pos_ref[...].astype(F32))


def local_kernel(pos_ref, q_ref, k_ref, qmap_ref, kmap_ref, phi_ref, inner_ref, own_ref):
    heads = qmap_ref.shape[0]
    row, start = positions_of(pos_ref)
    key = lax.broadcasted_iota(jnp.int32, (T, T), 1).astype(F32)
    seen = every_head(((key <= row) & (key >= start)).astype(F32), heads)
    own = feature_map(exact_left(nn, k_ref[...], split3(kmap_ref[0])))
    own_ref[...] = own
    logits = jnp.concatenate(
        [exact_left(nn, q_ref[:, h * T : h * T + T], split3(qmap_ref[h])) for h in range(heads)],
        axis=0,
    )
    phi = feature_map(logits)
    phi_ref[...] = phi
    inner_ref[...] = product(nt, split2(phi), split2(own)) * seen


def main_kernel(places, pos_ref, q_ref, kmap_ref, phi_ref, inner_ref, own_ref, *rest):
    count = len(places)
    blocks = rest[:count]
    payload_ref, dlogit_ref, gn_ref, gkphi_ref = rest[count : count + 4]
    k_s, v_s, phi_s = rest[count + 4 :]
    heads = q_ref.shape[1] // T
    row, start = positions_of(pos_ref)
    entry = -pos_ref[0:1, 0:1].astype(F32)
    crossing = (start < 0.0).astype(F32)
    lane = lax.broadcasted_iota(jnp.int32, (T, T), 1)
    for ref, held in zip(blocks, places):
        for slot, block in enumerate(held):
            at = (WINDOW - block) * T
            k_s[at : at + T, :T] = ref[slot * 2 * T : slot * 2 * T + T, :]
            v_s[at : at + T, :T] = ref[slot * 2 * T + T : slot * 2 * T + 2 * T, :]
            hidden = jnp.where(row - float(block * T) >= entry, 0.0, NEGATIVE)
            hidden = jnp.where(lane == 0, NEGATIVE, jnp.where(lane == 1, hidden, 0.0))
            k_s[at : at + T, T:] = (hidden if block else jnp.zeros((T, T), F32)).astype(BF16)
    v_s[:, T:] = jnp.ones((KEYS, T), BF16)

    map_parts = split3(kmap_ref[0])
    state = jnp.zeros((2 * T, 2 * T), F32)
    for at in range(0, WINDOW * T, CHUNK):
        key_row = lax.broadcasted_iota(jnp.int32, (CHUNK, 1), 0) + (at - WINDOW * T)
        features = feature_map(exact_left(nn, k_s[at : at + CHUNK, :T], map_parts))
        features = jnp.where(key_row.astype(F32) >= entry, features, 0.0)
        phi_s[at : at + CHUNK, :] = features
        state = state + exact_right(tn, split2(features), v_s[at : at + CHUNK, :])
    norms = jnp.transpose(state[:, T:])[0:1, :]
    state = split2(state)

    own_key = lane.astype(F32)
    visible = (own_key <= row) & (own_key >= start)
    seen = every_head(visible.astype(F32), heads)
    bias = every_head(jnp.where(visible, 0.0, NEGATIVE), heads)
    cross = every_head(jnp.broadcast_to(crossing, (T, T)), heads)
    hider = jnp.where(lane == 0, 1.0 - crossing, jnp.where(lane == 1, 1.0, 0.0)).astype(BF16)
    queries = jnp.concatenate([stacked(q_ref), every_head(hider, heads)], axis=1)
    scores = nt(queries, k_s[...])
    near = scores[:, WINDOW * T :] + bias
    far = scores[:, : WINDOW * T]
    highest = jnp.maximum(
        jnp.max(near, axis=-1, keepdims=True), jnp.max(far, axis=-1, keepdims=True)
    )
    rate = math.log2(math.e) / math.sqrt(T)
    near = jnp.exp2((near - highest) * rate)
    far = jnp.exp2((far - highest) * rate)
    total = jnp.sum(near, axis=-1, keepdims=True) + jnp.sum(far, axis=-1, keepdims=True)
    own_v = v_s[WINDOW * T :, :]
    teacher = nn(near.astype(BF16), own_v[:, :T]) + nn(far.astype(BF16), v_s[: WINDOW * T, :T])
    teacher = teacher / total

    own = own_ref[...]
    own_phi = split2(own)
    phi = phi_ref[...]
    phi_parts = split2(phi)
    near = exact_right(nn, split2(inner_ref[...]), own_v)
    far = product(nn, phi_parts, state)
    inverse = 1.0 / (near[:, T:] + cross * far[:, T:])
    outputs = (near[:, :T] + cross * far[:, :T]) * inverse
    error = outputs - teacher

    grad_numer = error * inverse
    grad_denom = -row_sums(error * outputs) * inverse
    gn_ref[...] = grad_numer
    far_numer = cross * grad_numer
    far_denom = cross * grad_denom
    mixing = (exact_right(nt, split2(grad_numer), own_v[:, :T]) + grad_denom) * seen
    mixing_parts = split2(mixing)
    near = product(nn, mixing_parts, own_phi)
    far = product(nt, split2(far_numer), [part[:, :T] for part in state])
    grad_phi = jnp.concatenate(
        [
            near[:, :T] + far[:, :T] + far_denom * norms[:, :T],
            near[:, T:] + far[:, T:] + far_denom * norms[:, T:],
        ],
        axis=1,
    )
    back = product(tn, phi_parts, split2(jnp.concatenate([far_numer, far_denom], axis=1)))
    backn = jnp.transpose(back[:, T:])[0:1, :]
    gkphi = product(tn, mixing_parts, phi_parts)
    gkphi_ref[...] = gkphi
    dlogit = feature_back(phi, grad_phi)
    dlogit_ref[...] = dlogit
    dlogit_parts = split2(dlogit)
    for h in range(heads):
        at = slice(h * T, h * T + T)
        grad_map = exact_left(tn, q_ref[:, at], [part[at, :] for part in dlogit_parts])
        for quarter in range(4):
            payload_ref[4 * h + quarter, 0:STATE_ROW, :] = grad_map[
                quarter * 32 : quarter * 32 + 32, :
            ]
    for piece in range(32):
        payload_ref[piece, STATE_ROW : STATE_ROW + 8, :] = back[piece * 8 : piece * 8 + 8, :T]

    part = split2(feature_back(own, gkphi))
    grad_map = exact_left(tn, k_s[WINDOW * T :, :T], part)
    back_parts = split2(jnp.concatenate([back[:, :T], back[:, T:] * (1.0 / T)], axis=1))
    for at in range(0, WINDOW * T, CHUNK):
        grad = exact_left(nt, v_s[at : at + CHUNK, :], back_parts)
        part = split2(feature_back(phi_s[at : at + CHUNK, :], grad))
        grad_map = grad_map + exact_left(tn, k_s[at : at + CHUNK, :T], part)
    tail = jnp.concatenate(
        [
            backn[:, :T],
            backn[:, T:],
            jnp.broadcast_to(pos_ref[0:1, 0:1].astype(F32), (1, T)),
            jnp.zeros((1, T), F32),
        ],
        axis=0,
    )
    for piece in range(32):
        payload_ref[piece, KMAP_ROW:PIECE, :] = jnp.concatenate(
            [grad_map[piece * 4 : piece * 4 + 4, :], tail], axis=0
        )


def query_kernel(dlogit_ref, inner_ref, gn_ref, qmap_ref, gq_ref, gv_ref):
    for h in range(qmap_ref.shape[0]):
        at = slice(h * T, h * T + T)
        gq_ref[:, at] = product(nt, split2(dlogit_ref[at, :]), split2(qmap_ref[h]))
    gv_ref[...] = product(tn, split2(inner_ref[...]), split2(gn_ref[...]))


def middle_kernel(me_ref, got_ref, out_ref, norms_ref, state_s):
    pieces = got_ref.shape[0]
    total = got_ref[0]
    for i in range(1, pieces):
        total = total + got_ref[i]
    qmap, kmap = total[0:STATE_ROW, :], total[KMAP_ROW:NORM_ROW, :]
    squares = jnp.sum(qmap * qmap) + jnp.sum(kmap * kmap)
    parts = [part.astype(F32) for part in split3(jnp.full((1, T), squares, F32))]
    tail = jnp.concatenate([kmap] + parts + [jnp.zeros((1, T), F32)], axis=0).astype(BF16)
    qmap = qmap.astype(BF16)
    for j in range(pieces):
        out_ref[j, 0:HIGH_ROW, :] = qmap
        out_ref[j, KEY_ROW:REPLY, :] = tail
    sender = lax.broadcasted_iota(jnp.int32, (pieces, T), 0)
    target = lax.broadcasted_iota(jnp.int32, (pieces, T), 1)
    first = (sender * T).astype(F32) - got_ref[:, INFO_ROW, :]
    links = (sender > target) & (first <= (target * T + (T - 1)).astype(F32))
    reach = links.astype(F32)[:, :pieces].astype(BF16)
    for i in range(8):
        state_s[:, i, :] = exact_left(tn, reach, split3(got_ref[:, STATE_ROW + i, :]))
    high, low = split2(state_s[...])
    out_ref[:, HIGH_ROW:LOW_ROW, :] = high
    out_ref[:, LOW_ROW:KEY_ROW, :] = low
    me = me_ref[0]
    mine = (sender > me) & (first <= (me * T + (T - 1)).astype(F32))
    for half in range(2):
        norms_ref[0:1, half * T : half * T + T] = jnp.sum(
            jnp.where(mine, got_ref[:, NORM_ROW + half, :], 0.0), axis=0, keepdims=True
        )


def last_kernel(pos_ref, got_ref, norms_ref, v_ref, kmap_ref, phi_ref, gkphi_ref, gv_ref, gk_ref, gvo_ref):
    _, start = positions_of(pos_ref)
    last_start = float(T - 1) - pos_ref[0:1, T - 1 : T].astype(F32)
    keeping = (start == last_start).astype(F32)
    pieces = got_ref.shape[0]
    back = [
        jnp.concatenate([got_ref[r, at : at + 8, :] for r in range(pieces)], axis=0)
        for at in (HIGH_ROW, LOW_ROW)
    ]
    phi = phi_ref[...]
    own_v = v_ref[...]
    grad = gkphi_ref[...] + keeping * (exact_left(nt, own_v, back) + norms_ref[...])
    gvo_ref[...] = gv_ref[...] + keeping * product(nn, split2(phi), back)
    gk_ref[...] = product(nt, split2(feature_back(phi, grad)), split2(kmap_ref[0]))


def squares_kernel(tail_ref, out_ref):
    total = jnp.sum(tail_ref[:, KEY_ROW:REPLY, :].astype(F32), axis=0)
    total = jnp.sum(total[SQUARE_ROW - KEY_ROW : SQUARE_ROW - KEY_ROW + 3, :], axis=0)
    out_ref[...] = jnp.broadcast_to(total.reshape(1, 1, T), out_ref.shape)


def scale_kernel(limit, got_ref, squares_ref, qmap_ref, kmap_ref):
    pieces = got_ref.shape[0]
    squared = jnp.sum(squares_ref[:, 0, :], axis=0, keepdims=True)
    factor = jnp.minimum(1.0, limit / (jnp.sqrt(squared) + EPSILON))
    for piece in range(pieces):
        rows = slice(piece % 4 * 32, piece % 4 * 32 + 32)
        qmap_ref[piece // 4, rows, :] = factor * got_ref[piece, 0:HIGH_ROW, :].astype(F32)
        tail = got_ref[piece, KEY_ROW:REPLY, :].astype(F32)
        kmap_ref[0, piece * 4 : piece * 4 + 4, :] = factor * tail[0 : SQUARE_ROW - KEY_ROW, :]


def call(body, name, ins, outs, scratch=(), limit=32):
    return pl.pallas_call(
        body,
        in_specs=[pl.BlockSpec(memory_space=space) for space in ins],
        out_specs=[pl.BlockSpec(memory_space=pltpu.VMEM)] * len(outs),
        out_shape=[
            out if isinstance(out, jax.ShapeDtypeStruct) else jax.ShapeDtypeStruct(out, F32)
            for out in outs
        ],
        scratch_shapes=list(scratch),
        compiler_params=pltpu.CompilerParams(vmem_limit_bytes=limit << 20),
        name=name,
    )


def joined(a, b):
    return lax.pad(a, jnp.zeros((), a.dtype), ((0, b.shape[0], 0), (0, 0, 0))) + lax.pad(
        b, jnp.zeros((), b.dtype), ((a.shape[0], 0, 0), (0, 0, 0))
    )


def window_of(kv):
    n = lax.axis_size("seq")
    size = kv.shape[0]

    def shift(x, k, ends=()):
        pairs = [(i, (i + k) % n) for i in range(n) if 0 <= i + k < n or i in ends]
        return lax.ppermute(x, "seq", pairs)

    b8, b1, b4, b7 = shift(kv, 8), shift(kv, 1), shift(kv, 4, (n - 4,)), shift(kv, 7, (n - 7,))
    near = jnp.concatenate([b8, b1, b4, b7], axis=0)
    far = shift(near, 8, (n - 8,))
    up, down = slice(size, 3 * size), slice(2 * size, 4 * size)
    n1, n2 = shift(near[up], 1), shift(near[down], -1, (0,))
    f1, f2 = shift(far[up], 1), shift(far[down], -1, (0,))
    arrays = [kv, near, far, n1, n2, f1, f2]
    places = [(0,), (8, 1, 4, 7), (16, 9, 12, 15), (2, 5), (3, 6), (10, 13), (11, 14)]
    return arrays, places


def on_device(queries, key_vectors, value_vectors, positions, query_map, key_map):
    group = query_map.shape[0]
    pieces = lax.axis_size("seq")
    heads = lax.axis_size("head")
    rows = group * T
    me = lax.axis_index("seq").astype(jnp.int32).reshape(1)
    pos = positions.reshape(1, T)
    kv = joined(key_vectors, value_vectors)
    arrays, places = window_of(kv)
    V = pltpu.VMEM
    phi, inner, own = call(
        local_kernel, "local_features", [V] * 5, [(rows, 2 * T), (rows, T), (T, 2 * T)]
    )(pos, queries, key_vectors, query_map, key_map)
    payload, dlogit, grad_numer, gkphi = call(
        functools.partial(main_kernel, places),
        "attention_transfer",
        [V] * (6 + len(arrays)),
        [(pieces, PIECE, T), (rows, T), (rows, T), (T, 2 * T)],
        [V((KEYS, 2 * T), BF16), V((KEYS, 2 * T), BF16), V((WINDOW * T, 2 * T), F32)],
        32,
    )(pos, queries, key_map, phi, inner, own, *arrays)
    gathered = lax.all_to_all(payload, "seq", 0, 0)
    grad_queries, near_values = call(
        query_kernel, "query_gradients", [V] * 4, [(T, rows), (T, T)]
    )(dlogit, inner, grad_numer, query_map)
    reduced, norms = call(
        middle_kernel,
        "sum_pieces",
        [pltpu.SMEM, V],
        [jax.ShapeDtypeStruct((pieces, REPLY, T), BF16), (1, 2 * T)],
        [V((pieces, 8, T), F32)],
    )(me, gathered)
    back = lax.all_to_all(reduced, "seq", 0, 0)
    squares = call(squares_kernel, "head_squares", [V], [(heads, 8, T)])(back)[0]
    squares = lax.all_to_all(squares, "head", 0, 0)
    grad_keys, grad_values = call(last_kernel, "key_gradients", [V] * 8, [(T, T), (T, T)])(
        pos, back, norms, value_vectors, key_map, own, gkphi, near_values
    )
    clip_limit = 0.25 * math.sqrt((group + 1) * heads * T * T)
    query_map_grad, key_map_grad = call(
        functools.partial(scale_kernel, clip_limit),
        "clip_maps",
        [V] * 2,
        [(group, T, T), (1, T, T)],
    )(back, squares)
    return (grad_queries, grad_keys, grad_values, query_map_grad, key_map_grad)


def solution(mesh):
    placed = (
        P("seq", "head"),
        P("seq", "head"),
        P("seq", "head"),
        P("seq"),
        P("head", None, None),
        P("head", None, None),
    )
    return jax.shard_map(
        on_device,
        mesh=mesh,
        in_specs=placed,
        out_specs=(
            P("seq", "head"),
            P("seq", "head"),
            P("seq", "head"),
            P("head", None, None),
            P("head", None, None),
        ),
        check_vma=False,
    )
```

```python
import functools
import math

import jax
import jax.numpy as jnp
from jax import lax
from jax.experimental import pallas as pl
from jax.experimental.pallas import tpu as pltpu
from jax.sharding import PartitionSpec as P

F32 = jnp.float32
BF16 = jnp.bfloat16
NEGATIVE = -1e30
EPSILON = 1e-06
T = 128
WINDOW = 16
KEYS = (WINDOW + 1) * T
TEACHER = 512
CHUNK = 1024
PIECE = 48
STATE_ROW, KMAP_ROW, NORM_ROW, INFO_ROW = 32, 40, 44, 46
REPLY = 56
HIGH_ROW, LOW_ROW, KEY_ROW, SQUARE_ROW = 32, 40, 48, 52


def nn(a, b):
    return lax.dot_general(a, b, (((1,), (0,)), ((), ())), preferred_element_type=F32)


def nt(a, b):
    return lax.dot_general(a, b, (((1,), (1,)), ((), ())), preferred_element_type=F32)


def tn(a, b):
    return lax.dot_general(a, b, (((0,), (0,)), ((), ())), preferred_element_type=F32)


def split2(x):
    high = x.astype(BF16)
    return high, (x - high.astype(F32)).astype(BF16)


def split3(x):
    high = x.astype(BF16)
    rest = x - high.astype(F32)
    middle = rest.astype(BF16)
    return high, middle, (rest - middle.astype(F32)).astype(BF16)


def product(form, a, b):
    return form(a[0], b[0]) + (form(a[0], b[1]) + form(a[1], b[0]))


def exact_left(form, a, parts):
    total = form(a, parts[-1])
    for part in parts[-2::-1]:
        total = total + form(a, part)
    return total


def exact_right(form, parts, b):
    return form(parts[0], b) + form(parts[1], b)


def deep(parts):
    return jnp.concatenate(parts, axis=1)


def deep_exact_right(form, parts, b):
    return form(deep(parts), jnp.concatenate([b, b], axis=0 if form is nn else 1))


def deep_product(form, a, b):
    return deep_exact_right(form, a, b[0]) + form(a[0], b[1])


def wide_exact_left(form, a, parts):
    both = form(a, deep(parts))
    return both[:, :T] + both[:, T:]


def row_sums(x):
    return nn(deep(split2(x)), jnp.ones((2 * T, T), BF16))


def half_sums(x):
    i = lax.broadcasted_iota(jnp.int32, (2 * T, 2 * T), 0) < T
    j = lax.broadcasted_iota(jnp.int32, (2 * T, 2 * T), 1) < T
    return exact_right(nn, split2(x), (i == j).astype(F32).astype(BF16))


def map_of(weights):
    high, middle, low = split3(weights)
    rest = jnp.concatenate([middle, jnp.zeros_like(middle)], axis=1)
    return jnp.concatenate([deep([high, low]), rest], axis=0)


def logits_of(x, matrix):
    both = nn(deep([x, x]), matrix)
    return both[:, :T] + both[:, T:]


def feature_map(logits):
    upper = jnp.exp(logits - jnp.max(logits, axis=-1, keepdims=True))
    lower = jnp.exp(jnp.min(logits, axis=-1, keepdims=True) - logits)
    both = deep([upper, lower])
    return both / half_sums(both)


def feature_back(phi, grad):
    both = phi * (grad - half_sums(phi * grad))
    return both[:, :T] - both[:, T:]


def column_of(row):
    i = lax.broadcasted_iota(jnp.int32, (T, T), 0)
    j = lax.broadcasted_iota(jnp.int32, (T, T), 1)
    return jnp.sum(jnp.where(i == j, row, 0.0), axis=1, keepdims=True)


def stacked(ref):
    return jnp.concatenate([ref[:, h * T : h * T + T] for h in range(ref.shape[1] // T)], axis=0)


def every_head(x, heads):
    return jnp.concatenate([x] * heads, axis=0)


def positions_of(pos_ref):
    row = lax.broadcasted_iota(jnp.int32, (T, 1), 0).astype(F32)
    return row, row - column_of(pos_ref[...].astype(F32))


def local_kernel(pos_ref, q_ref, k_ref, qmap_ref, kmap_ref, phi_ref, inner_ref, own_ref):
    heads = qmap_ref.shape[0]
    row, start = positions_of(pos_ref)
    key = lax.broadcasted_iota(jnp.int32, (T, T), 1).astype(F32)
    seen = every_head(((key <= row) & (key >= start)).astype(F32), heads)
    own = feature_map(logits_of(k_ref[...], map_of(kmap_ref[0])))
    own_ref[...] = own
    logits = jnp.concatenate(
        [logits_of(q_ref[:, h * T : h * T + T], map_of(qmap_ref[h])) for h in range(heads)],
        axis=0,
    )
    phi = feature_map(logits)
    phi_ref[...] = phi
    inner_ref[...] = product(nt, split2(phi), split2(own)) * seen


def main_kernel(places, pos_ref, q_ref, kmap_ref, phi_ref, inner_ref, own_ref, *rest):
    count = len(places)
    blocks = rest[:count]
    payload_ref, dlogit_ref, gn_ref, gkphi_ref = rest[count : count + 4]
    k_s, v_s, phi_s = rest[count + 4 :]
    heads = q_ref.shape[1] // T
    row, start = positions_of(pos_ref)
    entry = -pos_ref[0:1, 0:1].astype(F32)
    crossing = (start < 0.0).astype(F32)
    lane = lax.broadcasted_iota(jnp.int32, (T, T), 1)
    for ref, held in zip(blocks, places):
        for slot, block in enumerate(held):
            at = (WINDOW - block) * T
            k_s[at : at + T, :T] = ref[slot * 2 * T : slot * 2 * T + T, :]
            v_s[at : at + T, :T] = ref[slot * 2 * T + T : slot * 2 * T + 2 * T, :]
            hidden = jnp.where(row - float(block * T) >= entry, 0.0, NEGATIVE)
            hidden = jnp.where(lane == 0, NEGATIVE, jnp.where(lane == 1, hidden, 0.0))
            k_s[at : at + T, T:] = (hidden if block else jnp.zeros((T, T), F32)).astype(BF16)
    v_s[:, T:] = jnp.ones((KEYS, T), BF16)

    matrix = map_of(kmap_ref[0])
    state = jnp.zeros((2 * T, 2 * T), F32)
    for at in range(0, WINDOW * T, CHUNK):
        key_row = lax.broadcasted_iota(jnp.int32, (CHUNK, 1), 0) + (at - WINDOW * T)
        features = feature_map(logits_of(k_s[at : at + CHUNK, :T], matrix))
        features = jnp.where(key_row.astype(F32) >= entry, features, 0.0)
        phi_s[at : at + CHUNK, :] = features
        state = state + exact_right(tn, split2(features), v_s[at : at + CHUNK, :])
    norms = jnp.transpose(state[:, T:])[0:1, :]
    state = split2(state)

    own_key = lane.astype(F32)
    visible = (own_key <= row) & (own_key >= start)
    seen = every_head(visible.astype(F32), heads)
    bias = every_head(jnp.where(visible, 0.0, NEGATIVE), heads)
    cross = every_head(jnp.broadcast_to(crossing, (T, T)), heads)
    hider = jnp.where(lane == 0, 1.0 - crossing, jnp.where(lane == 1, 1.0, 0.0)).astype(BF16)
    queries = jnp.concatenate([stacked(q_ref), every_head(hider, heads)], axis=1)
    own_v = v_s[WINDOW * T :, :]
    rate = math.log2(math.e) / math.sqrt(T)
    teachers = []
    for at in range(0, heads * T, TEACHER):
        rows = slice(at, at + TEACHER)
        scores = nt(queries[rows, :], k_s[...])
        near = scores[:, WINDOW * T :] + bias[rows, :]
        far = scores[:, : WINDOW * T]
        highest = jnp.maximum(
            jnp.max(near, axis=-1, keepdims=True), jnp.max(far, axis=-1, keepdims=True)
        )
        near = jnp.exp2((near - highest) * rate)
        far = jnp.exp2((far - highest) * rate)
        total = jnp.sum(near, axis=-1, keepdims=True) + jnp.sum(far, axis=-1, keepdims=True)
        summed = nn(near.astype(BF16), own_v[:, :T]) + nn(far.astype(BF16), v_s[: WINDOW * T, :T])
        teachers.append(summed / total)
    teacher = jnp.concatenate(teachers, axis=0)

    own = own_ref[...]
    own_phi = split2(own)
    phi = phi_ref[...]
    phi_parts = split2(phi)
    near = deep_exact_right(nn, split2(inner_ref[...]), own_v)
    far = product(nn, phi_parts, state)
    inverse = 1.0 / (near[:, T:] + cross * far[:, T:])
    outputs = (near[:, :T] + cross * far[:, :T]) * inverse
    error = outputs - teacher

    grad_numer = error * inverse
    grad_denom = -row_sums(error * outputs) * inverse
    gn_ref[...] = grad_numer
    far_numer = cross * grad_numer
    far_denom = cross * grad_denom
    mixing = (deep_exact_right(nt, split2(grad_numer), own_v[:, :T]) + grad_denom) * seen
    mixing_parts = split2(mixing)
    near = deep_product(nn, mixing_parts, own_phi)
    far = deep_product(nt, split2(far_numer), [part[:, :T] for part in state])
    grad_phi = jnp.concatenate(
        [
            near[:, :T] + far[:, :T] + far_denom * norms[:, :T],
            near[:, T:] + far[:, T:] + far_denom * norms[:, T:],
        ],
        axis=1,
    )
    back = product(tn, phi_parts, split2(jnp.concatenate([far_numer, far_denom], axis=1)))
    backn = jnp.transpose(back[:, T:])[0:1, :]
    gkphi = product(tn, mixing_parts, phi_parts)
    gkphi_ref[...] = gkphi
    dlogit = feature_back(phi, grad_phi)
    dlogit_ref[...] = dlogit
    dlogit_parts = split2(dlogit)
    for h in range(heads):
        at = slice(h * T, h * T + T)
        grad_map = wide_exact_left(tn, q_ref[:, at], [part[at, :] for part in dlogit_parts])
        for quarter in range(4):
            payload_ref[4 * h + quarter, 0:STATE_ROW, :] = grad_map[
                quarter * 32 : quarter * 32 + 32, :
            ]
    for piece in range(32):
        payload_ref[piece, STATE_ROW : STATE_ROW + 8, :] = back[piece * 8 : piece * 8 + 8, :T]

    part = split2(feature_back(own, gkphi))
    grad_map = wide_exact_left(tn, k_s[WINDOW * T :, :T], part)
    back_parts = split2(jnp.concatenate([back[:, :T], back[:, T:] * (1.0 / T)], axis=1))
    for at in range(0, WINDOW * T, CHUNK):
        grad = exact_left(nt, v_s[at : at + CHUNK, :], back_parts)
        part = split2(feature_back(phi_s[at : at + CHUNK, :], grad))
        grad_map = grad_map + wide_exact_left(tn, k_s[at : at + CHUNK, :T], part)
    tail = jnp.concatenate(
        [
            backn[:, :T],
            backn[:, T:],
            jnp.broadcast_to(pos_ref[0:1, 0:1].astype(F32), (1, T)),
            jnp.zeros((1, T), F32),
        ],
        axis=0,
    )
    for piece in range(32):
        payload_ref[piece, KMAP_ROW:PIECE, :] = jnp.concatenate(
            [grad_map[piece * 4 : piece * 4 + 4, :], tail], axis=0
        )


def query_kernel(dlogit_ref, inner_ref, gn_ref, qmap_ref, gq_ref, gv_ref):
    for h in range(qmap_ref.shape[0]):
        at = slice(h * T, h * T + T)
        gq_ref[:, at] = product(nt, split2(dlogit_ref[at, :]), split2(qmap_ref[h]))
    gv_ref[...] = product(tn, split2(inner_ref[...]), split2(gn_ref[...]))


def middle_kernel(me_ref, got_ref, out_ref, norms_ref, state_s):
    pieces = got_ref.shape[0]
    total = got_ref[0]
    for i in range(1, pieces):
        total = total + got_ref[i]
    qmap, kmap = total[0:STATE_ROW, :], total[KMAP_ROW:NORM_ROW, :]
    squares = jnp.sum(qmap * qmap) + jnp.sum(kmap * kmap)
    parts = [part.astype(F32) for part in split3(jnp.full((1, T), squares, F32))]
    tail = jnp.concatenate([kmap] + parts + [jnp.zeros((1, T), F32)], axis=0).astype(BF16)
    qmap = qmap.astype(BF16)
    for j in range(pieces):
        out_ref[j, 0:HIGH_ROW, :] = qmap
        out_ref[j, KEY_ROW:REPLY, :] = tail
    sender = lax.broadcasted_iota(jnp.int32, (pieces, T), 0)
    target = lax.broadcasted_iota(jnp.int32, (pieces, T), 1)
    first = (sender * T).astype(F32) - got_ref[:, INFO_ROW, :]
    links = (sender > target) & (first <= (target * T + (T - 1)).astype(F32))
    reach = links.astype(F32)[:, :pieces].astype(BF16)
    for i in range(8):
        state_s[:, i, :] = exact_left(tn, reach, split3(got_ref[:, STATE_ROW + i, :]))
    high, low = split2(state_s[...])
    out_ref[:, HIGH_ROW:LOW_ROW, :] = high
    out_ref[:, LOW_ROW:KEY_ROW, :] = low
    me = me_ref[0]
    mine = (sender > me) & (first <= (me * T + (T - 1)).astype(F32))
    for half in range(2):
        norms_ref[0:1, half * T : half * T + T] = jnp.sum(
            jnp.where(mine, got_ref[:, NORM_ROW + half, :], 0.0), axis=0, keepdims=True
        )


def last_kernel(pos_ref, got_ref, norms_ref, v_ref, kmap_ref, phi_ref, gkphi_ref, gv_ref, gk_ref, gvo_ref):
    _, start = positions_of(pos_ref)
    last_start = float(T - 1) - pos_ref[0:1, T - 1 : T].astype(F32)
    keeping = (start == last_start).astype(F32)
    pieces = got_ref.shape[0]
    back = [
        jnp.concatenate([got_ref[r, at : at + 8, :] for r in range(pieces)], axis=0)
        for at in (HIGH_ROW, LOW_ROW)
    ]
    phi = phi_ref[...]
    own_v = v_ref[...]
    grad = gkphi_ref[...] + keeping * (exact_left(nt, own_v, back) + norms_ref[...])
    gvo_ref[...] = gv_ref[...] + keeping * product(nn, split2(phi), back)
    gk_ref[...] = product(nt, split2(feature_back(phi, grad)), split2(kmap_ref[0]))


def squares_kernel(tail_ref, out_ref):
    total = jnp.sum(tail_ref[:, KEY_ROW:REPLY, :].astype(F32), axis=0)
    total = jnp.sum(total[SQUARE_ROW - KEY_ROW : SQUARE_ROW - KEY_ROW + 3, :], axis=0)
    out_ref[...] = jnp.broadcast_to(total.reshape(1, 1, T), out_ref.shape)


def scale_kernel(limit, got_ref, squares_ref, qmap_ref, kmap_ref):
    pieces = got_ref.shape[0]
    squared = jnp.sum(squares_ref[:, 0, :], axis=0, keepdims=True)
    factor = jnp.minimum(1.0, limit / (jnp.sqrt(squared) + EPSILON))
    for piece in range(pieces):
        rows = slice(piece % 4 * 32, piece % 4 * 32 + 32)
        qmap_ref[piece // 4, rows, :] = factor * got_ref[piece, 0:HIGH_ROW, :].astype(F32)
        tail = got_ref[piece, KEY_ROW:REPLY, :].astype(F32)
        kmap_ref[0, piece * 4 : piece * 4 + 4, :] = factor * tail[0 : SQUARE_ROW - KEY_ROW, :]


def call(body, name, ins, outs, scratch=(), limit=32):
    return pl.pallas_call(
        body,
        in_specs=[pl.BlockSpec(memory_space=space) for space in ins],
        out_specs=[pl.BlockSpec(memory_space=pltpu.VMEM)] * len(outs),
        out_shape=[
            out if isinstance(out, jax.ShapeDtypeStruct) else jax.ShapeDtypeStruct(out, F32)
            for out in outs
        ],
        scratch_shapes=list(scratch),
        compiler_params=pltpu.CompilerParams(vmem_limit_bytes=limit << 20),
        name=name,
    )


def joined(a, b):
    return lax.pad(a, jnp.zeros((), a.dtype), ((0, b.shape[0], 0), (0, 0, 0))) + lax.pad(
        b, jnp.zeros((), b.dtype), ((a.shape[0], 0, 0), (0, 0, 0))
    )


def window_of(kv):
    n = lax.axis_size("seq")
    size = kv.shape[0]

    def shift(x, k):
        return lax.ppermute(x, "seq", [(i, (i + k) % n) for i in range(n)])

    b1, b4, b7, b8 = (shift(kv, k) for k in (1, 4, 7, 8))
    near = jnp.concatenate([b8, b1, b4, b7], axis=0)
    far = shift(near, 8)
    up, down = slice(size, 3 * size), slice(2 * size, 4 * size)
    n1, n2 = shift(near[up], 1), shift(near[down], -1)
    f1, f2 = shift(far[up], 1), shift(far[down], -1)
    arrays = [kv, near, far, n1, n2, f1, f2]
    places = [(0,), (8, 1, 4, 7), (16, 9, 12, 15), (2, 5), (3, 6), (10, 13), (11, 14)]
    return arrays, places


def on_device(queries, key_vectors, value_vectors, positions, query_map, key_map):
    group = query_map.shape[0]
    pieces = lax.axis_size("seq")
    heads = lax.axis_size("head")
    rows = group * T
    me = lax.axis_index("seq").astype(jnp.int32).reshape(1)
    pos = positions.reshape(1, T)
    kv = joined(key_vectors, value_vectors)
    arrays, places = window_of(kv)
    V = pltpu.VMEM
    phi, inner, own = call(
        local_kernel, "local_features", [V] * 5, [(rows, 2 * T), (rows, T), (T, 2 * T)]
    )(pos, queries, key_vectors, query_map, key_map)
    payload, dlogit, grad_numer, gkphi = call(
        functools.partial(main_kernel, places),
        "attention_transfer",
        [V] * (6 + len(arrays)),
        [(pieces, PIECE, T), (rows, T), (rows, T), (T, 2 * T)],
        [V((KEYS, 2 * T), BF16), V((KEYS, 2 * T), BF16), V((WINDOW * T, 2 * T), F32)],
        32,
    )(pos, queries, key_map, phi, inner, own, *arrays)
    gathered = lax.all_to_all(payload, "seq", 0, 0)
    grad_queries, near_values = call(
        query_kernel, "query_gradients", [V] * 4, [(T, rows), (T, T)]
    )(dlogit, inner, grad_numer, query_map)
    reduced, norms = call(
        middle_kernel,
        "sum_pieces",
        [pltpu.SMEM, V],
        [jax.ShapeDtypeStruct((pieces, REPLY, T), BF16), (1, 2 * T)],
        [V((pieces, 8, T), F32)],
    )(me, gathered)
    back = lax.all_to_all(reduced, "seq", 0, 0)
    squares = call(squares_kernel, "head_squares", [V], [(heads, 8, T)])(back)[0]
    squares = lax.all_to_all(squares, "head", 0, 0)
    grad_keys, grad_values = call(last_kernel, "key_gradients", [V] * 8, [(T, T), (T, T)])(
        pos, back, norms, value_vectors, key_map, own, gkphi, near_values
    )
    clip_limit = 0.25 * math.sqrt((group + 1) * heads * T * T)
    query_map_grad, key_map_grad = call(
        functools.partial(scale_kernel, clip_limit),
        "clip_maps",
        [V] * 2,
        [(group, T, T), (1, T, T)],
    )(back, squares)
    return (grad_queries, grad_keys, grad_values, query_map_grad, key_map_grad)


def solution(mesh):
    placed = (
        P("seq", "head"),
        P("seq", "head"),
        P("seq", "head"),
        P("seq"),
        P("head", None, None),
        P("head", None, None),
    )
    return jax.shard_map(
        on_device,
        mesh=mesh,
        in_specs=placed,
        out_specs=(
            P("seq", "head"),
            P("seq", "head"),
            P("seq", "head"),
            P("head", None, None),
            P("head", None, None),
        ),
        check_vma=False,
    )
```

```python
import functools
import math

import jax
import jax.numpy as jnp
from jax import lax
from jax.experimental import pallas as pl
from jax.experimental.pallas import tpu as pltpu
from jax.sharding import PartitionSpec as P

F32 = jnp.float32
BF16 = jnp.bfloat16
NEGATIVE = -1e30
EPSILON = 1e-06
T = 128
WINDOW = 16
KEYS = (WINDOW + 1) * T
TEACHER = 512
CHUNK = 1024
PIECE = 48
STATE_ROW, KMAP_ROW, NORM_ROW, INFO_ROW = 32, 40, 44, 46
REPLY = 56
HIGH_ROW, LOW_ROW, KEY_ROW, SQUARE_ROW = 32, 40, 48, 52


def nn(a, b):
    return lax.dot_general(a, b, (((1,), (0,)), ((), ())), preferred_element_type=F32)


def nt(a, b):
    return lax.dot_general(a, b, (((1,), (1,)), ((), ())), preferred_element_type=F32)


def tn(a, b):
    return lax.dot_general(a, b, (((0,), (0,)), ((), ())), preferred_element_type=F32)


def split2(x):
    high = x.astype(BF16)
    return high, (x - high.astype(F32)).astype(BF16)


def split3(x):
    high = x.astype(BF16)
    rest = x - high.astype(F32)
    middle = rest.astype(BF16)
    return high, middle, (rest - middle.astype(F32)).astype(BF16)


def product(form, a, b):
    return form(a[0], b[0]) + (form(a[0], b[1]) + form(a[1], b[0]))


def exact_left(form, a, parts):
    total = form(a, parts[-1])
    for part in parts[-2::-1]:
        total = total + form(a, part)
    return total


def exact_right(form, parts, b):
    return form(parts[0], b) + form(parts[1], b)


def deep(parts):
    return jnp.concatenate(parts, axis=1)


def deep_exact_right(form, parts, b):
    return form(deep(parts), jnp.concatenate([b, b], axis=0 if form is nn else 1))


def deep_product(form, a, b):
    return deep_exact_right(form, a, b[0]) + form(a[0], b[1])


def wide_exact_left(form, a, parts):
    both = form(a, deep(parts))
    return both[:, :T] + both[:, T:]


def row_sums(x):
    return nn(deep(split2(x)), jnp.ones((2 * T, T), BF16))


def half_sums(x):
    i = lax.broadcasted_iota(jnp.int32, (2 * T, 2 * T), 0) < T
    j = lax.broadcasted_iota(jnp.int32, (2 * T, 2 * T), 1) < T
    return exact_right(nn, split2(x), (i == j).astype(F32).astype(BF16))


def map_of(weights):
    high, middle, low = split3(weights)
    rest = jnp.concatenate([middle, jnp.zeros_like(middle)], axis=1)
    return jnp.concatenate([deep([high, low]), rest], axis=0)


def logits_of(x, matrix):
    both = nn(deep([x, x]), matrix)
    return both[:, :T] + both[:, T:]


def feature_map(logits):
    upper = jnp.exp(logits - jnp.max(logits, axis=-1, keepdims=True))
    lower = jnp.exp(jnp.min(logits, axis=-1, keepdims=True) - logits)
    both = deep([upper, lower])
    return both / half_sums(both)


def feature_back(phi, grad):
    both = phi * (grad - half_sums(phi * grad))
    return both[:, :T] - both[:, T:]


def column_of(row):
    i = lax.broadcasted_iota(jnp.int32, (T, T), 0)
    j = lax.broadcasted_iota(jnp.int32, (T, T), 1)
    return jnp.sum(jnp.where(i == j, row, 0.0), axis=1, keepdims=True)


def stacked(ref):
    return jnp.concatenate([ref[:, h * T : h * T + T] for h in range(ref.shape[1] // T)], axis=0)


def every_head(x, heads):
    return jnp.concatenate([x] * heads, axis=0)


def positions_of(pos_ref):
    row = lax.broadcasted_iota(jnp.int32, (T, 1), 0).astype(F32)
    return row, row - column_of(pos_ref[...].astype(F32))


def local_kernel(pos_ref, q_ref, k_ref, qmap_ref, kmap_ref, phi_ref, inner_ref, own_ref):
    heads = qmap_ref.shape[0]
    row, start = positions_of(pos_ref)
    key = lax.broadcasted_iota(jnp.int32, (T, T), 1).astype(F32)
    seen = every_head(((key <= row) & (key >= start)).astype(F32), heads)
    own = feature_map(logits_of(k_ref[...], map_of(kmap_ref[0])))
    own_ref[...] = own
    logits = jnp.concatenate(
        [logits_of(q_ref[:, h * T : h * T + T], map_of(qmap_ref[h])) for h in range(heads)],
        axis=0,
    )
    phi = feature_map(logits)
    phi_ref[...] = phi
    inner_ref[...] = product(nt, split2(phi), split2(own)) * seen


def main_kernel(places, pos_ref, q_ref, kmap_ref, phi_ref, inner_ref, own_ref, *rest):
    count = len(places)
    blocks = rest[:count]
    payload_ref, dlogit_ref, gn_ref, gkphi_ref = rest[count : count + 4]
    k_s, v_s, phi_s = rest[count + 4 :]
    heads = q_ref.shape[1] // T
    row, start = positions_of(pos_ref)
    entry = -pos_ref[0:1, 0:1].astype(F32)
    crossing = (start < 0.0).astype(F32)
    lane = lax.broadcasted_iota(jnp.int32, (T, T), 1)
    for ref, held in zip(blocks, places):
        for slot, block in enumerate(held):
            at = (WINDOW - block) * T
            k_s[at : at + T, :T] = ref[slot * 2 * T : slot * 2 * T + T, :]
            v_s[at : at + T, :T] = ref[slot * 2 * T + T : slot * 2 * T + 2 * T, :]
            hidden = jnp.where(row - float(block * T) >= entry, 0.0, NEGATIVE)
            hidden = jnp.where(lane == 0, NEGATIVE, jnp.where(lane == 1, hidden, 0.0))
            k_s[at : at + T, T:] = (hidden if block else jnp.zeros((T, T), F32)).astype(BF16)
    v_s[:, T:] = jnp.ones((KEYS, T), BF16)

    matrix = map_of(kmap_ref[0])
    state = jnp.zeros((2 * T, 2 * T), F32)
    for at in range(0, WINDOW * T, CHUNK):
        key_row = lax.broadcasted_iota(jnp.int32, (CHUNK, 1), 0) + (at - WINDOW * T)
        features = feature_map(logits_of(k_s[at : at + CHUNK, :T], matrix))
        features = jnp.where(key_row.astype(F32) >= entry, features, 0.0)
        phi_s[at : at + CHUNK, :] = features
        state = state + exact_right(tn, split2(features), v_s[at : at + CHUNK, :])
    norms = jnp.transpose(state[:, T:])[0:1, :]
    state = split2(state)

    own_key = lane.astype(F32)
    visible = (own_key <= row) & (own_key >= start)
    seen = every_head(visible.astype(F32), heads)
    bias = every_head(jnp.where(visible, 0.0, NEGATIVE), heads)
    cross = every_head(jnp.broadcast_to(crossing, (T, T)), heads)
    hider = jnp.where(lane == 0, 1.0 - crossing, jnp.where(lane == 1, 1.0, 0.0)).astype(BF16)
    queries = jnp.concatenate([stacked(q_ref), every_head(hider, heads)], axis=1)
    own_v = v_s[WINDOW * T :, :]
    rate = math.log2(math.e) / math.sqrt(T)
    teachers = []
    for at in range(0, heads * T, TEACHER):
        rows = slice(at, at + TEACHER)
        scores = nt(queries[rows, :], k_s[...])
        near = scores[:, WINDOW * T :] + bias[rows, :]
        far = scores[:, : WINDOW * T]
        highest = jnp.maximum(
            jnp.max(near, axis=-1, keepdims=True), jnp.max(far, axis=-1, keepdims=True)
        )
        near = jnp.exp2((near - highest) * rate)
        far = jnp.exp2((far - highest) * rate)
        total = jnp.sum(near, axis=-1, keepdims=True) + jnp.sum(far, axis=-1, keepdims=True)
        summed = nn(near.astype(BF16), own_v[:, :T]) + nn(far.astype(BF16), v_s[: WINDOW * T, :T])
        teachers.append(summed / total)
    teacher = jnp.concatenate(teachers, axis=0)

    own = own_ref[...]
    own_phi = split2(own)
    phi = phi_ref[...]
    phi_parts = split2(phi)
    near = deep_exact_right(nn, split2(inner_ref[...]), own_v)
    far = product(nn, phi_parts, state)
    inverse = 1.0 / (near[:, T:] + cross * far[:, T:])
    outputs = (near[:, :T] + cross * far[:, :T]) * inverse
    error = outputs - teacher

    grad_numer = error * inverse
    grad_denom = -row_sums(error * outputs) * inverse
    gn_ref[...] = grad_numer
    far_numer = cross * grad_numer
    far_denom = cross * grad_denom
    mixing = (deep_exact_right(nt, split2(grad_numer), own_v[:, :T]) + grad_denom) * seen
    mixing_parts = split2(mixing)
    near = deep_product(nn, mixing_parts, own_phi)
    far = deep_product(nt, split2(far_numer), [part[:, :T] for part in state])
    grad_phi = jnp.concatenate(
        [
            near[:, :T] + far[:, :T] + far_denom * norms[:, :T],
            near[:, T:] + far[:, T:] + far_denom * norms[:, T:],
        ],
        axis=1,
    )
    back = product(tn, phi_parts, split2(jnp.concatenate([far_numer, far_denom], axis=1)))
    backn = jnp.transpose(back[:, T:])[0:1, :]
    gkphi = product(tn, mixing_parts, phi_parts)
    gkphi_ref[...] = gkphi
    dlogit = feature_back(phi, grad_phi)
    dlogit_ref[...] = dlogit
    dlogit_parts = split2(dlogit)
    for h in range(heads):
        at = slice(h * T, h * T + T)
        grad_map = wide_exact_left(tn, q_ref[:, at], [part[at, :] for part in dlogit_parts])
        for quarter in range(4):
            payload_ref[4 * h + quarter, 0:STATE_ROW, :] = grad_map[
                quarter * 32 : quarter * 32 + 32, :
            ]
    for piece in range(32):
        payload_ref[piece, STATE_ROW : STATE_ROW + 8, :] = back[piece * 8 : piece * 8 + 8, :T]

    part = split2(feature_back(own, gkphi))
    grad_map = wide_exact_left(tn, k_s[WINDOW * T :, :T], part)
    back_parts = split2(jnp.concatenate([back[:, :T], back[:, T:] * (1.0 / T)], axis=1))
    for at in range(0, WINDOW * T, CHUNK):
        grad = exact_left(nt, v_s[at : at + CHUNK, :], back_parts)
        part = split2(feature_back(phi_s[at : at + CHUNK, :], grad))
        grad_map = grad_map + wide_exact_left(tn, k_s[at : at + CHUNK, :T], part)
    tail = jnp.concatenate(
        [
            backn[:, :T],
            backn[:, T:],
            jnp.broadcast_to(pos_ref[0:1, 0:1].astype(F32), (1, T)),
            jnp.zeros((1, T), F32),
        ],
        axis=0,
    )
    for piece in range(32):
        payload_ref[piece, KMAP_ROW:PIECE, :] = jnp.concatenate(
            [grad_map[piece * 4 : piece * 4 + 4, :], tail], axis=0
        )


def query_kernel(dlogit_ref, inner_ref, gn_ref, qmap_ref, gq_ref, gv_ref):
    for h in range(qmap_ref.shape[0]):
        at = slice(h * T, h * T + T)
        gq_ref[:, at] = product(nt, split2(dlogit_ref[at, :]), split2(qmap_ref[h]))
    gv_ref[...] = product(tn, split2(inner_ref[...]), split2(gn_ref[...]))


def middle_kernel(me_ref, got_ref, out_ref, norms_ref, state_s):
    pieces = got_ref.shape[0]
    total = got_ref[0]
    for i in range(1, pieces):
        total = total + got_ref[i]
    qmap, kmap = total[0:STATE_ROW, :], total[KMAP_ROW:NORM_ROW, :]
    squares = jnp.sum(qmap * qmap) + jnp.sum(kmap * kmap)
    parts = [part.astype(F32) for part in split3(jnp.full((1, T), squares, F32))]
    tail = jnp.concatenate([kmap] + parts + [jnp.zeros((1, T), F32)], axis=0).astype(BF16)
    qmap = qmap.astype(BF16)
    for j in range(pieces):
        out_ref[j, 0:HIGH_ROW, :] = qmap
        out_ref[j, KEY_ROW:REPLY, :] = tail
    sender = lax.broadcasted_iota(jnp.int32, (pieces, T), 0)
    target = lax.broadcasted_iota(jnp.int32, (pieces, T), 1)
    first = (sender * T).astype(F32) - got_ref[:, INFO_ROW, :]
    links = (sender > target) & (first <= (target * T + (T - 1)).astype(F32))
    reach = links.astype(F32)[:, :pieces].astype(BF16)
    for i in range(8):
        state_s[:, i, :] = exact_left(tn, reach, split3(got_ref[:, STATE_ROW + i, :]))
    high, low = split2(state_s[...])
    out_ref[:, HIGH_ROW:LOW_ROW, :] = high
    out_ref[:, LOW_ROW:KEY_ROW, :] = low
    me = me_ref[0]
    mine = (sender > me) & (first <= (me * T + (T - 1)).astype(F32))
    for half in range(2):
        norms_ref[0:1, half * T : half * T + T] = jnp.sum(
            jnp.where(mine, got_ref[:, NORM_ROW + half, :], 0.0), axis=0, keepdims=True
        )


def last_kernel(pos_ref, got_ref, norms_ref, v_ref, kmap_ref, phi_ref, gkphi_ref, gv_ref, gk_ref, gvo_ref):
    _, start = positions_of(pos_ref)
    last_start = float(T - 1) - pos_ref[0:1, T - 1 : T].astype(F32)
    keeping = (start == last_start).astype(F32)
    pieces = got_ref.shape[0]
    back = [
        jnp.concatenate([got_ref[r, at : at + 8, :] for r in range(pieces)], axis=0)
        for at in (HIGH_ROW, LOW_ROW)
    ]
    phi = phi_ref[...]
    own_v = v_ref[...]
    grad = gkphi_ref[...] + keeping * (exact_left(nt, own_v, back) + norms_ref[...])
    gvo_ref[...] = gv_ref[...] + keeping * product(nn, split2(phi), back)
    gk_ref[...] = product(nt, split2(feature_back(phi, grad)), split2(kmap_ref[0]))


def squares_kernel(tail_ref, out_ref):
    total = jnp.sum(tail_ref[:, KEY_ROW:REPLY, :].astype(F32), axis=0)
    total = jnp.sum(total[SQUARE_ROW - KEY_ROW : SQUARE_ROW - KEY_ROW + 3, :], axis=0)
    out_ref[...] = jnp.broadcast_to(total.reshape(1, 1, T), out_ref.shape)


def scale_kernel(limit, got_ref, squares_ref, qmap_ref, kmap_ref):
    pieces = got_ref.shape[0]
    squared = jnp.sum(squares_ref[:, 0, :], axis=0, keepdims=True)
    factor = jnp.minimum(1.0, limit / (jnp.sqrt(squared) + EPSILON))
    for piece in range(pieces):
        rows = slice(piece % 4 * 32, piece % 4 * 32 + 32)
        qmap_ref[piece // 4, rows, :] = factor * got_ref[piece, 0:HIGH_ROW, :].astype(F32)
        tail = got_ref[piece, KEY_ROW:REPLY, :].astype(F32)
        kmap_ref[0, piece * 4 : piece * 4 + 4, :] = factor * tail[0 : SQUARE_ROW - KEY_ROW, :]


def call(body, name, ins, outs, scratch=(), limit=32):
    return pl.pallas_call(
        body,
        in_specs=[pl.BlockSpec(memory_space=space) for space in ins],
        out_specs=[pl.BlockSpec(memory_space=pltpu.VMEM)] * len(outs),
        out_shape=[
            out if isinstance(out, jax.ShapeDtypeStruct) else jax.ShapeDtypeStruct(out, F32)
            for out in outs
        ],
        scratch_shapes=list(scratch),
        compiler_params=pltpu.CompilerParams(vmem_limit_bytes=limit << 20),
        name=name,
    )


def joined(a, b):
    return lax.pad(a, jnp.zeros((), a.dtype), ((0, b.shape[0], 0), (0, 0, 0))) + lax.pad(
        b, jnp.zeros((), b.dtype), ((a.shape[0], 0, 0), (0, 0, 0))
    )


def window_of(kv):
    n = lax.axis_size("seq")
    size = kv.shape[0]

    def shift(x, k):
        return lax.ppermute(x, "seq", [(i, (i + k) % n) for i in range(n)])

    b1, b4, b7, b8 = (shift(kv, k) for k in (1, 4, 7, 8))
    near = jnp.concatenate([b8, b1, b4, b7], axis=0)
    far = shift(near, 8)
    up, down = slice(size, 3 * size), slice(2 * size, 4 * size)
    n1, n2 = shift(near[up], 1), shift(near[down], -1)
    f1, f2 = shift(n1, 8), shift(n2, 8)
    arrays = [kv, near, far, n1, n2, f1, f2]
    places = [(0,), (8, 1, 4, 7), (16, 9, 12, 15), (2, 5), (3, 6), (10, 13), (11, 14)]
    return arrays, places


def on_device(queries, key_vectors, value_vectors, positions, query_map, key_map):
    group = query_map.shape[0]
    pieces = lax.axis_size("seq")
    heads = lax.axis_size("head")
    rows = group * T
    me = lax.axis_index("seq").astype(jnp.int32).reshape(1)
    pos = positions.reshape(1, T)
    kv = joined(key_vectors, value_vectors)
    arrays, places = window_of(kv)
    V = pltpu.VMEM
    phi, inner, own = call(
        local_kernel, "local_features", [V] * 5, [(rows, 2 * T), (rows, T), (T, 2 * T)]
    )(pos, queries, key_vectors, query_map, key_map)
    payload, dlogit, grad_numer, gkphi = call(
        functools.partial(main_kernel, places),
        "attention_transfer",
        [V] * (6 + len(arrays)),
        [(pieces, PIECE, T), (rows, T), (rows, T), (T, 2 * T)],
        [V((KEYS, 2 * T), BF16), V((KEYS, 2 * T), BF16), V((WINDOW * T, 2 * T), F32)],
        32,
    )(pos, queries, key_map, phi, inner, own, *arrays)
    gathered = lax.all_to_all(payload, "seq", 0, 0)
    grad_queries, near_values = call(
        query_kernel, "query_gradients", [V] * 4, [(T, rows), (T, T)]
    )(dlogit, inner, grad_numer, query_map)
    reduced, norms = call(
        middle_kernel,
        "sum_pieces",
        [pltpu.SMEM, V],
        [jax.ShapeDtypeStruct((pieces, REPLY, T), BF16), (1, 2 * T)],
        [V((pieces, 8, T), F32)],
    )(me, gathered)
    back = lax.all_to_all(reduced, "seq", 0, 0)
    squares = call(squares_kernel, "head_squares", [V], [(heads, 8, T)])(back)[0]
    squares = lax.all_to_all(squares, "head", 0, 0)
    grad_keys, grad_values = call(last_kernel, "key_gradients", [V] * 8, [(T, T), (T, T)])(
        pos, back, norms, value_vectors, key_map, own, gkphi, near_values
    )
    clip_limit = 0.25 * math.sqrt((group + 1) * heads * T * T)
    query_map_grad, key_map_grad = call(
        functools.partial(scale_kernel, clip_limit),
        "clip_maps",
        [V] * 2,
        [(group, T, T), (1, T, T)],
    )(back, squares)
    return (grad_queries, grad_keys, grad_values, query_map_grad, key_map_grad)


def solution(mesh):
    placed = (
        P("seq", "head"),
        P("seq", "head"),
        P("seq", "head"),
        P("seq"),
        P("head", None, None),
        P("head", None, None),
    )
    return jax.shard_map(
        on_device,
        mesh=mesh,
        in_specs=placed,
        out_specs=(
            P("seq", "head"),
            P("seq", "head"),
            P("seq", "head"),
            P("head", None, None),
            P("head", None, None),
        ),
        check_vma=False,
    )
```

```python
import functools
import math

import jax
import jax.numpy as jnp
from jax import lax
from jax.experimental import pallas as pl
from jax.experimental.pallas import tpu as pltpu
from jax.sharding import PartitionSpec as P

F32 = jnp.float32
BF16 = jnp.bfloat16
NEGATIVE = -1e30
EPSILON = 1e-06
T = 128
WINDOW = 16
KEYS = (WINDOW + 1) * T
TEACHER = 512
CHUNK = 1024
PIECE = 48
STATE_ROW, KMAP_ROW, NORM_ROW, INFO_ROW = 32, 40, 44, 46
REPLY = 56
HIGH_ROW, LOW_ROW, KEY_ROW, SQUARE_ROW = 32, 40, 48, 52


def nn(a, b):
    return lax.dot_general(a, b, (((1,), (0,)), ((), ())), preferred_element_type=F32)


def nt(a, b):
    return lax.dot_general(a, b, (((1,), (1,)), ((), ())), preferred_element_type=F32)


def tn(a, b):
    return lax.dot_general(a, b, (((0,), (0,)), ((), ())), preferred_element_type=F32)


def split2(x):
    high = x.astype(BF16)
    return high, (x - high.astype(F32)).astype(BF16)


def split3(x):
    high = x.astype(BF16)
    rest = x - high.astype(F32)
    middle = rest.astype(BF16)
    return high, middle, (rest - middle.astype(F32)).astype(BF16)


def product(form, a, b):
    return form(a[0], b[0]) + (form(a[0], b[1]) + form(a[1], b[0]))


def exact_left(form, a, parts):
    total = form(a, parts[-1])
    for part in parts[-2::-1]:
        total = total + form(a, part)
    return total


def exact_right(form, parts, b):
    return form(parts[0], b) + form(parts[1], b)


def deep(parts):
    return jnp.concatenate(parts, axis=1)


def deep_exact_right(form, parts, b):
    return form(deep(parts), jnp.concatenate([b, b], axis=0 if form is nn else 1))


def deep_product(form, a, b):
    return deep_exact_right(form, a, b[0]) + form(a[0], b[1])


def wide_exact_left(form, a, parts):
    both = form(a, deep(parts))
    return both[:, :T] + both[:, T:]


def row_sums(x):
    return nn(deep(split2(x)), jnp.ones((2 * T, T), BF16))


def half_sums(x):
    i = lax.broadcasted_iota(jnp.int32, (2 * T, 2 * T), 0) < T
    j = lax.broadcasted_iota(jnp.int32, (2 * T, 2 * T), 1) < T
    return exact_right(nn, split2(x), (i == j).astype(F32).astype(BF16))


def map_of(weights):
    high, middle, low = split3(weights)
    rest = jnp.concatenate([middle, jnp.zeros_like(middle)], axis=1)
    return jnp.concatenate([deep([high, low]), rest], axis=0)


def logits_of(x, matrix):
    both = nn(deep([x, x]), matrix)
    return both[:, :T] + both[:, T:]


def feature_map(logits):
    upper = jnp.exp(logits - jnp.max(logits, axis=-1, keepdims=True))
    lower = jnp.exp(jnp.min(logits, axis=-1, keepdims=True) - logits)
    both = deep([upper, lower])
    return both / half_sums(both)


def feature_back(phi, grad):
    both = phi * (grad - half_sums(phi * grad))
    return both[:, :T] - both[:, T:]


def column_of(row):
    i = lax.broadcasted_iota(jnp.int32, (T, T), 0)
    j = lax.broadcasted_iota(jnp.int32, (T, T), 1)
    return jnp.sum(jnp.where(i == j, row, 0.0), axis=1, keepdims=True)


def stacked(ref):
    return jnp.concatenate([ref[:, h * T : h * T + T] for h in range(ref.shape[1] // T)], axis=0)


def every_head(x, heads):
    return jnp.concatenate([x] * heads, axis=0)


def positions_of(pos_ref):
    row = lax.broadcasted_iota(jnp.int32, (T, 1), 0).astype(F32)
    return row, row - column_of(pos_ref[...].astype(F32))


def local_kernel(pos_ref, q_ref, k_ref, qmap_ref, kmap_ref, phi_ref, inner_ref, own_ref):
    heads = qmap_ref.shape[0]
    row, start = positions_of(pos_ref)
    key = lax.broadcasted_iota(jnp.int32, (T, T), 1).astype(F32)
    seen = every_head(((key <= row) & (key >= start)).astype(F32), heads)
    own = feature_map(logits_of(k_ref[...], map_of(kmap_ref[0])))
    own_ref[...] = own
    logits = jnp.concatenate(
        [logits_of(q_ref[:, h * T : h * T + T], map_of(qmap_ref[h])) for h in range(heads)],
        axis=0,
    )
    phi = feature_map(logits)
    phi_ref[...] = phi
    inner_ref[...] = product(nt, split2(phi), split2(own)) * seen


def main_kernel(places, pos_ref, q_ref, kmap_ref, phi_ref, inner_ref, own_ref, *rest):
    count = len(places)
    blocks = rest[:count]
    payload_ref, dlogit_ref, gn_ref, gkphi_ref = rest[count : count + 4]
    k_s, v_s, phi_s = rest[count + 4 :]
    heads = q_ref.shape[1] // T
    row, start = positions_of(pos_ref)
    entry = -pos_ref[0:1, 0:1].astype(F32)
    crossing = (start < 0.0).astype(F32)
    lane = lax.broadcasted_iota(jnp.int32, (T, T), 1)
    for ref, held in zip(blocks, places):
        for slot, block in enumerate(held):
            at = (WINDOW - block) * T
            k_s[at : at + T, :T] = ref[slot * 2 * T : slot * 2 * T + T, :]
            v_s[at : at + T, :T] = ref[slot * 2 * T + T : slot * 2 * T + 2 * T, :]
            hidden = jnp.where(row - float(block * T) >= entry, 0.0, NEGATIVE)
            hidden = jnp.where(lane == 0, NEGATIVE, jnp.where(lane == 1, hidden, 0.0))
            k_s[at : at + T, T:] = (hidden if block else jnp.zeros((T, T), F32)).astype(BF16)
    v_s[:, T:] = jnp.ones((KEYS, T), BF16)

    matrix = map_of(kmap_ref[0])
    state = jnp.zeros((2 * T, 2 * T), F32)
    for at in range(0, WINDOW * T, CHUNK):
        key_row = lax.broadcasted_iota(jnp.int32, (CHUNK, 1), 0) + (at - WINDOW * T)
        features = feature_map(logits_of(k_s[at : at + CHUNK, :T], matrix))
        features = jnp.where(key_row.astype(F32) >= entry, features, 0.0)
        phi_s[at : at + CHUNK, :] = features
        state = state + exact_right(tn, split2(features), v_s[at : at + CHUNK, :])
    norms = jnp.transpose(state[:, T:])[0:1, :]
    state = split2(state)

    own_key = lane.astype(F32)
    visible = (own_key <= row) & (own_key >= start)
    seen = every_head(visible.astype(F32), heads)
    bias = every_head(jnp.where(visible, 0.0, NEGATIVE), heads)
    cross = every_head(jnp.broadcast_to(crossing, (T, T)), heads)
    hider = jnp.where(lane == 0, 1.0 - crossing, jnp.where(lane == 1, 1.0, 0.0)).astype(BF16)
    queries = jnp.concatenate([stacked(q_ref), every_head(hider, heads)], axis=1)
    own_v = v_s[WINDOW * T :, :]
    rate = math.log2(math.e) / math.sqrt(T)
    teachers = []
    for at in range(0, heads * T, TEACHER):
        rows = slice(at, at + TEACHER)
        scores = nt(queries[rows, :], k_s[...])
        near = scores[:, WINDOW * T :] + bias[rows, :]
        far = scores[:, : WINDOW * T]
        highest = jnp.maximum(
            jnp.max(near, axis=-1, keepdims=True), jnp.max(far, axis=-1, keepdims=True)
        )
        near = jnp.exp2((near - highest) * rate)
        far = jnp.exp2((far - highest) * rate)
        total = jnp.sum(near, axis=-1, keepdims=True) + jnp.sum(far, axis=-1, keepdims=True)
        summed = nn(near.astype(BF16), own_v[:, :T]) + nn(far.astype(BF16), v_s[: WINDOW * T, :T])
        teachers.append(summed / total)
    teacher = jnp.concatenate(teachers, axis=0)

    own = own_ref[...]
    own_phi = split2(own)
    phi = phi_ref[...]
    phi_parts = split2(phi)
    near = deep_exact_right(nn, split2(inner_ref[...]), own_v)
    far = product(nn, phi_parts, state)
    inverse = 1.0 / (near[:, T:] + cross * far[:, T:])
    outputs = (near[:, :T] + cross * far[:, :T]) * inverse
    error = outputs - teacher

    grad_numer = error * inverse
    grad_denom = -row_sums(error * outputs) * inverse
    gn_ref[...] = grad_numer
    far_numer = cross * grad_numer
    far_denom = cross * grad_denom
    mixing = (deep_exact_right(nt, split2(grad_numer), own_v[:, :T]) + grad_denom) * seen
    mixing_parts = split2(mixing)
    near = deep_product(nn, mixing_parts, own_phi)
    far = deep_product(nt, split2(far_numer), [part[:, :T] for part in state])
    grad_phi = jnp.concatenate(
        [
            near[:, :T] + far[:, :T] + far_denom * norms[:, :T],
            near[:, T:] + far[:, T:] + far_denom * norms[:, T:],
        ],
        axis=1,
    )
    back = product(tn, phi_parts, split2(jnp.concatenate([far_numer, far_denom], axis=1)))
    backn = jnp.transpose(back[:, T:])[0:1, :]
    gkphi = product(tn, mixing_parts, phi_parts)
    gkphi_ref[...] = gkphi
    dlogit = feature_back(phi, grad_phi)
    dlogit_ref[...] = dlogit
    dlogit_parts = split2(dlogit)
    for h in range(heads):
        at = slice(h * T, h * T + T)
        grad_map = wide_exact_left(tn, q_ref[:, at], [part[at, :] for part in dlogit_parts])
        for quarter in range(4):
            payload_ref[4 * h + quarter, 0:STATE_ROW, :] = grad_map[
                quarter * 32 : quarter * 32 + 32, :
            ]
    for piece in range(32):
        payload_ref[piece, STATE_ROW : STATE_ROW + 8, :] = back[piece * 8 : piece * 8 + 8, :T]

    part = split2(feature_back(own, gkphi))
    grad_map = wide_exact_left(tn, k_s[WINDOW * T :, :T], part)
    back_parts = split2(jnp.concatenate([back[:, :T], back[:, T:] * (1.0 / T)], axis=1))
    for at in range(0, WINDOW * T, CHUNK):
        grad = exact_left(nt, v_s[at : at + CHUNK, :], back_parts)
        part = split2(feature_back(phi_s[at : at + CHUNK, :], grad))
        grad_map = grad_map + wide_exact_left(tn, k_s[at : at + CHUNK, :T], part)
    tail = jnp.concatenate(
        [
            backn[:, :T],
            backn[:, T:],
            jnp.broadcast_to(pos_ref[0:1, 0:1].astype(F32), (1, T)),
            jnp.zeros((1, T), F32),
        ],
        axis=0,
    )
    for piece in range(32):
        payload_ref[piece, KMAP_ROW:PIECE, :] = jnp.concatenate(
            [grad_map[piece * 4 : piece * 4 + 4, :], tail], axis=0
        )


def query_kernel(dlogit_ref, inner_ref, gn_ref, qmap_ref, gq_ref, gv_ref):
    for h in range(qmap_ref.shape[0]):
        at = slice(h * T, h * T + T)
        gq_ref[:, at] = product(nt, split2(dlogit_ref[at, :]), split2(qmap_ref[h]))
    gv_ref[...] = product(tn, split2(inner_ref[...]), split2(gn_ref[...]))


def middle_kernel(me_ref, got_ref, out_ref, norms_ref, state_s):
    pieces = got_ref.shape[0]
    total = got_ref[0]
    for i in range(1, pieces):
        total = total + got_ref[i]
    qmap, kmap = total[0:STATE_ROW, :], total[KMAP_ROW:NORM_ROW, :]
    squares = jnp.sum(qmap * qmap) + jnp.sum(kmap * kmap)
    parts = [part.astype(F32) for part in split3(jnp.full((1, T), squares, F32))]
    tail = jnp.concatenate([kmap] + parts + [jnp.zeros((1, T), F32)], axis=0).astype(BF16)
    qmap = qmap.astype(BF16)
    for j in range(pieces):
        out_ref[j, 0:HIGH_ROW, :] = qmap
        out_ref[j, KEY_ROW:REPLY, :] = tail
    sender = lax.broadcasted_iota(jnp.int32, (pieces, T), 0)
    target = lax.broadcasted_iota(jnp.int32, (pieces, T), 1)
    first = (sender * T).astype(F32) - got_ref[:, INFO_ROW, :]
    links = (sender > target) & (first <= (target * T + (T - 1)).astype(F32))
    reach = links.astype(F32)[:, :pieces].astype(BF16)
    for i in range(8):
        state_s[:, i, :] = exact_left(tn, reach, split3(got_ref[:, STATE_ROW + i, :]))
    high, low = split2(state_s[...])
    out_ref[:, HIGH_ROW:LOW_ROW, :] = high
    out_ref[:, LOW_ROW:KEY_ROW, :] = low
    me = me_ref[0]
    mine = (sender > me) & (first <= (me * T + (T - 1)).astype(F32))
    for half in range(2):
        norms_ref[0:1, half * T : half * T + T] = jnp.sum(
            jnp.where(mine, got_ref[:, NORM_ROW + half, :], 0.0), axis=0, keepdims=True
        )


def last_kernel(pos_ref, got_ref, norms_ref, v_ref, kmap_ref, phi_ref, gkphi_ref, gv_ref, gk_ref, gvo_ref):
    _, start = positions_of(pos_ref)
    last_start = float(T - 1) - pos_ref[0:1, T - 1 : T].astype(F32)
    keeping = (start == last_start).astype(F32)
    pieces = got_ref.shape[0]
    back = [
        jnp.concatenate([got_ref[r, at : at + 8, :] for r in range(pieces)], axis=0)
        for at in (HIGH_ROW, LOW_ROW)
    ]
    phi = phi_ref[...]
    own_v = v_ref[...]
    grad = gkphi_ref[...] + keeping * (exact_left(nt, own_v, back) + norms_ref[...])
    gvo_ref[...] = gv_ref[...] + keeping * product(nn, split2(phi), back)
    gk_ref[...] = product(nt, split2(feature_back(phi, grad)), split2(kmap_ref[0]))


def squares_kernel(tail_ref, out_ref):
    total = jnp.sum(tail_ref[:, KEY_ROW:REPLY, :].astype(F32), axis=0)
    total = jnp.sum(total[SQUARE_ROW - KEY_ROW : SQUARE_ROW - KEY_ROW + 3, :], axis=0)
    out_ref[...] = jnp.broadcast_to(total.reshape(1, 1, T), out_ref.shape)


def scale_kernel(limit, got_ref, squares_ref, qmap_ref, kmap_ref):
    pieces = got_ref.shape[0]
    squared = jnp.sum(squares_ref[:, 0, :], axis=0, keepdims=True)
    factor = jnp.minimum(1.0, limit / (jnp.sqrt(squared) + EPSILON))
    for piece in range(pieces):
        rows = slice(piece % 4 * 32, piece % 4 * 32 + 32)
        qmap_ref[piece // 4, rows, :] = factor * got_ref[piece, 0:HIGH_ROW, :].astype(F32)
        tail = got_ref[piece, KEY_ROW:REPLY, :].astype(F32)
        kmap_ref[0, piece * 4 : piece * 4 + 4, :] = factor * tail[0 : SQUARE_ROW - KEY_ROW, :]


def call(body, name, ins, outs, scratch=(), limit=32):
    return pl.pallas_call(
        body,
        in_specs=[pl.BlockSpec(memory_space=space) for space in ins],
        out_specs=[pl.BlockSpec(memory_space=pltpu.VMEM)] * len(outs),
        out_shape=[
            out if isinstance(out, jax.ShapeDtypeStruct) else jax.ShapeDtypeStruct(out, F32)
            for out in outs
        ],
        scratch_shapes=list(scratch),
        compiler_params=pltpu.CompilerParams(vmem_limit_bytes=limit << 20),
        name=name,
    )


def joined(a, b):
    return lax.pad(a, jnp.zeros((), a.dtype), ((0, b.shape[0], 0), (0, 0, 0))) + lax.pad(
        b, jnp.zeros((), b.dtype), ((a.shape[0], 0, 0), (0, 0, 0))
    )


def window_of(kv):
    n = lax.axis_size("seq")

    def shift(x, k):
        return lax.ppermute(x, "seq", [(i, (i + k) % n) for i in range(n)])

    b4, b8, b1, b7 = (shift(kv, k) for k in (4, 8, 1, 7))
    near = jnp.concatenate([b4, b8, b1, b7], axis=0)
    n1 = shift(jnp.concatenate([b1, b4], axis=0), 1)
    n2 = shift(jnp.concatenate([b4, b7], axis=0), -1)
    far = shift(near, 8)
    f1, f2 = shift(n1, 8), shift(n2, 8)
    arrays = [kv, near, far, n1, n2, f1, f2]
    places = [(0,), (4, 8, 1, 7), (12, 16, 9, 15), (2, 5), (3, 6), (10, 13), (11, 14)]
    return arrays, places


def on_device(queries, key_vectors, value_vectors, positions, query_map, key_map):
    group = query_map.shape[0]
    pieces = lax.axis_size("seq")
    heads = lax.axis_size("head")
    rows = group * T
    me = lax.axis_index("seq").astype(jnp.int32).reshape(1)
    pos = positions.reshape(1, T)
    kv = joined(key_vectors, value_vectors)
    arrays, places = window_of(kv)
    V = pltpu.VMEM
    phi, inner, own = call(
        local_kernel, "local_features", [V] * 5, [(rows, 2 * T), (rows, T), (T, 2 * T)]
    )(pos, queries, key_vectors, query_map, key_map)
    payload, dlogit, grad_numer, gkphi = call(
        functools.partial(main_kernel, places),
        "attention_transfer",
        [V] * (6 + len(arrays)),
        [(pieces, PIECE, T), (rows, T), (rows, T), (T, 2 * T)],
        [V((KEYS, 2 * T), BF16), V((KEYS, 2 * T), BF16), V((WINDOW * T, 2 * T), F32)],
        32,
    )(pos, queries, key_map, phi, inner, own, *arrays)
    gathered = lax.all_to_all(payload, "seq", 0, 0)
    grad_queries, near_values = call(
        query_kernel, "query_gradients", [V] * 4, [(T, rows), (T, T)]
    )(dlogit, inner, grad_numer, query_map)
    reduced, norms = call(
        middle_kernel,
        "sum_pieces",
        [pltpu.SMEM, V],
        [jax.ShapeDtypeStruct((pieces, REPLY, T), BF16), (1, 2 * T)],
        [V((pieces, 8, T), F32)],
    )(me, gathered)
    back = lax.all_to_all(reduced, "seq", 0, 0)
    squares = call(squares_kernel, "head_squares", [V], [(heads, 8, T)])(back)[0]
    squares = lax.all_to_all(squares, "head", 0, 0)
    grad_keys, grad_values = call(last_kernel, "key_gradients", [V] * 8, [(T, T), (T, T)])(
        pos, back, norms, value_vectors, key_map, own, gkphi, near_values
    )
    clip_limit = 0.25 * math.sqrt((group + 1) * heads * T * T)
    query_map_grad, key_map_grad = call(
        functools.partial(scale_kernel, clip_limit),
        "clip_maps",
        [V] * 2,
        [(group, T, T), (1, T, T)],
    )(back, squares)
    return (grad_queries, grad_keys, grad_values, query_map_grad, key_map_grad)


def solution(mesh):
    placed = (
        P("seq", "head"),
        P("seq", "head"),
        P("seq", "head"),
        P("seq"),
        P("head", None, None),
        P("head", None, None),
    )
    return jax.shard_map(
        on_device,
        mesh=mesh,
        in_specs=placed,
        out_specs=(
            P("seq", "head"),
            P("seq", "head"),
            P("seq", "head"),
            P("head", None, None),
            P("head", None, None),
        ),
        check_vma=False,
    )
```

```python
import functools
import math

import jax
import jax.numpy as jnp
from jax import lax
from jax.experimental import pallas as pl
from jax.experimental.pallas import tpu as pltpu
from jax.sharding import PartitionSpec as P

F32 = jnp.float32
BF16 = jnp.bfloat16
NEGATIVE = -1e30
EPSILON = 1e-06
T = 128
WINDOW = 16
KEYS = (WINDOW + 1) * T
TEACHER = 512
PIECE = 48
STATE_ROW, KMAP_ROW, NORM_ROW, INFO_ROW = 32, 40, 44, 46
REPLY = 56
HIGH_ROW, LOW_ROW, KEY_ROW, SQUARE_ROW = 32, 40, 48, 52


def nn(a, b):
    return lax.dot_general(a, b, (((1,), (0,)), ((), ())), preferred_element_type=F32)


def nt(a, b):
    return lax.dot_general(a, b, (((1,), (1,)), ((), ())), preferred_element_type=F32)


def tn(a, b):
    return lax.dot_general(a, b, (((0,), (0,)), ((), ())), preferred_element_type=F32)


def split2(x):
    high = x.astype(BF16)
    return high, (x - high.astype(F32)).astype(BF16)


def split3(x):
    high = x.astype(BF16)
    rest = x - high.astype(F32)
    middle = rest.astype(BF16)
    return high, middle, (rest - middle.astype(F32)).astype(BF16)


def product(form, a, b):
    return form(a[0], b[0]) + (form(a[0], b[1]) + form(a[1], b[0]))


def exact_left(form, a, parts):
    total = form(a, parts[-1])
    for part in parts[-2::-1]:
        total = total + form(a, part)
    return total


def exact_right(form, parts, b):
    return form(parts[0], b) + form(parts[1], b)


def deep(parts):
    return jnp.concatenate(parts, axis=1)


def deep_exact_right(form, parts, b):
    return form(deep(parts), jnp.concatenate([b, b], axis=0 if form is nn else 1))


def deep_product(form, a, b):
    return deep_exact_right(form, a, b[0]) + form(a[0], b[1])


def wide_exact_left(form, a, parts):
    both = form(a, deep(parts))
    return both[:, :T] + both[:, T:]


def row_sums(x):
    return nn(deep(split2(x)), jnp.ones((2 * T, T), BF16))


def half_sums(x):
    i = lax.broadcasted_iota(jnp.int32, (2 * T, 2 * T), 0) < T
    j = lax.broadcasted_iota(jnp.int32, (2 * T, 2 * T), 1) < T
    return exact_right(nn, split2(x), (i == j).astype(F32).astype(BF16))


def map_of(weights):
    high, middle, low = split3(weights)
    rest = jnp.concatenate([middle, jnp.zeros_like(middle)], axis=1)
    return jnp.concatenate([deep([high, low]), rest], axis=0)


def logits_of(x, matrix):
    both = nn(deep([x, x]), matrix)
    return both[:, :T] + both[:, T:]


def feature_map(logits):
    upper = jnp.exp(logits - jnp.max(logits, axis=-1, keepdims=True))
    lower = jnp.exp(jnp.min(logits, axis=-1, keepdims=True) - logits)
    both = deep([upper, lower])
    return both / half_sums(both)


def feature_back(phi, grad):
    both = phi * (grad - half_sums(phi * grad))
    return both[:, :T] - both[:, T:]


def column_of(row):
    i = lax.broadcasted_iota(jnp.int32, (T, T), 0)
    j = lax.broadcasted_iota(jnp.int32, (T, T), 1)
    return jnp.sum(jnp.where(i == j, row, 0.0), axis=1, keepdims=True)


def stacked(ref):
    return jnp.concatenate([ref[:, h * T : h * T + T] for h in range(ref.shape[1] // T)], axis=0)


def every_head(x, heads):
    return jnp.concatenate([x] * heads, axis=0)


def positions_of(pos_ref):
    row = lax.broadcasted_iota(jnp.int32, (T, 1), 0).astype(F32)
    return row, row - column_of(pos_ref[...].astype(F32))


def local_kernel(pos_ref, q_ref, k_ref, qmap_ref, kmap_ref, phi_ref, inner_ref, own_ref):
    heads = qmap_ref.shape[0]
    row, start = positions_of(pos_ref)
    key = lax.broadcasted_iota(jnp.int32, (T, T), 1).astype(F32)
    seen = every_head(((key <= row) & (key >= start)).astype(F32), heads)
    own = feature_map(logits_of(k_ref[...], map_of(kmap_ref[0])))
    own_ref[...] = own
    logits = jnp.concatenate(
        [logits_of(q_ref[:, h * T : h * T + T], map_of(qmap_ref[h])) for h in range(heads)],
        axis=0,
    )
    phi = feature_map(logits)
    phi_ref[...] = phi
    inner_ref[...] = product(nt, split2(phi), split2(own)) * seen


def hold_keys(arrays, places, pos_ref, k_s, v_s):
    row = lax.broadcasted_iota(jnp.int32, (T, 1), 0).astype(F32)
    entry = -pos_ref[0:1, 0:1].astype(F32)
    lane = lax.broadcasted_iota(jnp.int32, (T, T), 1)
    at = 0
    keys = []
    for ref, held in zip(arrays, places):
        for slot, block in enumerate(held):
            k_s[at : at + T, :T] = ref[slot * 2 * T : slot * 2 * T + T, :]
            v_s[at : at + T, :T] = ref[slot * 2 * T + T : slot * 2 * T + 2 * T, :]
            key = row - float(block * T)
            hidden = jnp.where(key >= entry, 0.0, NEGATIVE)
            hidden = jnp.where(lane == 0, NEGATIVE, jnp.where(lane == 1, hidden, 0.0))
            k_s[at : at + T, T:] = (hidden if block else jnp.zeros((T, T), F32)).astype(BF16)
            keys.append(key)
            at += T
    v_s[:, T:] = jnp.ones(v_s[:, T:].shape, BF16)
    return keys, entry


def key_features(rows, keys, entry, matrix, k_s, v_s):
    features = feature_map(logits_of(k_s[rows, :T], matrix))
    features = jnp.where(jnp.concatenate(keys, axis=0) >= entry, features, 0.0)
    return features, exact_right(tn, split2(features), v_s[rows, :])


def asking(q_ref, crossing):
    heads = q_ref.shape[1] // T
    lane = lax.broadcasted_iota(jnp.int32, (T, T), 1)
    hider = jnp.where(lane == 0, 1.0 - crossing, jnp.where(lane == 1, 1.0, 0.0)).astype(BF16)
    return deep([stacked(q_ref), every_head(hider, heads)])


RATE = math.log2(math.e) / math.sqrt(T)


def part_kernel(places, pos_ref, q_ref, kmap_ref, *rest):
    count = len(places)
    phi_ref, state_ref, top_ref, total_ref, sum_ref = rest[count : count + 5]
    k_s, v_s = rest[count + 5 :]
    _, start = positions_of(pos_ref)
    keys, entry = hold_keys(rest[:count], places, pos_ref, k_s, v_s)
    phi_ref[...], state_ref[...] = key_features(
        slice(None), keys, entry, map_of(kmap_ref[0]), k_s, v_s
    )
    queries = asking(q_ref, (start < 0.0).astype(F32))
    for at in range(0, queries.shape[0], TEACHER):
        rows = slice(at, at + TEACHER)
        scores = nt(queries[rows, :], k_s[...])
        top = jnp.max(scores, axis=-1, keepdims=True)
        weights = jnp.exp2((scores - top) * RATE)
        total = jnp.sum(weights, axis=-1, keepdims=True)
        sum_ref[rows, :] = nn(weights.astype(BF16), v_s[:, :T])
        top_ref[rows, :] = jnp.broadcast_to(top, (TEACHER, T))
        total_ref[rows, :] = jnp.broadcast_to(total, (TEACHER, T))


def main_kernel(places, parts, pos_ref, q_ref, kmap_ref, phi_ref, inner_ref, own_ref, *rest):
    count = len(places)
    blocks = rest[:count]
    done = [rest[count + 5 * i : count + 5 * i + 5] for i in range(parts)]
    rest = rest[count + 5 * parts :]
    payload_ref, dlogit_ref, gn_ref, gkphi_ref, k_s, v_s = rest
    heads = q_ref.shape[1] // T
    row, start = positions_of(pos_ref)
    crossing = (start < 0.0).astype(F32)
    keys, entry = hold_keys(blocks, places, pos_ref, k_s, v_s)
    first = sum(part[0].shape[0] for part in done)
    late, state = key_features(
        slice(first, WINDOW * T), keys[first // T : WINDOW], entry, map_of(kmap_ref[0]), k_s, v_s
    )
    for part in done:
        state = state + part[1][...]
    norms = jnp.transpose(state[:, T:])[0:1, :]
    state = split2(state)

    own_key = lax.broadcasted_iota(jnp.int32, (T, T), 1).astype(F32)
    visible = (own_key <= row) & (own_key >= start)
    seen = every_head(visible.astype(F32), heads)
    bias = every_head(jnp.where(visible, 0.0, NEGATIVE), heads)
    cross = every_head(jnp.broadcast_to(crossing, (T, T)), heads)
    queries = asking(q_ref, crossing)
    own_v = v_s[WINDOW * T :, :]
    teachers = []
    for at in range(0, heads * T, TEACHER):
        rows = slice(at, at + TEACHER)
        scores = nt(queries[rows, :], k_s[first:, :])
        near = scores[:, WINDOW * T - first :] + bias[rows, :]
        far = scores[:, : WINDOW * T - first]
        top = jnp.maximum(
            jnp.max(near, axis=-1, keepdims=True), jnp.max(far, axis=-1, keepdims=True)
        )
        top = jnp.broadcast_to(top, (TEACHER, T))
        for part in done:
            top = jnp.maximum(top, part[2][rows, :])
        near = jnp.exp2((near - top) * RATE)
        far = jnp.exp2((far - top[:, 0:1]) * RATE)
        total = jnp.sum(near, axis=-1, keepdims=True) + jnp.sum(far, axis=-1, keepdims=True)
        summed = nn(deep([far, near]).astype(BF16), v_s[first:, :T])
        for part in done:
            fading = jnp.exp2((part[2][rows, :] - top) * RATE)
            total = total + fading * part[3][rows, :]
            summed = summed + fading * part[4][rows, :]
        teachers.append(summed / total)
    teacher = jnp.concatenate(teachers, axis=0)

    own = own_ref[...]
    own_phi = split2(own)
    phi = phi_ref[...]
    phi_parts = split2(phi)
    near = deep_exact_right(nn, split2(inner_ref[...]), own_v)
    far = product(nn, phi_parts, state)
    inverse = 1.0 / (near[:, T:] + cross * far[:, T:])
    outputs = (near[:, :T] + cross * far[:, :T]) * inverse
    error = outputs - teacher

    grad_numer = error * inverse
    grad_denom = -row_sums(error * outputs) * inverse
    gn_ref[...] = grad_numer
    far_numer = cross * grad_numer
    far_denom = cross * grad_denom
    mixing = (deep_exact_right(nt, split2(grad_numer), own_v[:, :T]) + grad_denom) * seen
    mixing_parts = split2(mixing)
    near = deep_product(nn, mixing_parts, own_phi)
    far = deep_product(nt, split2(far_numer), [part[:, :T] for part in state])
    grad_phi = jnp.concatenate(
        [
            near[:, :T] + far[:, :T] + far_denom * norms[:, :T],
            near[:, T:] + far[:, T:] + far_denom * norms[:, T:],
        ],
        axis=1,
    )
    back = product(tn, phi_parts, split2(jnp.concatenate([far_numer, far_denom], axis=1)))
    backn = jnp.transpose(back[:, T:])[0:1, :]
    gkphi = product(tn, mixing_parts, phi_parts)
    gkphi_ref[...] = gkphi
    dlogit = feature_back(phi, grad_phi)
    dlogit_ref[...] = dlogit
    dlogit_parts = split2(dlogit)
    for h in range(heads):
        at = slice(h * T, h * T + T)
        grad_map = wide_exact_left(tn, q_ref[:, at], [part[at, :] for part in dlogit_parts])
        for quarter in range(4):
            payload_ref[4 * h + quarter, 0:STATE_ROW, :] = grad_map[
                quarter * 32 : quarter * 32 + 32, :
            ]
    for piece in range(32):
        payload_ref[piece, STATE_ROW : STATE_ROW + 8, :] = back[piece * 8 : piece * 8 + 8, :T]

    part = split2(feature_back(own, gkphi))
    grad_map = wide_exact_left(tn, k_s[WINDOW * T :, :T], part)
    back_parts = split2(jnp.concatenate([back[:, :T], back[:, T:] * (1.0 / T)], axis=1))
    at = 0
    for features in [part[0][...] for part in done] + [late]:
        rows = slice(at, at + features.shape[0])
        grad = exact_left(nt, v_s[rows, :], back_parts)
        part = split2(feature_back(features, grad))
        grad_map = grad_map + wide_exact_left(tn, k_s[rows, :T], part)
        at += features.shape[0]
    tail = jnp.concatenate(
        [
            backn[:, :T],
            backn[:, T:],
            jnp.broadcast_to(pos_ref[0:1, 0:1].astype(F32), (1, T)),
            jnp.zeros((1, T), F32),
        ],
        axis=0,
    )
    for piece in range(32):
        payload_ref[piece, KMAP_ROW:PIECE, :] = jnp.concatenate(
            [grad_map[piece * 4 : piece * 4 + 4, :], tail], axis=0
        )


def query_kernel(dlogit_ref, inner_ref, gn_ref, qmap_ref, gq_ref, gv_ref):
    for h in range(qmap_ref.shape[0]):
        at = slice(h * T, h * T + T)
        gq_ref[:, at] = product(nt, split2(dlogit_ref[at, :]), split2(qmap_ref[h]))
    gv_ref[...] = product(tn, split2(inner_ref[...]), split2(gn_ref[...]))


def middle_kernel(me_ref, got_ref, out_ref, norms_ref, state_s):
    pieces = got_ref.shape[0]
    total = got_ref[0]
    for i in range(1, pieces):
        total = total + got_ref[i]
    qmap, kmap = total[0:STATE_ROW, :], total[KMAP_ROW:NORM_ROW, :]
    squares = jnp.sum(qmap * qmap) + jnp.sum(kmap * kmap)
    parts = [part.astype(F32) for part in split3(jnp.full((1, T), squares, F32))]
    tail = jnp.concatenate([kmap] + parts + [jnp.zeros((1, T), F32)], axis=0).astype(BF16)
    qmap = qmap.astype(BF16)
    for j in range(pieces):
        out_ref[j, 0:HIGH_ROW, :] = qmap
        out_ref[j, KEY_ROW:REPLY, :] = tail
    sender = lax.broadcasted_iota(jnp.int32, (pieces, T), 0)
    target = lax.broadcasted_iota(jnp.int32, (pieces, T), 1)
    first = (sender * T).astype(F32) - got_ref[:, INFO_ROW, :]
    links = (sender > target) & (first <= (target * T + (T - 1)).astype(F32))
    reach = links.astype(F32)[:, :pieces].astype(BF16)
    for i in range(8):
        state_s[:, i, :] = exact_left(tn, reach, split3(got_ref[:, STATE_ROW + i, :]))
    high, low = split2(state_s[...])
    out_ref[:, HIGH_ROW:LOW_ROW, :] = high
    out_ref[:, LOW_ROW:KEY_ROW, :] = low
    me = me_ref[0]
    mine = (sender > me) & (first <= (me * T + (T - 1)).astype(F32))
    for half in range(2):
        norms_ref[0:1, half * T : half * T + T] = jnp.sum(
            jnp.where(mine, got_ref[:, NORM_ROW + half, :], 0.0), axis=0, keepdims=True
        )


def last_kernel(pos_ref, got_ref, norms_ref, v_ref, kmap_ref, phi_ref, gkphi_ref, gv_ref, gk_ref, gvo_ref):
    _, start = positions_of(pos_ref)
    last_start = float(T - 1) - pos_ref[0:1, T - 1 : T].astype(F32)
    keeping = (start == last_start).astype(F32)
    pieces = got_ref.shape[0]
    back = [
        jnp.concatenate([got_ref[r, at : at + 8, :] for r in range(pieces)], axis=0)
        for at in (HIGH_ROW, LOW_ROW)
    ]
    phi = phi_ref[...]
    own_v = v_ref[...]
    grad = gkphi_ref[...] + keeping * (exact_left(nt, own_v, back) + norms_ref[...])
    gvo_ref[...] = gv_ref[...] + keeping * product(nn, split2(phi), back)
    gk_ref[...] = product(nt, split2(feature_back(phi, grad)), split2(kmap_ref[0]))


def squares_kernel(tail_ref, out_ref):
    total = jnp.sum(tail_ref[:, KEY_ROW:REPLY, :].astype(F32), axis=0)
    total = jnp.sum(total[SQUARE_ROW - KEY_ROW : SQUARE_ROW - KEY_ROW + 3, :], axis=0)
    out_ref[...] = jnp.broadcast_to(total.reshape(1, 1, T), out_ref.shape)


def scale_kernel(limit, got_ref, squares_ref, qmap_ref, kmap_ref):
    pieces = got_ref.shape[0]
    squared = jnp.sum(squares_ref[:, 0, :], axis=0, keepdims=True)
    factor = jnp.minimum(1.0, limit / (jnp.sqrt(squared) + EPSILON))
    for piece in range(pieces):
        rows = slice(piece % 4 * 32, piece % 4 * 32 + 32)
        qmap_ref[piece // 4, rows, :] = factor * got_ref[piece, 0:HIGH_ROW, :].astype(F32)
        tail = got_ref[piece, KEY_ROW:REPLY, :].astype(F32)
        kmap_ref[0, piece * 4 : piece * 4 + 4, :] = factor * tail[0 : SQUARE_ROW - KEY_ROW, :]


def call(body, name, ins, outs, scratch=(), limit=32):
    return pl.pallas_call(
        body,
        in_specs=[pl.BlockSpec(memory_space=space) for space in ins],
        out_specs=[pl.BlockSpec(memory_space=pltpu.VMEM)] * len(outs),
        out_shape=[
            out if isinstance(out, jax.ShapeDtypeStruct) else jax.ShapeDtypeStruct(out, F32)
            for out in outs
        ],
        scratch_shapes=list(scratch),
        compiler_params=pltpu.CompilerParams(vmem_limit_bytes=limit << 20),
        name=name,
    )


def joined(a, b):
    return lax.pad(a, jnp.zeros((), a.dtype), ((0, b.shape[0], 0), (0, 0, 0))) + lax.pad(
        b, jnp.zeros((), b.dtype), ((a.shape[0], 0, 0), (0, 0, 0))
    )


def on_device(queries, key_vectors, value_vectors, positions, query_map, key_map):
    group = query_map.shape[0]
    pieces = lax.axis_size("seq")
    heads = lax.axis_size("head")
    rows = group * T
    me = lax.axis_index("seq").astype(jnp.int32).reshape(1)
    pos = positions.reshape(1, T)
    kv = joined(key_vectors, value_vectors)
    V = pltpu.VMEM

    def shift(x, k):
        return lax.ppermute(x, "seq", [(i, (i + k) % pieces) for i in range(pieces)])

    def part_of(name, arrays, places):
        size = T * sum(len(held) for held in places)
        return call(
            functools.partial(part_kernel, places),
            name,
            [V] * (3 + len(arrays)),
            [(size, 2 * T), (2 * T, 2 * T), (rows, T), (rows, T), (rows, T)],
            [V((size, 2 * T), BF16), V((size, 2 * T), BF16)],
            24,
        )(pos, queries, key_map, *arrays)

    b4, b8, b1, b7 = (shift(kv, k) for k in (4, 8, 1, 7))
    phi, inner, own = call(
        local_kernel, "local_features", [V] * 5, [(rows, 2 * T), (rows, T), (T, 2 * T)]
    )(pos, queries, key_vectors, query_map, key_map)
    b4, b8, b1, b7, own = lax.optimization_barrier((b4, b8, b1, b7, own))
    near = jnp.concatenate([b4, b8, b1, b7], axis=0)
    n1 = shift(jnp.concatenate([b1, b4], axis=0), 1)
    n2 = shift(jnp.concatenate([b4, b7], axis=0), -1)
    far = shift(near, 8)
    early = list(part_of("early_keys", [near], [(4, 8, 1, 7)]))
    n1, n2, early[1] = lax.optimization_barrier((n1, n2, early[1]))
    f1, f2 = shift(n1, 8), shift(n2, 8)
    middle = part_of("middle_keys", [far, n1, n2], [(12, 16, 9, 15), (2, 5), (3, 6)])
    arrays = [near, far, n1, n2, f1, f2, kv]
    places = [(4, 8, 1, 7), (12, 16, 9, 15), (2, 5), (3, 6), (10, 13), (11, 14), (0,)]
    payload, dlogit, grad_numer, gkphi = call(
        functools.partial(main_kernel, places, 2),
        "attention_transfer",
        [V] * (6 + len(arrays) + 10),
        [(pieces, PIECE, T), (rows, T), (rows, T), (T, 2 * T)],
        [V((KEYS, 2 * T), BF16), V((KEYS, 2 * T), BF16)],
        32,
    )(pos, queries, key_map, phi, inner, own, *arrays, *early, *middle)
    gathered = lax.all_to_all(payload, "seq", 0, 0)
    grad_queries, near_values = call(
        query_kernel, "query_gradients", [V] * 4, [(T, rows), (T, T)]
    )(dlogit, inner, grad_numer, query_map)
    reduced, norms = call(
        middle_kernel,
        "sum_pieces",
        [pltpu.SMEM, V],
        [jax.ShapeDtypeStruct((pieces, REPLY, T), BF16), (1, 2 * T)],
        [V((pieces, 8, T), F32)],
    )(me, gathered)
    back = lax.all_to_all(reduced, "seq", 0, 0)
    squares = call(squares_kernel, "head_squares", [V], [(heads, 8, T)])(back)[0]
    squares = lax.all_to_all(squares, "head", 0, 0)
    grad_keys, grad_values = call(last_kernel, "key_gradients", [V] * 8, [(T, T), (T, T)])(
        pos, back, norms, value_vectors, key_map, own, gkphi, near_values
    )
    clip_limit = 0.25 * math.sqrt((group + 1) * heads * T * T)
    query_map_grad, key_map_grad = call(
        functools.partial(scale_kernel, clip_limit),
        "clip_maps",
        [V] * 2,
        [(group, T, T), (1, T, T)],
    )(back, squares)
    return (grad_queries, grad_keys, grad_values, query_map_grad, key_map_grad)


def solution(mesh):
    placed = (
        P("seq", "head"),
        P("seq", "head"),
        P("seq", "head"),
        P("seq"),
        P("head", None, None),
        P("head", None, None),
    )
    return jax.shard_map(
        on_device,
        mesh=mesh,
        in_specs=placed,
        out_specs=(
            P("seq", "head"),
            P("seq", "head"),
            P("seq", "head"),
            P("head", None, None),
            P("head", None, None),
        ),
        check_vma=False,
    )
```

```python
import functools
import math

import jax
import jax.numpy as jnp
from jax import lax
from jax.experimental import pallas as pl
from jax.experimental.pallas import tpu as pltpu
from jax.sharding import PartitionSpec as P

F32 = jnp.float32
BF16 = jnp.bfloat16
NEGATIVE = -1e30
EPSILON = 1e-06
T = 128
WINDOW = 16
KEYS = (WINDOW + 1) * T
TEACHER = 512
PIECE = 48
STATE_ROW, KMAP_ROW, NORM_ROW, INFO_ROW = 32, 40, 44, 46
REPLY = 56
HIGH_ROW, LOW_ROW, KEY_ROW, SQUARE_ROW = 32, 40, 48, 52


def nn(a, b):
    return lax.dot_general(a, b, (((1,), (0,)), ((), ())), preferred_element_type=F32)


def nt(a, b):
    return lax.dot_general(a, b, (((1,), (1,)), ((), ())), preferred_element_type=F32)


def tn(a, b):
    return lax.dot_general(a, b, (((0,), (0,)), ((), ())), preferred_element_type=F32)


def split2(x):
    high = x.astype(BF16)
    return high, (x - high.astype(F32)).astype(BF16)


def split3(x):
    high = x.astype(BF16)
    rest = x - high.astype(F32)
    middle = rest.astype(BF16)
    return high, middle, (rest - middle.astype(F32)).astype(BF16)


def product(form, a, b):
    return form(a[0], b[0]) + (form(a[0], b[1]) + form(a[1], b[0]))


def exact_left(form, a, parts):
    total = form(a, parts[-1])
    for part in parts[-2::-1]:
        total = total + form(a, part)
    return total


def exact_right(form, parts, b):
    return form(parts[0], b) + form(parts[1], b)


def deep(parts):
    return jnp.concatenate(parts, axis=1)


def deep_exact_right(form, parts, b):
    return form(deep(parts), jnp.concatenate([b, b], axis=0 if form is nn else 1))


def deep_product(form, a, b):
    return deep_exact_right(form, a, b[0]) + form(a[0], b[1])


def wide_exact_left(form, a, parts):
    both = form(a, deep(parts))
    return both[:, :T] + both[:, T:]


def row_sums(x):
    return nn(deep(split2(x)), jnp.ones((2 * T, T), BF16))


def half_sums(x):
    i = lax.broadcasted_iota(jnp.int32, (2 * T, 2 * T), 0) < T
    j = lax.broadcasted_iota(jnp.int32, (2 * T, 2 * T), 1) < T
    return exact_right(nn, split2(x), (i == j).astype(F32).astype(BF16))


def map_of(weights):
    high, middle, low = split3(weights)
    rest = jnp.concatenate([middle, jnp.zeros_like(middle)], axis=1)
    return jnp.concatenate([deep([high, low]), rest], axis=0)


def logits_of(x, matrix):
    both = nn(deep([x, x]), matrix)
    return both[:, :T] + both[:, T:]


def feature_map(logits):
    upper = jnp.exp(logits - jnp.max(logits, axis=-1, keepdims=True))
    lower = jnp.exp(jnp.min(logits, axis=-1, keepdims=True) - logits)
    both = deep([upper, lower])
    return both / half_sums(both)


def feature_back(phi, grad):
    both = phi * (grad - half_sums(phi * grad))
    return both[:, :T] - both[:, T:]


def column_of(row):
    i = lax.broadcasted_iota(jnp.int32, (T, T), 0)
    j = lax.broadcasted_iota(jnp.int32, (T, T), 1)
    return jnp.sum(jnp.where(i == j, row, 0.0), axis=1, keepdims=True)


def stacked(ref):
    return jnp.concatenate([ref[:, h * T : h * T + T] for h in range(ref.shape[1] // T)], axis=0)


def every_head(x, heads):
    return jnp.concatenate([x] * heads, axis=0)


def positions_of(pos_ref):
    row = lax.broadcasted_iota(jnp.int32, (T, 1), 0).astype(F32)
    return row, row - column_of(pos_ref[...].astype(F32))


def local_kernel(pos_ref, q_ref, k_ref, qmap_ref, kmap_ref, phi_ref, inner_ref, own_ref):
    heads = qmap_ref.shape[0]
    row, start = positions_of(pos_ref)
    key = lax.broadcasted_iota(jnp.int32, (T, T), 1).astype(F32)
    seen = every_head(((key <= row) & (key >= start)).astype(F32), heads)
    own = feature_map(logits_of(k_ref[...], map_of(kmap_ref[0])))
    own_ref[...] = own
    logits = jnp.concatenate(
        [logits_of(q_ref[:, h * T : h * T + T], map_of(qmap_ref[h])) for h in range(heads)],
        axis=0,
    )
    phi = feature_map(logits)
    phi_ref[...] = phi
    inner_ref[...] = product(nt, split2(phi), split2(own)) * seen


def hold_keys(arrays, places, pos_ref, k_s, v_s):
    row = lax.broadcasted_iota(jnp.int32, (T, 1), 0).astype(F32)
    entry = -pos_ref[0:1, 0:1].astype(F32)
    lane = lax.broadcasted_iota(jnp.int32, (T, T), 1)
    at = 0
    keys = []
    for ref, held in zip(arrays, places):
        for slot, block in enumerate(held):
            k_s[at : at + T, :T] = ref[slot * 2 * T : slot * 2 * T + T, :]
            v_s[at : at + T, :T] = ref[slot * 2 * T + T : slot * 2 * T + 2 * T, :]
            key = row - float(block * T)
            hidden = jnp.where(key >= entry, 0.0, NEGATIVE)
            hidden = jnp.where(lane == 0, NEGATIVE, jnp.where(lane == 1, hidden, 0.0))
            k_s[at : at + T, T:] = (hidden if block else jnp.zeros((T, T), F32)).astype(BF16)
            keys.append(key)
            at += T
    v_s[:, T:] = jnp.ones(v_s[:, T:].shape, BF16)
    return keys, entry


def key_features(rows, keys, entry, matrix, k_s, v_s):
    features = feature_map(logits_of(k_s[rows, :T], matrix))
    features = jnp.where(jnp.concatenate(keys, axis=0) >= entry, features, 0.0)
    return features, exact_right(tn, split2(features), v_s[rows, :])


def asking(q_ref, crossing):
    heads = q_ref.shape[1] // T
    lane = lax.broadcasted_iota(jnp.int32, (T, T), 1)
    hider = jnp.where(lane == 0, 1.0 - crossing, jnp.where(lane == 1, 1.0, 0.0)).astype(BF16)
    return deep([stacked(q_ref), every_head(hider, heads)])


RATE = math.log2(math.e) / math.sqrt(T)


def part_kernel(places, pos_ref, q_ref, kmap_ref, *rest):
    count = len(places)
    phi_ref, state_ref, top_ref, total_ref, sum_ref = rest[count : count + 5]
    k_s, v_s = rest[count + 5 :]
    _, start = positions_of(pos_ref)
    keys, entry = hold_keys(rest[:count], places, pos_ref, k_s, v_s)
    phi_ref[...], state_ref[...] = key_features(
        slice(None), keys, entry, map_of(kmap_ref[0]), k_s, v_s
    )
    queries = asking(q_ref, (start < 0.0).astype(F32))
    for at in range(0, queries.shape[0], TEACHER):
        rows = slice(at, at + TEACHER)
        scores = nt(queries[rows, :], k_s[...])
        top = jnp.max(scores, axis=-1, keepdims=True)
        weights = jnp.exp2((scores - top) * RATE)
        total = jnp.sum(weights, axis=-1, keepdims=True)
        sum_ref[rows, :] = nn(weights.astype(BF16), v_s[:, :T])
        top_ref[rows, :] = jnp.broadcast_to(top, (TEACHER, T))
        total_ref[rows, :] = jnp.broadcast_to(total, (TEACHER, T))


def main_kernel(places, parts, pos_ref, q_ref, kmap_ref, phi_ref, inner_ref, own_ref, *rest):
    count = len(places)
    blocks = rest[:count]
    done = [rest[count + 5 * i : count + 5 * i + 5] for i in range(parts)]
    rest = rest[count + 5 * parts :]
    payload_ref, dlogit_ref, gn_ref, gkphi_ref, k_s, v_s = rest
    heads = q_ref.shape[1] // T
    row, start = positions_of(pos_ref)
    crossing = (start < 0.0).astype(F32)
    keys, entry = hold_keys(blocks, places, pos_ref, k_s, v_s)
    first = sum(part[0].shape[0] for part in done)
    late, state = key_features(
        slice(first, WINDOW * T), keys[first // T : WINDOW], entry, map_of(kmap_ref[0]), k_s, v_s
    )
    for part in done:
        state = state + part[1][...]
    norms = jnp.transpose(state[:, T:])[0:1, :]
    state = split2(state)

    own_key = lax.broadcasted_iota(jnp.int32, (T, T), 1).astype(F32)
    visible = (own_key <= row) & (own_key >= start)
    seen = every_head(visible.astype(F32), heads)
    bias = every_head(jnp.where(visible, 0.0, NEGATIVE), heads)
    cross = every_head(jnp.broadcast_to(crossing, (T, T)), heads)
    queries = asking(q_ref, crossing)
    own_v = v_s[WINDOW * T :, :]
    teachers = []
    for at in range(0, heads * T, TEACHER):
        rows = slice(at, at + TEACHER)
        scores = nt(queries[rows, :], k_s[first:, :])
        near = scores[:, WINDOW * T - first :] + bias[rows, :]
        far = scores[:, : WINDOW * T - first]
        top = jnp.maximum(
            jnp.max(near, axis=-1, keepdims=True), jnp.max(far, axis=-1, keepdims=True)
        )
        top = jnp.broadcast_to(top, (TEACHER, T))
        for part in done:
            top = jnp.maximum(top, part[2][rows, :])
        near = jnp.exp2((near - top) * RATE)
        far = jnp.exp2((far - top[:, 0:1]) * RATE)
        total = jnp.sum(near, axis=-1, keepdims=True) + jnp.sum(far, axis=-1, keepdims=True)
        summed = nn(deep([far, near]).astype(BF16), v_s[first:, :T])
        for part in done:
            fading = jnp.exp2((part[2][rows, :] - top) * RATE)
            total = total + fading * part[3][rows, :]
            summed = summed + fading * part[4][rows, :]
        teachers.append(summed / total)
    teacher = jnp.concatenate(teachers, axis=0)

    own = own_ref[...]
    own_phi = split2(own)
    phi = phi_ref[...]
    phi_parts = split2(phi)
    near = deep_exact_right(nn, split2(inner_ref[...]), own_v)
    far = product(nn, phi_parts, state)
    inverse = 1.0 / (near[:, T:] + cross * far[:, T:])
    outputs = (near[:, :T] + cross * far[:, :T]) * inverse
    error = outputs - teacher

    grad_numer = error * inverse
    grad_denom = -row_sums(error * outputs) * inverse
    gn_ref[...] = grad_numer
    far_numer = cross * grad_numer
    far_denom = cross * grad_denom
    mixing = (deep_exact_right(nt, split2(grad_numer), own_v[:, :T]) + grad_denom) * seen
    mixing_parts = split2(mixing)
    near = deep_product(nn, mixing_parts, own_phi)
    far = deep_product(nt, split2(far_numer), [part[:, :T] for part in state])
    grad_phi = jnp.concatenate(
        [
            near[:, :T] + far[:, :T] + far_denom * norms[:, :T],
            near[:, T:] + far[:, T:] + far_denom * norms[:, T:],
        ],
        axis=1,
    )
    back = product(tn, phi_parts, split2(jnp.concatenate([far_numer, far_denom], axis=1)))
    backn = jnp.transpose(back[:, T:])[0:1, :]
    gkphi = product(tn, mixing_parts, phi_parts)
    gkphi_ref[...] = gkphi
    dlogit = feature_back(phi, grad_phi)
    dlogit_ref[...] = dlogit
    dlogit_parts = split2(dlogit)
    for h in range(heads):
        at = slice(h * T, h * T + T)
        grad_map = wide_exact_left(tn, q_ref[:, at], [part[at, :] for part in dlogit_parts])
        for quarter in range(4):
            payload_ref[4 * h + quarter, 0:STATE_ROW, :] = grad_map[
                quarter * 32 : quarter * 32 + 32, :
            ]
    for piece in range(32):
        payload_ref[piece, STATE_ROW : STATE_ROW + 8, :] = back[piece * 8 : piece * 8 + 8, :T]

    part = split2(feature_back(own, gkphi))
    grad_map = wide_exact_left(tn, k_s[WINDOW * T :, :T], part)
    back_parts = split2(jnp.concatenate([back[:, :T], back[:, T:] * (1.0 / T)], axis=1))
    at = 0
    for features in [part[0][...] for part in done] + [late]:
        rows = slice(at, at + features.shape[0])
        grad = exact_left(nt, v_s[rows, :], back_parts)
        part = split2(feature_back(features, grad))
        grad_map = grad_map + wide_exact_left(tn, k_s[rows, :T], part)
        at += features.shape[0]
    tail = jnp.concatenate(
        [
            backn[:, :T],
            backn[:, T:],
            jnp.broadcast_to(pos_ref[0:1, 0:1].astype(F32), (1, T)),
            jnp.zeros((1, T), F32),
        ],
        axis=0,
    )
    for piece in range(32):
        payload_ref[piece, KMAP_ROW:PIECE, :] = jnp.concatenate(
            [grad_map[piece * 4 : piece * 4 + 4, :], tail], axis=0
        )


def query_kernel(dlogit_ref, inner_ref, gn_ref, qmap_ref, gq_ref, gv_ref):
    for h in range(qmap_ref.shape[0]):
        at = slice(h * T, h * T + T)
        gq_ref[:, at] = product(nt, split2(dlogit_ref[at, :]), split2(qmap_ref[h]))
    gv_ref[...] = product(tn, split2(inner_ref[...]), split2(gn_ref[...]))


def middle_kernel(me_ref, got_ref, out_ref, norms_ref, state_s):
    pieces = got_ref.shape[0]
    total = got_ref[0]
    for i in range(1, pieces):
        total = total + got_ref[i]
    qmap, kmap = total[0:STATE_ROW, :], total[KMAP_ROW:NORM_ROW, :]
    squares = jnp.sum(qmap * qmap) + jnp.sum(kmap * kmap)
    parts = [part.astype(F32) for part in split3(jnp.full((1, T), squares, F32))]
    tail = jnp.concatenate([kmap] + parts + [jnp.zeros((1, T), F32)], axis=0).astype(BF16)
    qmap = qmap.astype(BF16)
    for j in range(pieces):
        out_ref[j, 0:HIGH_ROW, :] = qmap
        out_ref[j, KEY_ROW:REPLY, :] = tail
    sender = lax.broadcasted_iota(jnp.int32, (pieces, T), 0)
    target = lax.broadcasted_iota(jnp.int32, (pieces, T), 1)
    first = (sender * T).astype(F32) - got_ref[:, INFO_ROW, :]
    links = (sender > target) & (first <= (target * T + (T - 1)).astype(F32))
    reach = links.astype(F32)[:, :pieces].astype(BF16)
    for i in range(8):
        state_s[:, i, :] = exact_left(tn, reach, split3(got_ref[:, STATE_ROW + i, :]))
    high, low = split2(state_s[...])
    out_ref[:, HIGH_ROW:LOW_ROW, :] = high
    out_ref[:, LOW_ROW:KEY_ROW, :] = low
    me = me_ref[0]
    mine = (sender > me) & (first <= (me * T + (T - 1)).astype(F32))
    for half in range(2):
        norms_ref[0:1, half * T : half * T + T] = jnp.sum(
            jnp.where(mine, got_ref[:, NORM_ROW + half, :], 0.0), axis=0, keepdims=True
        )


def last_kernel(pos_ref, got_ref, norms_ref, v_ref, kmap_ref, phi_ref, gkphi_ref, gv_ref, gk_ref, gvo_ref):
    _, start = positions_of(pos_ref)
    last_start = float(T - 1) - pos_ref[0:1, T - 1 : T].astype(F32)
    keeping = (start == last_start).astype(F32)
    pieces = got_ref.shape[0]
    back = [
        jnp.concatenate([got_ref[r, at : at + 8, :] for r in range(pieces)], axis=0)
        for at in (HIGH_ROW, LOW_ROW)
    ]
    phi = phi_ref[...]
    own_v = v_ref[...]
    grad = gkphi_ref[...] + keeping * (exact_left(nt, own_v, back) + norms_ref[...])
    gvo_ref[...] = gv_ref[...] + keeping * product(nn, split2(phi), back)
    gk_ref[...] = product(nt, split2(feature_back(phi, grad)), split2(kmap_ref[0]))


def squares_kernel(tail_ref, out_ref):
    total = jnp.sum(tail_ref[:, KEY_ROW:REPLY, :].astype(F32), axis=0)
    total = jnp.sum(total[SQUARE_ROW - KEY_ROW : SQUARE_ROW - KEY_ROW + 3, :], axis=0)
    out_ref[...] = jnp.broadcast_to(total.reshape(1, 1, T), out_ref.shape)


def scale_kernel(limit, got_ref, squares_ref, qmap_ref, kmap_ref):
    pieces = got_ref.shape[0]
    squared = jnp.sum(squares_ref[:, 0, :], axis=0, keepdims=True)
    factor = jnp.minimum(1.0, limit / (jnp.sqrt(squared) + EPSILON))
    for piece in range(pieces):
        rows = slice(piece % 4 * 32, piece % 4 * 32 + 32)
        qmap_ref[piece // 4, rows, :] = factor * got_ref[piece, 0:HIGH_ROW, :].astype(F32)
        tail = got_ref[piece, KEY_ROW:REPLY, :].astype(F32)
        kmap_ref[0, piece * 4 : piece * 4 + 4, :] = factor * tail[0 : SQUARE_ROW - KEY_ROW, :]


def call(body, name, ins, outs, scratch=(), limit=32):
    return pl.pallas_call(
        body,
        in_specs=[pl.BlockSpec(memory_space=space) for space in ins],
        out_specs=[pl.BlockSpec(memory_space=pltpu.VMEM)] * len(outs),
        out_shape=[
            out if isinstance(out, jax.ShapeDtypeStruct) else jax.ShapeDtypeStruct(out, F32)
            for out in outs
        ],
        scratch_shapes=list(scratch),
        compiler_params=pltpu.CompilerParams(vmem_limit_bytes=limit << 20),
        name=name,
    )


def joined(a, b):
    return lax.pad(a, jnp.zeros((), a.dtype), ((0, b.shape[0], 0), (0, 0, 0))) + lax.pad(
        b, jnp.zeros((), b.dtype), ((a.shape[0], 0, 0), (0, 0, 0))
    )


def on_device(queries, key_vectors, value_vectors, positions, query_map, key_map):
    group = query_map.shape[0]
    pieces = lax.axis_size("seq")
    heads = lax.axis_size("head")
    rows = group * T
    me = lax.axis_index("seq").astype(jnp.int32).reshape(1)
    pos = positions.reshape(1, T)
    kv = joined(key_vectors, value_vectors)
    V = pltpu.VMEM

    def shift(x, k):
        return lax.ppermute(x, "seq", [(i, (i + k) % pieces) for i in range(pieces)])

    def part_of(name, arrays, places):
        size = T * sum(len(held) for held in places)
        return call(
            functools.partial(part_kernel, places),
            name,
            [V] * (3 + len(arrays)),
            [(size, 2 * T), (2 * T, 2 * T), (rows, T), (rows, T), (rows, T)],
            [V((size, 2 * T), BF16), V((size, 2 * T), BF16)],
            24,
        )(pos, queries, key_map, *arrays)

    b4, b8, b1, b7 = (shift(kv, k) for k in (4, 8, 1, 7))
    phi, inner, own = call(
        local_kernel, "local_features", [V] * 5, [(rows, 2 * T), (rows, T), (T, 2 * T)]
    )(pos, queries, key_vectors, query_map, key_map)
    b4, b8, b1, b7, own = lax.optimization_barrier((b4, b8, b1, b7, own))
    near = jnp.concatenate([b4, b8, b1, b7], axis=0)
    near, b4, b1, b7 = lax.optimization_barrier((near, b4, b1, b7))
    far = shift(near, 8)
    n1 = shift(jnp.concatenate([b1, b4], axis=0), 1)
    n2 = shift(jnp.concatenate([b4, b7], axis=0), -1)
    early = list(part_of("early_keys", [near], [(4, 8, 1, 7)]))
    n1, n2, far, early[1] = lax.optimization_barrier((n1, n2, far, early[1]))
    f1, f2 = shift(n1, 8), shift(n2, 8)
    middle = part_of("middle_keys", [far, n1, n2], [(12, 16, 9, 15), (2, 5), (3, 6)])
    arrays = [near, far, n1, n2, f1, f2, kv]
    places = [(4, 8, 1, 7), (12, 16, 9, 15), (2, 5), (3, 6), (10, 13), (11, 14), (0,)]
    payload, dlogit, grad_numer, gkphi = call(
        functools.partial(main_kernel, places, 2),
        "attention_transfer",
        [V] * (6 + len(arrays) + 10),
        [(pieces, PIECE, T), (rows, T), (rows, T), (T, 2 * T)],
        [V((KEYS, 2 * T), BF16), V((KEYS, 2 * T), BF16)],
        32,
    )(pos, queries, key_map, phi, inner, own, *arrays, *early, *middle)
    gathered = lax.all_to_all(payload, "seq", 0, 0)
    grad_queries, near_values = call(
        query_kernel, "query_gradients", [V] * 4, [(T, rows), (T, T)]
    )(dlogit, inner, grad_numer, query_map)
    reduced, norms = call(
        middle_kernel,
        "sum_pieces",
        [pltpu.SMEM, V],
        [jax.ShapeDtypeStruct((pieces, REPLY, T), BF16), (1, 2 * T)],
        [V((pieces, 8, T), F32)],
    )(me, gathered)
    back = lax.all_to_all(reduced, "seq", 0, 0)
    squares = call(squares_kernel, "head_squares", [V], [(heads, 8, T)])(back)[0]
    squares = lax.all_to_all(squares, "head", 0, 0)
    grad_keys, grad_values = call(last_kernel, "key_gradients", [V] * 8, [(T, T), (T, T)])(
        pos, back, norms, value_vectors, key_map, own, gkphi, near_values
    )
    clip_limit = 0.25 * math.sqrt((group + 1) * heads * T * T)
    query_map_grad, key_map_grad = call(
        functools.partial(scale_kernel, clip_limit),
        "clip_maps",
        [V] * 2,
        [(group, T, T), (1, T, T)],
    )(back, squares)
    return (grad_queries, grad_keys, grad_values, query_map_grad, key_map_grad)


def solution(mesh):
    placed = (
        P("seq", "head"),
        P("seq", "head"),
        P("seq", "head"),
        P("seq"),
        P("head", None, None),
        P("head", None, None),
    )
    return jax.shard_map(
        on_device,
        mesh=mesh,
        in_specs=placed,
        out_specs=(
            P("seq", "head"),
            P("seq", "head"),
            P("seq", "head"),
            P("head", None, None),
            P("head", None, None),
        ),
        check_vma=False,
    )
```

```python
import functools
import math

import jax
import jax.numpy as jnp
from jax import lax
from jax.experimental import pallas as pl
from jax.experimental.pallas import tpu as pltpu
from jax.sharding import PartitionSpec as P

F32 = jnp.float32
BF16 = jnp.bfloat16
NEGATIVE = -1e30
EPSILON = 1e-06
T = 128
WINDOW = 16
KEYS = (WINDOW + 1) * T
TEACHER = 512
PIECE = 48
STATE_ROW, KMAP_ROW, NORM_ROW, INFO_ROW = 32, 40, 44, 46
REPLY = 56
HIGH_ROW, LOW_ROW, KEY_ROW, SQUARE_ROW = 32, 40, 48, 52


def nn(a, b):
    return lax.dot_general(a, b, (((1,), (0,)), ((), ())), preferred_element_type=F32)


def nt(a, b):
    return lax.dot_general(a, b, (((1,), (1,)), ((), ())), preferred_element_type=F32)


def tn(a, b):
    return lax.dot_general(a, b, (((0,), (0,)), ((), ())), preferred_element_type=F32)


def split2(x):
    high = x.astype(BF16)
    return high, (x - high.astype(F32)).astype(BF16)


def split3(x):
    high = x.astype(BF16)
    rest = x - high.astype(F32)
    middle = rest.astype(BF16)
    return high, middle, (rest - middle.astype(F32)).astype(BF16)


def product(form, a, b):
    return form(a[0], b[0]) + (form(a[0], b[1]) + form(a[1], b[0]))


def exact_left(form, a, parts):
    total = form(a, parts[-1])
    for part in parts[-2::-1]:
        total = total + form(a, part)
    return total


def exact_right(form, parts, b):
    return form(parts[0], b) + form(parts[1], b)


def deep(parts):
    return jnp.concatenate(parts, axis=1)


def deep_exact_right(form, parts, b):
    return form(deep(parts), jnp.concatenate([b, b], axis=0 if form is nn else 1))


def deep_product(form, a, b):
    return deep_exact_right(form, a, b[0]) + form(a[0], b[1])


def wide_exact_left(form, a, parts):
    both = form(a, deep(parts))
    return both[:, :T] + both[:, T:]


def row_sums(x):
    return nn(deep(split2(x)), jnp.ones((2 * T, T), BF16))


def half_sums(x):
    i = lax.broadcasted_iota(jnp.int32, (2 * T, 2 * T), 0) < T
    j = lax.broadcasted_iota(jnp.int32, (2 * T, 2 * T), 1) < T
    return exact_right(nn, split2(x), (i == j).astype(F32).astype(BF16))


def map_of(weights):
    high, middle, low = split3(weights)
    rest = jnp.concatenate([middle, jnp.zeros_like(middle)], axis=1)
    return jnp.concatenate([deep([high, low]), rest], axis=0)


def logits_of(x, matrix):
    both = nn(deep([x, x]), matrix)
    return both[:, :T] + both[:, T:]


def feature_map(logits):
    upper = jnp.exp(logits - jnp.max(logits, axis=-1, keepdims=True))
    lower = jnp.exp(jnp.min(logits, axis=-1, keepdims=True) - logits)
    both = deep([upper, lower])
    return both / half_sums(both)


def feature_back(phi, grad):
    both = phi * (grad - half_sums(phi * grad))
    return both[:, :T] - both[:, T:]


def column_of(row):
    i = lax.broadcasted_iota(jnp.int32, (T, T), 0)
    j = lax.broadcasted_iota(jnp.int32, (T, T), 1)
    return jnp.sum(jnp.where(i == j, row, 0.0), axis=1, keepdims=True)


def stacked(ref):
    return jnp.concatenate([ref[:, h * T : h * T + T] for h in range(ref.shape[1] // T)], axis=0)


def every_head(x, heads):
    return jnp.concatenate([x] * heads, axis=0)


def positions_of(pos_ref):
    row = lax.broadcasted_iota(jnp.int32, (T, 1), 0).astype(F32)
    return row, row - column_of(pos_ref[...].astype(F32))


def local_kernel(pos_ref, q_ref, k_ref, qmap_ref, kmap_ref, phi_ref, inner_ref, own_ref):
    heads = qmap_ref.shape[0]
    row, start = positions_of(pos_ref)
    key = lax.broadcasted_iota(jnp.int32, (T, T), 1).astype(F32)
    seen = every_head(((key <= row) & (key >= start)).astype(F32), heads)
    own = feature_map(logits_of(k_ref[...], map_of(kmap_ref[0])))
    own_ref[...] = own
    logits = jnp.concatenate(
        [logits_of(q_ref[:, h * T : h * T + T], map_of(qmap_ref[h])) for h in range(heads)],
        axis=0,
    )
    phi = feature_map(logits)
    phi_ref[...] = phi
    inner_ref[...] = product(nt, split2(phi), split2(own)) * seen


def hold_keys(arrays, places, pos_ref, k_s, v_s):
    row = lax.broadcasted_iota(jnp.int32, (T, 1), 0).astype(F32)
    entry = -pos_ref[0:1, 0:1].astype(F32)
    lane = lax.broadcasted_iota(jnp.int32, (T, T), 1)
    at = 0
    keys = []
    for ref, held in zip(arrays, places):
        for slot, block in enumerate(held):
            k_s[at : at + T, :T] = ref[slot * 2 * T : slot * 2 * T + T, :]
            v_s[at : at + T, :T] = ref[slot * 2 * T + T : slot * 2 * T + 2 * T, :]
            key = row - float(block * T)
            hidden = jnp.where(key >= entry, 0.0, NEGATIVE)
            hidden = jnp.where(lane == 0, NEGATIVE, jnp.where(lane == 1, hidden, 0.0))
            k_s[at : at + T, T:] = (hidden if block else jnp.zeros((T, T), F32)).astype(BF16)
            keys.append(key)
            at += T
    v_s[:, T:] = jnp.ones(v_s[:, T:].shape, BF16)
    return keys, entry


def key_features(rows, keys, entry, matrix, k_s, v_s):
    features = feature_map(logits_of(k_s[rows, :T], matrix))
    features = jnp.where(jnp.concatenate(keys, axis=0) >= entry, features, 0.0)
    return features, exact_right(tn, split2(features), v_s[rows, :])


def asking(q_ref, crossing):
    heads = q_ref.shape[1] // T
    lane = lax.broadcasted_iota(jnp.int32, (T, T), 1)
    hider = jnp.where(lane == 0, 1.0 - crossing, jnp.where(lane == 1, 1.0, 0.0)).astype(BF16)
    return deep([stacked(q_ref), every_head(hider, heads)])


RATE = math.log2(math.e) / math.sqrt(T)


def part_kernel(places, pos_ref, q_ref, kmap_ref, *rest):
    count = len(places)
    phi_ref, state_ref, top_ref, total_ref, sum_ref = rest[count : count + 5]
    k_s, v_s = rest[count + 5 :]
    _, start = positions_of(pos_ref)
    keys, entry = hold_keys(rest[:count], places, pos_ref, k_s, v_s)
    phi_ref[...], state_ref[...] = key_features(
        slice(None), keys, entry, map_of(kmap_ref[0]), k_s, v_s
    )
    queries = asking(q_ref, (start < 0.0).astype(F32))
    for at in range(0, queries.shape[0], TEACHER):
        rows = slice(at, at + TEACHER)
        scores = nt(queries[rows, :], k_s[...])
        top = jnp.max(scores, axis=-1, keepdims=True)
        weights = jnp.exp2((scores - top) * RATE)
        total = jnp.sum(weights, axis=-1, keepdims=True)
        sum_ref[rows, :] = nn(weights.astype(BF16), v_s[:, :T])
        top_ref[rows, :] = jnp.broadcast_to(top, (TEACHER, T))
        total_ref[rows, :] = jnp.broadcast_to(total, (TEACHER, T))


def main_kernel(places, parts, pos_ref, q_ref, kmap_ref, phi_ref, inner_ref, own_ref, *rest):
    count = len(places)
    blocks = rest[:count]
    done = [rest[count + 5 * i : count + 5 * i + 5] for i in range(parts)]
    rest = rest[count + 5 * parts :]
    payload_ref, dlogit_ref, gn_ref, gkphi_ref, k_s, v_s = rest
    heads = q_ref.shape[1] // T
    row, start = positions_of(pos_ref)
    crossing = (start < 0.0).astype(F32)
    keys, entry = hold_keys(blocks, places, pos_ref, k_s, v_s)
    first = sum(part[0].shape[0] for part in done)
    late, state = key_features(
        slice(first, WINDOW * T), keys[first // T : WINDOW], entry, map_of(kmap_ref[0]), k_s, v_s
    )
    for part in done:
        state = state + part[1][...]
    norms = jnp.transpose(state[:, T:])[0:1, :]
    state = split2(state)

    own_key = lax.broadcasted_iota(jnp.int32, (T, T), 1).astype(F32)
    visible = (own_key <= row) & (own_key >= start)
    seen = every_head(visible.astype(F32), heads)
    bias = every_head(jnp.where(visible, 0.0, NEGATIVE), heads)
    cross = every_head(jnp.broadcast_to(crossing, (T, T)), heads)
    queries = asking(q_ref, crossing)
    own_v = v_s[WINDOW * T :, :]
    teachers = []
    for at in range(0, heads * T, TEACHER):
        rows = slice(at, at + TEACHER)
        scores = nt(queries[rows, :], k_s[first:, :])
        near = scores[:, WINDOW * T - first :] + bias[rows, :]
        far = scores[:, : WINDOW * T - first]
        top = jnp.maximum(
            jnp.max(near, axis=-1, keepdims=True), jnp.max(far, axis=-1, keepdims=True)
        )
        top = jnp.broadcast_to(top, (TEACHER, T))
        for part in done:
            top = jnp.maximum(top, part[2][rows, :])
        near = jnp.exp2((near - top) * RATE)
        far = jnp.exp2((far - top[:, 0:1]) * RATE)
        total = jnp.sum(near, axis=-1, keepdims=True) + jnp.sum(far, axis=-1, keepdims=True)
        summed = nn(deep([far, near]).astype(BF16), v_s[first:, :T])
        for part in done:
            fading = jnp.exp2((part[2][rows, :] - top) * RATE)
            total = total + fading * part[3][rows, :]
            summed = summed + fading * part[4][rows, :]
        teachers.append(summed / total)
    teacher = jnp.concatenate(teachers, axis=0)

    own = own_ref[...]
    own_phi = split2(own)
    phi = phi_ref[...]
    phi_parts = split2(phi)
    near = deep_exact_right(nn, split2(inner_ref[...]), own_v)
    far = product(nn, phi_parts, state)
    inverse = 1.0 / (near[:, T:] + cross * far[:, T:])
    outputs = (near[:, :T] + cross * far[:, :T]) * inverse
    error = outputs - teacher

    grad_numer = error * inverse
    grad_denom = -row_sums(error * outputs) * inverse
    gn_ref[...] = grad_numer
    far_numer = cross * grad_numer
    far_denom = cross * grad_denom
    mixing = (deep_exact_right(nt, split2(grad_numer), own_v[:, :T]) + grad_denom) * seen
    mixing_parts = split2(mixing)
    near = deep_product(nn, mixing_parts, own_phi)
    far = deep_product(nt, split2(far_numer), [part[:, :T] for part in state])
    grad_phi = jnp.concatenate(
        [
            near[:, :T] + far[:, :T] + far_denom * norms[:, :T],
            near[:, T:] + far[:, T:] + far_denom * norms[:, T:],
        ],
        axis=1,
    )
    back = product(tn, phi_parts, split2(jnp.concatenate([far_numer, far_denom], axis=1)))
    backn = jnp.transpose(back[:, T:])[0:1, :]
    gkphi = product(tn, mixing_parts, phi_parts)
    gkphi_ref[...] = gkphi
    dlogit = feature_back(phi, grad_phi)
    dlogit_ref[...] = dlogit
    dlogit_parts = split2(dlogit)
    for h in range(heads):
        at = slice(h * T, h * T + T)
        grad_map = wide_exact_left(tn, q_ref[:, at], [part[at, :] for part in dlogit_parts])
        for quarter in range(4):
            payload_ref[4 * h + quarter, 0:STATE_ROW, :] = grad_map[
                quarter * 32 : quarter * 32 + 32, :
            ]
    for piece in range(32):
        payload_ref[piece, STATE_ROW : STATE_ROW + 8, :] = back[piece * 8 : piece * 8 + 8, :T]

    part = split2(feature_back(own, gkphi))
    grad_map = wide_exact_left(tn, k_s[WINDOW * T :, :T], part)
    back_parts = split2(jnp.concatenate([back[:, :T], back[:, T:] * (1.0 / T)], axis=1))
    at = 0
    for features in [part[0][...] for part in done] + [late]:
        rows = slice(at, at + features.shape[0])
        grad = exact_left(nt, v_s[rows, :], back_parts)
        part = split2(feature_back(features, grad))
        grad_map = grad_map + wide_exact_left(tn, k_s[rows, :T], part)
        at += features.shape[0]
    tail = jnp.concatenate(
        [
            backn[:, :T],
            backn[:, T:],
            jnp.broadcast_to(pos_ref[0:1, 0:1].astype(F32), (1, T)),
            jnp.zeros((1, T), F32),
        ],
        axis=0,
    )
    for piece in range(32):
        payload_ref[piece, KMAP_ROW:PIECE, :] = jnp.concatenate(
            [grad_map[piece * 4 : piece * 4 + 4, :], tail], axis=0
        )


def query_kernel(dlogit_ref, inner_ref, gn_ref, qmap_ref, gq_ref, gv_ref):
    for h in range(qmap_ref.shape[0]):
        at = slice(h * T, h * T + T)
        gq_ref[:, at] = product(nt, split2(dlogit_ref[at, :]), split2(qmap_ref[h]))
    gv_ref[...] = product(tn, split2(inner_ref[...]), split2(gn_ref[...]))


def middle_kernel(me_ref, got_ref, out_ref, norms_ref, state_s):
    pieces = got_ref.shape[0]
    total = got_ref[0]
    for i in range(1, pieces):
        total = total + got_ref[i]
    qmap, kmap = total[0:STATE_ROW, :], total[KMAP_ROW:NORM_ROW, :]
    squares = jnp.sum(qmap * qmap) + jnp.sum(kmap * kmap)
    parts = [part.astype(F32) for part in split3(jnp.full((1, T), squares, F32))]
    tail = jnp.concatenate([kmap] + parts + [jnp.zeros((1, T), F32)], axis=0).astype(BF16)
    qmap = qmap.astype(BF16)
    for j in range(pieces):
        out_ref[j, 0:HIGH_ROW, :] = qmap
        out_ref[j, KEY_ROW:REPLY, :] = tail
    sender = lax.broadcasted_iota(jnp.int32, (pieces, T), 0)
    target = lax.broadcasted_iota(jnp.int32, (pieces, T), 1)
    first = (sender * T).astype(F32) - got_ref[:, INFO_ROW, :]
    links = (sender > target) & (first <= (target * T + (T - 1)).astype(F32))
    reach = links.astype(F32)[:, :pieces].astype(BF16)
    for i in range(8):
        state_s[:, i, :] = exact_left(tn, reach, split3(got_ref[:, STATE_ROW + i, :]))
    high, low = split2(state_s[...])
    out_ref[:, HIGH_ROW:LOW_ROW, :] = high
    out_ref[:, LOW_ROW:KEY_ROW, :] = low
    me = me_ref[0]
    mine = (sender > me) & (first <= (me * T + (T - 1)).astype(F32))
    for half in range(2):
        norms_ref[0:1, half * T : half * T + T] = jnp.sum(
            jnp.where(mine, got_ref[:, NORM_ROW + half, :], 0.0), axis=0, keepdims=True
        )


def last_kernel(pos_ref, got_ref, norms_ref, v_ref, kmap_ref, phi_ref, gkphi_ref, gv_ref, gk_ref, gvo_ref):
    _, start = positions_of(pos_ref)
    last_start = float(T - 1) - pos_ref[0:1, T - 1 : T].astype(F32)
    keeping = (start == last_start).astype(F32)
    pieces = got_ref.shape[0]
    back = [
        jnp.concatenate([got_ref[r, at : at + 8, :] for r in range(pieces)], axis=0)
        for at in (HIGH_ROW, LOW_ROW)
    ]
    phi = phi_ref[...]
    own_v = v_ref[...]
    grad = gkphi_ref[...] + keeping * (exact_left(nt, own_v, back) + norms_ref[...])
    gvo_ref[...] = gv_ref[...] + keeping * product(nn, split2(phi), back)
    gk_ref[...] = product(nt, split2(feature_back(phi, grad)), split2(kmap_ref[0]))


def squares_kernel(tail_ref, out_ref):
    total = jnp.sum(tail_ref[:, KEY_ROW:REPLY, :].astype(F32), axis=0)
    total = jnp.sum(total[SQUARE_ROW - KEY_ROW : SQUARE_ROW - KEY_ROW + 3, :], axis=0)
    out_ref[...] = jnp.broadcast_to(total.reshape(1, 1, T), out_ref.shape)


def scale_kernel(limit, got_ref, squares_ref, qmap_ref, kmap_ref):
    pieces = got_ref.shape[0]
    squared = jnp.sum(squares_ref[:, 0, :], axis=0, keepdims=True)
    factor = jnp.minimum(1.0, limit / (jnp.sqrt(squared) + EPSILON))
    for piece in range(pieces):
        rows = slice(piece % 4 * 32, piece % 4 * 32 + 32)
        qmap_ref[piece // 4, rows, :] = factor * got_ref[piece, 0:HIGH_ROW, :].astype(F32)
        tail = got_ref[piece, KEY_ROW:REPLY, :].astype(F32)
        kmap_ref[0, piece * 4 : piece * 4 + 4, :] = factor * tail[0 : SQUARE_ROW - KEY_ROW, :]


def call(body, name, ins, outs, scratch=(), limit=32):
    return pl.pallas_call(
        body,
        in_specs=[pl.BlockSpec(memory_space=space) for space in ins],
        out_specs=[pl.BlockSpec(memory_space=pltpu.VMEM)] * len(outs),
        out_shape=[
            out if isinstance(out, jax.ShapeDtypeStruct) else jax.ShapeDtypeStruct(out, F32)
            for out in outs
        ],
        scratch_shapes=list(scratch),
        compiler_params=pltpu.CompilerParams(vmem_limit_bytes=limit << 20),
        name=name,
    )


def joined(a, b):
    return lax.pad(a, jnp.zeros((), a.dtype), ((0, b.shape[0], 0), (0, 0, 0))) + lax.pad(
        b, jnp.zeros((), b.dtype), ((a.shape[0], 0, 0), (0, 0, 0))
    )


def on_device(queries, key_vectors, value_vectors, positions, query_map, key_map):
    group = query_map.shape[0]
    pieces = lax.axis_size("seq")
    heads = lax.axis_size("head")
    rows = group * T
    me = lax.axis_index("seq").astype(jnp.int32).reshape(1)
    pos = positions.reshape(1, T)
    kv = joined(key_vectors, value_vectors)
    V = pltpu.VMEM

    def shift(x, k):
        return lax.ppermute(x, "seq", [(i, (i + k) % pieces) for i in range(pieces)])

    def part_of(name, arrays, places):
        size = T * sum(len(held) for held in places)
        return call(
            functools.partial(part_kernel, places),
            name,
            [V] * (3 + len(arrays)),
            [(size, 2 * T), (2 * T, 2 * T), (rows, T), (rows, T), (rows, T)],
            [V((size, 2 * T), BF16), V((size, 2 * T), BF16)],
            24,
        )(pos, queries, key_map, *arrays)

    b4, b8, b1, b7 = (shift(kv, k) for k in (4, 8, 1, 7))
    phi, inner, own = call(
        local_kernel, "local_features", [V] * 5, [(rows, 2 * T), (rows, T), (T, 2 * T)]
    )(pos, queries, key_vectors, query_map, key_map)
    near = jnp.concatenate([b4, b8, b1, b7], axis=0)
    near, b4, b1, b7 = lax.optimization_barrier((near, b4, b1, b7))
    far = shift(near, 8)
    n1 = shift(jnp.concatenate([b1, b4], axis=0), 1)
    n2 = shift(jnp.concatenate([b4, b7], axis=0), -1)
    early = list(part_of("early_keys", [near], [(4, 8, 1, 7)]))
    n1, n2, far, early[1] = lax.optimization_barrier((n1, n2, far, early[1]))
    f1, f2 = shift(n1, 8), shift(n2, 8)
    middle = part_of("middle_keys", [far, n1, n2], [(12, 16, 9, 15), (2, 5), (3, 6)])
    arrays = [near, far, n1, n2, f1, f2, kv]
    places = [(4, 8, 1, 7), (12, 16, 9, 15), (2, 5), (3, 6), (10, 13), (11, 14), (0,)]
    payload, dlogit, grad_numer, gkphi = call(
        functools.partial(main_kernel, places, 2),
        "attention_transfer",
        [V] * (6 + len(arrays) + 10),
        [(pieces, PIECE, T), (rows, T), (rows, T), (T, 2 * T)],
        [V((KEYS, 2 * T), BF16), V((KEYS, 2 * T), BF16)],
        32,
    )(pos, queries, key_map, phi, inner, own, *arrays, *early, *middle)
    gathered = lax.all_to_all(payload, "seq", 0, 0)
    grad_queries, near_values = call(
        query_kernel, "query_gradients", [V] * 4, [(T, rows), (T, T)]
    )(dlogit, inner, grad_numer, query_map)
    reduced, norms = call(
        middle_kernel,
        "sum_pieces",
        [pltpu.SMEM, V],
        [jax.ShapeDtypeStruct((pieces, REPLY, T), BF16), (1, 2 * T)],
        [V((pieces, 8, T), F32)],
    )(me, gathered)
    back = lax.all_to_all(reduced, "seq", 0, 0)
    squares = call(squares_kernel, "head_squares", [V], [(heads, 8, T)])(back)[0]
    squares = lax.all_to_all(squares, "head", 0, 0)
    grad_keys, grad_values = call(last_kernel, "key_gradients", [V] * 8, [(T, T), (T, T)])(
        pos, back, norms, value_vectors, key_map, own, gkphi, near_values
    )
    clip_limit = 0.25 * math.sqrt((group + 1) * heads * T * T)
    query_map_grad, key_map_grad = call(
        functools.partial(scale_kernel, clip_limit),
        "clip_maps",
        [V] * 2,
        [(group, T, T), (1, T, T)],
    )(back, squares)
    return (grad_queries, grad_keys, grad_values, query_map_grad, key_map_grad)


def solution(mesh):
    placed = (
        P("seq", "head"),
        P("seq", "head"),
        P("seq", "head"),
        P("seq"),
        P("head", None, None),
        P("head", None, None),
    )
    return jax.shard_map(
        on_device,
        mesh=mesh,
        in_specs=placed,
        out_specs=(
            P("seq", "head"),
            P("seq", "head"),
            P("seq", "head"),
            P("head", None, None),
            P("head", None, None),
        ),
        check_vma=False,
    )
```

```python
import functools
import math

import jax
import jax.numpy as jnp
from jax import lax
from jax.experimental import pallas as pl
from jax.experimental.pallas import tpu as pltpu
from jax.sharding import PartitionSpec as P

F32 = jnp.float32
BF16 = jnp.bfloat16
NEGATIVE = -1e30
EPSILON = 1e-06
T = 128
WINDOW = 16
KEYS = (WINDOW + 1) * T
TEACHER = 512
PIECE = 48
STATE_ROW, KMAP_ROW, NORM_ROW, INFO_ROW = 32, 40, 44, 46
REPLY = 56
HIGH_ROW, LOW_ROW, KEY_ROW, SQUARE_ROW = 32, 40, 48, 52


def nn(a, b):
    return lax.dot_general(a, b, (((1,), (0,)), ((), ())), preferred_element_type=F32)


def nt(a, b):
    return lax.dot_general(a, b, (((1,), (1,)), ((), ())), preferred_element_type=F32)


def tn(a, b):
    return lax.dot_general(a, b, (((0,), (0,)), ((), ())), preferred_element_type=F32)


def split2(x):
    high = x.astype(BF16)
    return high, (x - high.astype(F32)).astype(BF16)


def split3(x):
    high = x.astype(BF16)
    rest = x - high.astype(F32)
    middle = rest.astype(BF16)
    return high, middle, (rest - middle.astype(F32)).astype(BF16)


def product(form, a, b):
    return form(a[0], b[0]) + (form(a[0], b[1]) + form(a[1], b[0]))


def exact_left(form, a, parts):
    total = form(a, parts[-1])
    for part in parts[-2::-1]:
        total = total + form(a, part)
    return total


def exact_right(form, parts, b):
    return form(parts[0], b) + form(parts[1], b)


def deep(parts):
    return jnp.concatenate(parts, axis=1)


def deep_exact_right(form, parts, b):
    return form(deep(parts), jnp.concatenate([b, b], axis=0 if form is nn else 1))


def deep_product(form, a, b):
    return deep_exact_right(form, a, b[0]) + form(a[0], b[1])


def wide_exact_left(form, a, parts):
    both = form(a, deep(parts))
    return both[:, :T] + both[:, T:]


def row_sums(x):
    return nn(deep(split2(x)), jnp.ones((2 * T, T), BF16))


def half_sums(x):
    i = lax.broadcasted_iota(jnp.int32, (2 * T, 2 * T), 0) < T
    j = lax.broadcasted_iota(jnp.int32, (2 * T, 2 * T), 1) < T
    return exact_right(nn, split2(x), (i == j).astype(F32).astype(BF16))


def map_of(weights):
    high, middle, low = split3(weights)
    rest = jnp.concatenate([middle, jnp.zeros_like(middle)], axis=1)
    return jnp.concatenate([deep([high, low]), rest], axis=0)


def logits_of(x, matrix):
    both = nn(deep([x, x]), matrix)
    return both[:, :T] + both[:, T:]


def feature_map(logits):
    upper = jnp.exp(logits - jnp.max(logits, axis=-1, keepdims=True))
    lower = jnp.exp(jnp.min(logits, axis=-1, keepdims=True) - logits)
    both = deep([upper, lower])
    return both / half_sums(both)


def feature_back(phi, grad):
    both = phi * (grad - half_sums(phi * grad))
    return both[:, :T] - both[:, T:]


def column_of(row):
    i = lax.broadcasted_iota(jnp.int32, (T, T), 0)
    j = lax.broadcasted_iota(jnp.int32, (T, T), 1)
    return jnp.sum(jnp.where(i == j, row, 0.0), axis=1, keepdims=True)


def stacked(ref):
    return jnp.concatenate([ref[:, h * T : h * T + T] for h in range(ref.shape[1] // T)], axis=0)


def every_head(x, heads):
    return jnp.concatenate([x] * heads, axis=0)


def positions_of(pos_ref):
    row = lax.broadcasted_iota(jnp.int32, (T, 1), 0).astype(F32)
    return row, row - column_of(pos_ref[...].astype(F32))


def local_kernel(pos_ref, q_ref, k_ref, qmap_ref, kmap_ref, phi_ref, inner_ref, own_ref):
    heads = qmap_ref.shape[0]
    row, start = positions_of(pos_ref)
    key = lax.broadcasted_iota(jnp.int32, (T, T), 1).astype(F32)
    seen = every_head(((key <= row) & (key >= start)).astype(F32), heads)
    own = feature_map(logits_of(k_ref[...], map_of(kmap_ref[0])))
    own_ref[...] = own
    logits = jnp.concatenate(
        [logits_of(q_ref[:, h * T : h * T + T], map_of(qmap_ref[h])) for h in range(heads)],
        axis=0,
    )
    phi = feature_map(logits)
    phi_ref[...] = phi
    inner_ref[...] = product(nt, split2(phi), split2(own)) * seen


def hold_keys(arrays, places, pos_ref, k_s, v_s):
    row = lax.broadcasted_iota(jnp.int32, (T, 1), 0).astype(F32)
    entry = -pos_ref[0:1, 0:1].astype(F32)
    lane = lax.broadcasted_iota(jnp.int32, (T, T), 1)
    at = 0
    keys = []
    for ref, held in zip(arrays, places):
        for slot, block in enumerate(held):
            k_s[at : at + T, :T] = ref[slot * 2 * T : slot * 2 * T + T, :]
            v_s[at : at + T, :T] = ref[slot * 2 * T + T : slot * 2 * T + 2 * T, :]
            key = row - float(block * T)
            hidden = jnp.where(key >= entry, 0.0, NEGATIVE)
            hidden = jnp.where(lane == 0, NEGATIVE, jnp.where(lane == 1, hidden, 0.0))
            k_s[at : at + T, T:] = (hidden if block else jnp.zeros((T, T), F32)).astype(BF16)
            keys.append(key)
            at += T
    v_s[:, T:] = jnp.ones(v_s[:, T:].shape, BF16)
    return keys, entry


def key_features(rows, keys, entry, matrix, k_s, v_s):
    features = feature_map(logits_of(k_s[rows, :T], matrix))
    features = jnp.where(jnp.concatenate(keys, axis=0) >= entry, features, 0.0)
    return features, exact_right(tn, split2(features), v_s[rows, :])


def asking(q_ref, crossing):
    heads = q_ref.shape[1] // T
    lane = lax.broadcasted_iota(jnp.int32, (T, T), 1)
    hider = jnp.where(lane == 0, 1.0 - crossing, jnp.where(lane == 1, 1.0, 0.0)).astype(BF16)
    return deep([stacked(q_ref), every_head(hider, heads)])


RATE = math.log2(math.e) / math.sqrt(T)


def part_kernel(places, pos_ref, q_ref, kmap_ref, *rest):
    count = len(places)
    phi_ref, state_ref, top_ref, total_ref, sum_ref = rest[count : count + 5]
    k_s, v_s = rest[count + 5 :]
    _, start = positions_of(pos_ref)
    keys, entry = hold_keys(rest[:count], places, pos_ref, k_s, v_s)
    phi_ref[...], state_ref[...] = key_features(
        slice(None), keys, entry, map_of(kmap_ref[0]), k_s, v_s
    )
    queries = asking(q_ref, (start < 0.0).astype(F32))
    for at in range(0, queries.shape[0], TEACHER):
        rows = slice(at, at + TEACHER)
        scores = nt(queries[rows, :], k_s[...])
        top = jnp.max(scores, axis=-1, keepdims=True)
        weights = jnp.exp2((scores - top) * RATE)
        total = jnp.sum(weights, axis=-1, keepdims=True)
        sum_ref[rows, :] = nn(weights.astype(BF16), v_s[:, :T])
        top_ref[rows, :] = jnp.broadcast_to(top, (TEACHER, T))
        total_ref[rows, :] = jnp.broadcast_to(total, (TEACHER, T))


def main_kernel(places, parts, pos_ref, q_ref, kmap_ref, phi_ref, inner_ref, own_ref, *rest):
    count = len(places)
    blocks = rest[:count]
    done = [rest[count + 5 * i : count + 5 * i + 5] for i in range(parts)]
    rest = rest[count + 5 * parts :]
    payload_ref, dlogit_ref, gn_ref, gkphi_ref, k_s, v_s = rest
    heads = q_ref.shape[1] // T
    row, start = positions_of(pos_ref)
    crossing = (start < 0.0).astype(F32)
    keys, entry = hold_keys(blocks, places, pos_ref, k_s, v_s)
    first = sum(part[0].shape[0] for part in done)
    late, state = key_features(
        slice(first, WINDOW * T), keys[first // T : WINDOW], entry, map_of(kmap_ref[0]), k_s, v_s
    )
    for part in done:
        state = state + part[1][...]
    norms = jnp.transpose(state[:, T:])[0:1, :]
    state = split2(state)

    own_key = lax.broadcasted_iota(jnp.int32, (T, T), 1).astype(F32)
    visible = (own_key <= row) & (own_key >= start)
    seen = every_head(visible.astype(F32), heads)
    bias = every_head(jnp.where(visible, 0.0, NEGATIVE), heads)
    cross = every_head(jnp.broadcast_to(crossing, (T, T)), heads)
    queries = asking(q_ref, crossing)
    own_v = v_s[WINDOW * T :, :]
    teachers = []
    for at in range(0, heads * T, TEACHER):
        rows = slice(at, at + TEACHER)
        scores = nt(queries[rows, :], k_s[first:, :])
        near = scores[:, WINDOW * T - first :] + bias[rows, :]
        far = scores[:, : WINDOW * T - first]
        top = jnp.maximum(
            jnp.max(near, axis=-1, keepdims=True), jnp.max(far, axis=-1, keepdims=True)
        )
        top = jnp.broadcast_to(top, (TEACHER, T))
        for part in done:
            top = jnp.maximum(top, part[2][rows, :])
        near = jnp.exp2((near - top) * RATE)
        far = jnp.exp2((far - top[:, 0:1]) * RATE)
        total = jnp.sum(near, axis=-1, keepdims=True) + jnp.sum(far, axis=-1, keepdims=True)
        summed = nn(deep([far, near]).astype(BF16), v_s[first:, :T])
        for part in done:
            fading = jnp.exp2((part[2][rows, :] - top) * RATE)
            total = total + fading * part[3][rows, :]
            summed = summed + fading * part[4][rows, :]
        teachers.append(summed / total)
    teacher = jnp.concatenate(teachers, axis=0)

    own = own_ref[...]
    own_phi = split2(own)
    phi = phi_ref[...]
    phi_parts = split2(phi)
    near = deep_exact_right(nn, split2(inner_ref[...]), own_v)
    far = product(nn, phi_parts, state)
    inverse = 1.0 / (near[:, T:] + cross * far[:, T:])
    outputs = (near[:, :T] + cross * far[:, :T]) * inverse
    error = outputs - teacher

    grad_numer = error * inverse
    grad_denom = -row_sums(error * outputs) * inverse
    gn_ref[...] = grad_numer
    far_numer = cross * grad_numer
    far_denom = cross * grad_denom
    mixing = (deep_exact_right(nt, split2(grad_numer), own_v[:, :T]) + grad_denom) * seen
    mixing_parts = split2(mixing)
    near = deep_product(nn, mixing_parts, own_phi)
    far = deep_product(nt, split2(far_numer), [part[:, :T] for part in state])
    grad_phi = jnp.concatenate(
        [
            near[:, :T] + far[:, :T] + far_denom * norms[:, :T],
            near[:, T:] + far[:, T:] + far_denom * norms[:, T:],
        ],
        axis=1,
    )
    back = product(tn, phi_parts, split2(jnp.concatenate([far_numer, far_denom], axis=1)))
    backn = jnp.transpose(back[:, T:])[0:1, :]
    gkphi = product(tn, mixing_parts, phi_parts)
    gkphi_ref[...] = gkphi
    dlogit = feature_back(phi, grad_phi)
    dlogit_ref[...] = dlogit
    dlogit_parts = split2(dlogit)
    for h in range(heads):
        at = slice(h * T, h * T + T)
        grad_map = wide_exact_left(tn, q_ref[:, at], [part[at, :] for part in dlogit_parts])
        for quarter in range(4):
            payload_ref[4 * h + quarter, 0:STATE_ROW, :] = grad_map[
                quarter * 32 : quarter * 32 + 32, :
            ]
    for piece in range(32):
        payload_ref[piece, STATE_ROW : STATE_ROW + 8, :] = back[piece * 8 : piece * 8 + 8, :T]

    part = split2(feature_back(own, gkphi))
    grad_map = wide_exact_left(tn, k_s[WINDOW * T :, :T], part)
    back_parts = split2(jnp.concatenate([back[:, :T], back[:, T:] * (1.0 / T)], axis=1))
    at = 0
    for features in [part[0][...] for part in done] + [late]:
        rows = slice(at, at + features.shape[0])
        grad = exact_left(nt, v_s[rows, :], back_parts)
        part = split2(feature_back(features, grad))
        grad_map = grad_map + wide_exact_left(tn, k_s[rows, :T], part)
        at += features.shape[0]
    tail = jnp.concatenate(
        [
            backn[:, :T],
            backn[:, T:],
            jnp.broadcast_to(pos_ref[0:1, 0:1].astype(F32), (1, T)),
            jnp.zeros((1, T), F32),
        ],
        axis=0,
    )
    for piece in range(32):
        payload_ref[piece, KMAP_ROW:PIECE, :] = jnp.concatenate(
            [grad_map[piece * 4 : piece * 4 + 4, :], tail], axis=0
        )


def query_kernel(dlogit_ref, inner_ref, gn_ref, qmap_ref, gq_ref, gv_ref):
    for h in range(qmap_ref.shape[0]):
        at = slice(h * T, h * T + T)
        gq_ref[:, at] = product(nt, split2(dlogit_ref[at, :]), split2(qmap_ref[h]))
    gv_ref[...] = product(tn, split2(inner_ref[...]), split2(gn_ref[...]))


def middle_kernel(me_ref, got_ref, out_ref, norms_ref, state_s):
    pieces = got_ref.shape[0]
    total = got_ref[0]
    for i in range(1, pieces):
        total = total + got_ref[i]
    qmap, kmap = total[0:STATE_ROW, :], total[KMAP_ROW:NORM_ROW, :]
    squares = jnp.sum(qmap * qmap) + jnp.sum(kmap * kmap)
    parts = [part.astype(F32) for part in split3(jnp.full((1, T), squares, F32))]
    tail = jnp.concatenate([kmap] + parts + [jnp.zeros((1, T), F32)], axis=0).astype(BF16)
    qmap = qmap.astype(BF16)
    for j in range(pieces):
        out_ref[j, 0:HIGH_ROW, :] = qmap
        out_ref[j, KEY_ROW:REPLY, :] = tail
    sender = lax.broadcasted_iota(jnp.int32, (pieces, T), 0)
    target = lax.broadcasted_iota(jnp.int32, (pieces, T), 1)
    first = (sender * T).astype(F32) - got_ref[:, INFO_ROW, :]
    links = (sender > target) & (first <= (target * T + (T - 1)).astype(F32))
    reach = links.astype(F32)[:, :pieces].astype(BF16)
    for i in range(8):
        state_s[:, i, :] = exact_left(tn, reach, split3(got_ref[:, STATE_ROW + i, :]))
    high, low = split2(state_s[...])
    out_ref[:, HIGH_ROW:LOW_ROW, :] = high
    out_ref[:, LOW_ROW:KEY_ROW, :] = low
    me = me_ref[0]
    mine = (sender > me) & (first <= (me * T + (T - 1)).astype(F32))
    for half in range(2):
        norms_ref[0:1, half * T : half * T + T] = jnp.sum(
            jnp.where(mine, got_ref[:, NORM_ROW + half, :], 0.0), axis=0, keepdims=True
        )


def last_kernel(pos_ref, got_ref, norms_ref, v_ref, kmap_ref, phi_ref, gkphi_ref, gv_ref, gk_ref, gvo_ref):
    _, start = positions_of(pos_ref)
    last_start = float(T - 1) - pos_ref[0:1, T - 1 : T].astype(F32)
    keeping = (start == last_start).astype(F32)
    pieces = got_ref.shape[0]
    back = [
        jnp.concatenate([got_ref[r, at : at + 8, :] for r in range(pieces)], axis=0)
        for at in (HIGH_ROW, LOW_ROW)
    ]
    phi = phi_ref[...]
    own_v = v_ref[...]
    grad = gkphi_ref[...] + keeping * (exact_left(nt, own_v, back) + norms_ref[...])
    gvo_ref[...] = gv_ref[...] + keeping * product(nn, split2(phi), back)
    gk_ref[...] = product(nt, split2(feature_back(phi, grad)), split2(kmap_ref[0]))


def squares_kernel(tail_ref, out_ref):
    total = jnp.sum(tail_ref[:, KEY_ROW:REPLY, :].astype(F32), axis=0)
    total = jnp.sum(total[SQUARE_ROW - KEY_ROW : SQUARE_ROW - KEY_ROW + 3, :], axis=0)
    out_ref[...] = jnp.broadcast_to(total.reshape(1, 1, T), out_ref.shape)


def scale_kernel(limit, got_ref, squares_ref, qmap_ref, kmap_ref):
    pieces = got_ref.shape[0]
    squared = jnp.sum(squares_ref[:, 0, :], axis=0, keepdims=True)
    factor = jnp.minimum(1.0, limit / (jnp.sqrt(squared) + EPSILON))
    for piece in range(pieces):
        rows = slice(piece % 4 * 32, piece % 4 * 32 + 32)
        qmap_ref[piece // 4, rows, :] = factor * got_ref[piece, 0:HIGH_ROW, :].astype(F32)
        tail = got_ref[piece, KEY_ROW:REPLY, :].astype(F32)
        kmap_ref[0, piece * 4 : piece * 4 + 4, :] = factor * tail[0 : SQUARE_ROW - KEY_ROW, :]


def call(body, name, ins, outs, scratch=(), limit=32):
    return pl.pallas_call(
        body,
        in_specs=[pl.BlockSpec(memory_space=space) for space in ins],
        out_specs=[pl.BlockSpec(memory_space=pltpu.VMEM)] * len(outs),
        out_shape=[
            out if isinstance(out, jax.ShapeDtypeStruct) else jax.ShapeDtypeStruct(out, F32)
            for out in outs
        ],
        scratch_shapes=list(scratch),
        compiler_params=pltpu.CompilerParams(vmem_limit_bytes=limit << 20),
        name=name,
    )


def joined(a, b):
    return lax.pad(a, jnp.zeros((), a.dtype), ((0, b.shape[0], 0), (0, 0, 0))) + lax.pad(
        b, jnp.zeros((), b.dtype), ((a.shape[0], 0, 0), (0, 0, 0))
    )


def on_device(queries, key_vectors, value_vectors, positions, query_map, key_map):
    group = query_map.shape[0]
    pieces = lax.axis_size("seq")
    heads = lax.axis_size("head")
    rows = group * T
    me = lax.axis_index("seq").astype(jnp.int32).reshape(1)
    pos = positions.reshape(1, T)
    kv = joined(key_vectors, value_vectors)
    V = pltpu.VMEM

    def shift(x, k):
        return lax.ppermute(x, "seq", [(i, (i + k) % pieces) for i in range(pieces)])

    def part_of(name, arrays, places):
        size = T * sum(len(held) for held in places)
        return call(
            functools.partial(part_kernel, places),
            name,
            [V] * (3 + len(arrays)),
            [(size, 2 * T), (2 * T, 2 * T), (rows, T), (rows, T), (rows, T)],
            [V((size, 2 * T), BF16), V((size, 2 * T), BF16)],
            24,
        )(pos, queries, key_map, *arrays)

    b4, b8, b1, b7 = (shift(kv, k) for k in (4, 8, 1, 7))
    phi, inner, own = call(
        local_kernel, "local_features", [V] * 5, [(rows, 2 * T), (rows, T), (T, 2 * T)]
    )(pos, queries, key_vectors, query_map, key_map)
    b4, b8, b1, b7 = lax.optimization_barrier((b4, b8, b1, b7))
    near = jnp.concatenate([b4, b8, b1, b7], axis=0)
    near, b4, b1, b7 = lax.optimization_barrier((near, b4, b1, b7))
    far = shift(near, 8)
    n1 = shift(jnp.concatenate([b1, b4], axis=0), 1)
    n2 = shift(jnp.concatenate([b4, b7], axis=0), -1)
    early = list(part_of("early_keys", [near], [(4, 8, 1, 7)]))
    n1, n2, far, early[1] = lax.optimization_barrier((n1, n2, far, early[1]))
    f1, f2 = shift(n1, 8), shift(n2, 8)
    middle = part_of("middle_keys", [far, n1, n2], [(12, 16, 9, 15), (2, 5), (3, 6)])
    arrays = [near, far, n1, n2, f1, f2, kv]
    places = [(4, 8, 1, 7), (12, 16, 9, 15), (2, 5), (3, 6), (10, 13), (11, 14), (0,)]
    payload, dlogit, grad_numer, gkphi = call(
        functools.partial(main_kernel, places, 2),
        "attention_transfer",
        [V] * (6 + len(arrays) + 10),
        [(pieces, PIECE, T), (rows, T), (rows, T), (T, 2 * T)],
        [V((KEYS, 2 * T), BF16), V((KEYS, 2 * T), BF16)],
        32,
    )(pos, queries, key_map, phi, inner, own, *arrays, *early, *middle)
    gathered = lax.all_to_all(payload, "seq", 0, 0)
    grad_queries, near_values = call(
        query_kernel, "query_gradients", [V] * 4, [(T, rows), (T, T)]
    )(dlogit, inner, grad_numer, query_map)
    reduced, norms = call(
        middle_kernel,
        "sum_pieces",
        [pltpu.SMEM, V],
        [jax.ShapeDtypeStruct((pieces, REPLY, T), BF16), (1, 2 * T)],
        [V((pieces, 8, T), F32)],
    )(me, gathered)
    back = lax.all_to_all(reduced, "seq", 0, 0)
    squares = call(squares_kernel, "head_squares", [V], [(heads, 8, T)])(back)[0]
    squares = lax.all_to_all(squares, "head", 0, 0)
    grad_keys, grad_values = call(last_kernel, "key_gradients", [V] * 8, [(T, T), (T, T)])(
        pos, back, norms, value_vectors, key_map, own, gkphi, near_values
    )
    clip_limit = 0.25 * math.sqrt((group + 1) * heads * T * T)
    query_map_grad, key_map_grad = call(
        functools.partial(scale_kernel, clip_limit),
        "clip_maps",
        [V] * 2,
        [(group, T, T), (1, T, T)],
    )(back, squares)
    return (grad_queries, grad_keys, grad_values, query_map_grad, key_map_grad)


def solution(mesh):
    placed = (
        P("seq", "head"),
        P("seq", "head"),
        P("seq", "head"),
        P("seq"),
        P("head", None, None),
        P("head", None, None),
    )
    return jax.shard_map(
        on_device,
        mesh=mesh,
        in_specs=placed,
        out_specs=(
            P("seq", "head"),
            P("seq", "head"),
            P("seq", "head"),
            P("head", None, None),
            P("head", None, None),
        ),
        check_vma=False,
    )
```

```python
import functools
import math

import jax
import jax.numpy as jnp
from jax import lax
from jax.experimental import pallas as pl
from jax.experimental.pallas import tpu as pltpu
from jax.sharding import PartitionSpec as P

F32 = jnp.float32
BF16 = jnp.bfloat16
NEGATIVE = -1e30
EPSILON = 1e-06
T = 128
WINDOW = 16
KEYS = (WINDOW + 1) * T
TEACHER = 512
PIECE = 48
STATE_ROW, KMAP_ROW, NORM_ROW, INFO_ROW = 32, 40, 44, 46
REPLY = 56
HIGH_ROW, LOW_ROW, KEY_ROW, SQUARE_ROW = 32, 40, 48, 52


def nn(a, b):
    return lax.dot_general(a, b, (((1,), (0,)), ((), ())), preferred_element_type=F32)


def nt(a, b):
    return lax.dot_general(a, b, (((1,), (1,)), ((), ())), preferred_element_type=F32)


def tn(a, b):
    return lax.dot_general(a, b, (((0,), (0,)), ((), ())), preferred_element_type=F32)


def split2(x):
    high = x.astype(BF16)
    return high, (x - high.astype(F32)).astype(BF16)


def split3(x):
    high = x.astype(BF16)
    rest = x - high.astype(F32)
    middle = rest.astype(BF16)
    return high, middle, (rest - middle.astype(F32)).astype(BF16)


def product(form, a, b):
    return form(a[0], b[0]) + (form(a[0], b[1]) + form(a[1], b[0]))


def exact_left(form, a, parts):
    total = form(a, parts[-1])
    for part in parts[-2::-1]:
        total = total + form(a, part)
    return total


def exact_right(form, parts, b):
    return form(parts[0], b) + form(parts[1], b)


def deep(parts):
    return jnp.concatenate(parts, axis=1)


def deep_exact_right(form, parts, b):
    return form(deep(parts), jnp.concatenate([b, b], axis=0 if form is nn else 1))


def deep_product(form, a, b):
    return deep_exact_right(form, a, b[0]) + form(a[0], b[1])


def wide_exact_left(form, a, parts):
    both = form(a, deep(parts))
    return both[:, :T] + both[:, T:]


def row_sums(x):
    return nn(deep(split2(x)), jnp.ones((2 * T, T), BF16))


def half_sums(x):
    i = lax.broadcasted_iota(jnp.int32, (2 * T, 2 * T), 0) < T
    j = lax.broadcasted_iota(jnp.int32, (2 * T, 2 * T), 1) < T
    return exact_right(nn, split2(x), (i == j).astype(F32).astype(BF16))


def map_of(weights):
    high, middle, low = split3(weights)
    rest = jnp.concatenate([middle, jnp.zeros_like(middle)], axis=1)
    return jnp.concatenate([deep([high, low]), rest], axis=0)


def logits_of(x, matrix):
    both = nn(deep([x, x]), matrix)
    return both[:, :T] + both[:, T:]


def feature_map(logits):
    upper = jnp.exp(logits - jnp.max(logits, axis=-1, keepdims=True))
    lower = jnp.exp(jnp.min(logits, axis=-1, keepdims=True) - logits)
    both = deep([upper, lower])
    return both / half_sums(both)


def feature_back(phi, grad):
    both = phi * (grad - half_sums(phi * grad))
    return both[:, :T] - both[:, T:]


def column_of(row):
    i = lax.broadcasted_iota(jnp.int32, (T, T), 0)
    j = lax.broadcasted_iota(jnp.int32, (T, T), 1)
    return jnp.sum(jnp.where(i == j, row, 0.0), axis=1, keepdims=True)


def stacked(ref):
    return jnp.concatenate([ref[:, h * T : h * T + T] for h in range(ref.shape[1] // T)], axis=0)


def every_head(x, heads):
    return jnp.concatenate([x] * heads, axis=0)


def positions_of(pos_ref):
    row = lax.broadcasted_iota(jnp.int32, (T, 1), 0).astype(F32)
    return row, row - column_of(pos_ref[...].astype(F32))


def local_kernel(pos_ref, q_ref, k_ref, qmap_ref, kmap_ref, phi_ref, inner_ref, own_ref):
    heads = qmap_ref.shape[0]
    row, start = positions_of(pos_ref)
    key = lax.broadcasted_iota(jnp.int32, (T, T), 1).astype(F32)
    seen = every_head(((key <= row) & (key >= start)).astype(F32), heads)
    own = feature_map(logits_of(k_ref[...], map_of(kmap_ref[0])))
    own_ref[...] = own
    logits = jnp.concatenate(
        [logits_of(q_ref[:, h * T : h * T + T], map_of(qmap_ref[h])) for h in range(heads)],
        axis=0,
    )
    phi = feature_map(logits)
    phi_ref[...] = phi
    inner_ref[...] = product(nt, split2(phi), split2(own)) * seen


def hold_keys(arrays, places, pos_ref, k_s, v_s):
    row = lax.broadcasted_iota(jnp.int32, (T, 1), 0).astype(F32)
    entry = -pos_ref[0:1, 0:1].astype(F32)
    lane = lax.broadcasted_iota(jnp.int32, (T, T), 1)
    at = 0
    keys = []
    for ref, held in zip(arrays, places):
        for slot, block in enumerate(held):
            k_s[at : at + T, :T] = ref[slot * 2 * T : slot * 2 * T + T, :]
            v_s[at : at + T, :T] = ref[slot * 2 * T + T : slot * 2 * T + 2 * T, :]
            key = row - float(block * T)
            hidden = jnp.where(key >= entry, 0.0, NEGATIVE)
            hidden = jnp.where(lane == 0, NEGATIVE, jnp.where(lane == 1, hidden, 0.0))
            k_s[at : at + T, T:] = (hidden if block else jnp.zeros((T, T), F32)).astype(BF16)
            keys.append(key)
            at += T
    v_s[:, T:] = jnp.ones(v_s[:, T:].shape, BF16)
    return keys, entry


def key_features(rows, keys, entry, matrix, k_s, v_s):
    features = feature_map(logits_of(k_s[rows, :T], matrix))
    features = jnp.where(jnp.concatenate(keys, axis=0) >= entry, features, 0.0)
    return features, exact_right(tn, split2(features), v_s[rows, :])


def asking(q_ref, crossing):
    heads = q_ref.shape[1] // T
    lane = lax.broadcasted_iota(jnp.int32, (T, T), 1)
    hider = jnp.where(lane == 0, 1.0 - crossing, jnp.where(lane == 1, 1.0, 0.0)).astype(BF16)
    return deep([stacked(q_ref), every_head(hider, heads)])


RATE = math.log2(math.e) / math.sqrt(T)


def part_kernel(places, pos_ref, q_ref, kmap_ref, *rest):
    count = len(places)
    phi_ref, state_ref, top_ref, total_ref, sum_ref = rest[count : count + 5]
    k_s, v_s = rest[count + 5 :]
    _, start = positions_of(pos_ref)
    keys, entry = hold_keys(rest[:count], places, pos_ref, k_s, v_s)
    phi_ref[...], state_ref[...] = key_features(
        slice(None), keys, entry, map_of(kmap_ref[0]), k_s, v_s
    )
    queries = asking(q_ref, (start < 0.0).astype(F32))
    for at in range(0, queries.shape[0], TEACHER):
        rows = slice(at, at + TEACHER)
        scores = nt(queries[rows, :], k_s[...])
        top = jnp.max(scores, axis=-1, keepdims=True)
        weights = jnp.exp2((scores - top) * RATE)
        total = jnp.sum(weights, axis=-1, keepdims=True)
        sum_ref[rows, :] = nn(weights.astype(BF16), v_s[:, :T])
        top_ref[rows, :] = jnp.broadcast_to(top, (TEACHER, T))
        total_ref[rows, :] = jnp.broadcast_to(total, (TEACHER, T))


def main_kernel(places, parts, pos_ref, q_ref, kmap_ref, phi_ref, inner_ref, own_ref, *rest):
    count = len(places)
    blocks = rest[:count]
    done = [rest[count + 5 * i : count + 5 * i + 5] for i in range(parts)]
    rest = rest[count + 5 * parts :]
    payload_ref, dlogit_ref, gn_ref, gkphi_ref, k_s, v_s = rest
    heads = q_ref.shape[1] // T
    row, start = positions_of(pos_ref)
    crossing = (start < 0.0).astype(F32)
    keys, entry = hold_keys(blocks, places, pos_ref, k_s, v_s)
    first = sum(part[0].shape[0] for part in done)
    late, state = key_features(
        slice(first, WINDOW * T), keys[first // T : WINDOW], entry, map_of(kmap_ref[0]), k_s, v_s
    )
    for part in done:
        state = state + part[1][...]
    norms = jnp.transpose(state[:, T:])[0:1, :]
    state = split2(state)

    own_key = lax.broadcasted_iota(jnp.int32, (T, T), 1).astype(F32)
    visible = (own_key <= row) & (own_key >= start)
    seen = every_head(visible.astype(F32), heads)
    bias = every_head(jnp.where(visible, 0.0, NEGATIVE), heads)
    cross = every_head(jnp.broadcast_to(crossing, (T, T)), heads)
    queries = asking(q_ref, crossing)
    own_v = v_s[WINDOW * T :, :]
    teachers = []
    for at in range(0, heads * T, TEACHER):
        rows = slice(at, at + TEACHER)
        scores = nt(queries[rows, :], k_s[first:, :])
        near = scores[:, WINDOW * T - first :] + bias[rows, :]
        far = scores[:, : WINDOW * T - first]
        top = jnp.maximum(
            jnp.max(near, axis=-1, keepdims=True), jnp.max(far, axis=-1, keepdims=True)
        )
        top = jnp.broadcast_to(top, (TEACHER, T))
        for part in done:
            top = jnp.maximum(top, part[2][rows, :])
        near = jnp.exp2((near - top) * RATE)
        far = jnp.exp2((far - top[:, 0:1]) * RATE)
        total = jnp.sum(near, axis=-1, keepdims=True) + jnp.sum(far, axis=-1, keepdims=True)
        summed = nn(deep([far, near]).astype(BF16), v_s[first:, :T])
        for part in done:
            fading = jnp.exp2((part[2][rows, :] - top) * RATE)
            total = total + fading * part[3][rows, :]
            summed = summed + fading * part[4][rows, :]
        teachers.append(summed / total)
    teacher = jnp.concatenate(teachers, axis=0)

    own = own_ref[...]
    own_phi = split2(own)
    phi = phi_ref[...]
    phi_parts = split2(phi)
    near = deep_exact_right(nn, split2(inner_ref[...]), own_v)
    far = product(nn, phi_parts, state)
    inverse = 1.0 / (near[:, T:] + cross * far[:, T:])
    outputs = (near[:, :T] + cross * far[:, :T]) * inverse
    error = outputs - teacher

    grad_numer = error * inverse
    grad_denom = -row_sums(error * outputs) * inverse
    gn_ref[...] = grad_numer
    far_numer = cross * grad_numer
    far_denom = cross * grad_denom
    mixing = (deep_exact_right(nt, split2(grad_numer), own_v[:, :T]) + grad_denom) * seen
    mixing_parts = split2(mixing)
    near = deep_product(nn, mixing_parts, own_phi)
    far = deep_product(nt, split2(far_numer), [part[:, :T] for part in state])
    grad_phi = jnp.concatenate(
        [
            near[:, :T] + far[:, :T] + far_denom * norms[:, :T],
            near[:, T:] + far[:, T:] + far_denom * norms[:, T:],
        ],
        axis=1,
    )
    back = product(tn, phi_parts, split2(jnp.concatenate([far_numer, far_denom], axis=1)))
    backn = jnp.transpose(back[:, T:])[0:1, :]
    gkphi = product(tn, mixing_parts, phi_parts)
    gkphi_ref[...] = gkphi
    dlogit = feature_back(phi, grad_phi)
    dlogit_ref[...] = dlogit
    dlogit_parts = split2(dlogit)
    for h in range(heads):
        at = slice(h * T, h * T + T)
        grad_map = wide_exact_left(tn, q_ref[:, at], [part[at, :] for part in dlogit_parts])
        for quarter in range(4):
            payload_ref[4 * h + quarter, 0:STATE_ROW, :] = grad_map[
                quarter * 32 : quarter * 32 + 32, :
            ]
    for piece in range(32):
        payload_ref[piece, STATE_ROW : STATE_ROW + 8, :] = back[piece * 8 : piece * 8 + 8, :T]

    part = split2(feature_back(own, gkphi))
    grad_map = wide_exact_left(tn, k_s[WINDOW * T :, :T], part)
    back_parts = split2(jnp.concatenate([back[:, :T], back[:, T:] * (1.0 / T)], axis=1))
    at = 0
    for features in [part[0][...] for part in done] + [late]:
        rows = slice(at, at + features.shape[0])
        grad = exact_left(nt, v_s[rows, :], back_parts)
        part = split2(feature_back(features, grad))
        grad_map = grad_map + wide_exact_left(tn, k_s[rows, :T], part)
        at += features.shape[0]
    tail = jnp.concatenate(
        [
            backn[:, :T],
            backn[:, T:],
            jnp.broadcast_to(pos_ref[0:1, 0:1].astype(F32), (1, T)),
            jnp.zeros((1, T), F32),
        ],
        axis=0,
    )
    for piece in range(32):
        payload_ref[piece, KMAP_ROW:PIECE, :] = jnp.concatenate(
            [grad_map[piece * 4 : piece * 4 + 4, :], tail], axis=0
        )


def query_kernel(dlogit_ref, inner_ref, gn_ref, qmap_ref, gq_ref, gv_ref):
    for h in range(qmap_ref.shape[0]):
        at = slice(h * T, h * T + T)
        gq_ref[:, at] = product(nt, split2(dlogit_ref[at, :]), split2(qmap_ref[h]))
    gv_ref[...] = product(tn, split2(inner_ref[...]), split2(gn_ref[...]))


def middle_kernel(me_ref, got_ref, out_ref, norms_ref, state_s):
    pieces = got_ref.shape[0]
    total = got_ref[0]
    for i in range(1, pieces):
        total = total + got_ref[i]
    qmap, kmap = total[0:STATE_ROW, :], total[KMAP_ROW:NORM_ROW, :]
    squares = jnp.sum(qmap * qmap) + jnp.sum(kmap * kmap)
    parts = [part.astype(F32) for part in split3(jnp.full((1, T), squares, F32))]
    tail = jnp.concatenate([kmap] + parts + [jnp.zeros((1, T), F32)], axis=0).astype(BF16)
    qmap = qmap.astype(BF16)
    for j in range(pieces):
        out_ref[j, 0:HIGH_ROW, :] = qmap
        out_ref[j, KEY_ROW:REPLY, :] = tail
    sender = lax.broadcasted_iota(jnp.int32, (pieces, T), 0)
    target = lax.broadcasted_iota(jnp.int32, (pieces, T), 1)
    first = (sender * T).astype(F32) - got_ref[:, INFO_ROW, :]
    links = (sender > target) & (first <= (target * T + (T - 1)).astype(F32))
    reach = links.astype(F32)[:, :pieces].astype(BF16)
    for i in range(8):
        state_s[:, i, :] = exact_left(tn, reach, split3(got_ref[:, STATE_ROW + i, :]))
    high, low = split2(state_s[...])
    out_ref[:, HIGH_ROW:LOW_ROW, :] = high
    out_ref[:, LOW_ROW:KEY_ROW, :] = low
    me = me_ref[0]
    mine = (sender > me) & (first <= (me * T + (T - 1)).astype(F32))
    for half in range(2):
        norms_ref[0:1, half * T : half * T + T] = jnp.sum(
            jnp.where(mine, got_ref[:, NORM_ROW + half, :], 0.0), axis=0, keepdims=True
        )


def last_kernel(pos_ref, got_ref, norms_ref, v_ref, kmap_ref, phi_ref, gkphi_ref, gv_ref, gk_ref, gvo_ref):
    _, start = positions_of(pos_ref)
    last_start = float(T - 1) - pos_ref[0:1, T - 1 : T].astype(F32)
    keeping = (start == last_start).astype(F32)
    pieces = got_ref.shape[0]
    back = [
        jnp.concatenate([got_ref[r, at : at + 8, :] for r in range(pieces)], axis=0)
        for at in (HIGH_ROW, LOW_ROW)
    ]
    phi = phi_ref[...]
    own_v = v_ref[...]
    grad = gkphi_ref[...] + keeping * (exact_left(nt, own_v, back) + norms_ref[...])
    gvo_ref[...] = gv_ref[...] + keeping * product(nn, split2(phi), back)
    gk_ref[...] = product(nt, split2(feature_back(phi, grad)), split2(kmap_ref[0]))


def squares_kernel(tail_ref, out_ref):
    total = jnp.sum(tail_ref[:, KEY_ROW:REPLY, :].astype(F32), axis=0)
    total = jnp.sum(total[SQUARE_ROW - KEY_ROW : SQUARE_ROW - KEY_ROW + 3, :], axis=0)
    out_ref[...] = jnp.broadcast_to(total.reshape(1, 1, T), out_ref.shape)


def scale_kernel(limit, got_ref, squares_ref, qmap_ref, kmap_ref):
    pieces = got_ref.shape[0]
    squared = jnp.sum(squares_ref[:, 0, :], axis=0, keepdims=True)
    factor = jnp.minimum(1.0, limit / (jnp.sqrt(squared) + EPSILON))
    for piece in range(pieces):
        rows = slice(piece % 4 * 32, piece % 4 * 32 + 32)
        qmap_ref[piece // 4, rows, :] = factor * got_ref[piece, 0:HIGH_ROW, :].astype(F32)
        tail = got_ref[piece, KEY_ROW:REPLY, :].astype(F32)
        kmap_ref[0, piece * 4 : piece * 4 + 4, :] = factor * tail[0 : SQUARE_ROW - KEY_ROW, :]


def call(body, name, ins, outs, scratch=(), limit=32):
    return pl.pallas_call(
        body,
        in_specs=[pl.BlockSpec(memory_space=space) for space in ins],
        out_specs=[pl.BlockSpec(memory_space=pltpu.VMEM)] * len(outs),
        out_shape=[
            out if isinstance(out, jax.ShapeDtypeStruct) else jax.ShapeDtypeStruct(out, F32)
            for out in outs
        ],
        scratch_shapes=list(scratch),
        compiler_params=pltpu.CompilerParams(vmem_limit_bytes=limit << 20),
        name=name,
    )


def joined(a, b):
    return lax.pad(a, jnp.zeros((), a.dtype), ((0, b.shape[0], 0), (0, 0, 0))) + lax.pad(
        b, jnp.zeros((), b.dtype), ((a.shape[0], 0, 0), (0, 0, 0))
    )


def on_device(queries, key_vectors, value_vectors, positions, query_map, key_map):
    group = query_map.shape[0]
    pieces = lax.axis_size("seq")
    heads = lax.axis_size("head")
    rows = group * T
    me = lax.axis_index("seq").astype(jnp.int32).reshape(1)
    pos = positions.reshape(1, T)
    kv = joined(key_vectors, value_vectors)
    V = pltpu.VMEM

    def shift(x, k):
        return lax.ppermute(x, "seq", [(i, (i + k) % pieces) for i in range(pieces)])

    def part_of(name, arrays, places):
        size = T * sum(len(held) for held in places)
        return call(
            functools.partial(part_kernel, places),
            name,
            [V] * (3 + len(arrays)),
            [(size, 2 * T), (2 * T, 2 * T), (rows, T), (rows, T), (rows, T)],
            [V((size, 2 * T), BF16), V((size, 2 * T), BF16)],
            24,
        )(pos, queries, key_map, *arrays)

    b4, b8, b1, b7 = (shift(kv, k) for k in (4, 8, 1, 7))
    phi, inner, own = call(
        local_kernel, "local_features", [V] * 5, [(rows, 2 * T), (rows, T), (T, 2 * T)]
    )(pos, queries, key_vectors, query_map, key_map)
    b4, b8, b1, b7 = lax.optimization_barrier((b4, b8, b1, b7))
    near = jnp.concatenate([b4, b8, b1, b7], axis=0)
    near, b4, b1, b7 = lax.optimization_barrier((near, b4, b1, b7))
    far = shift(near, 8)
    n1 = shift(jnp.concatenate([b1, b4], axis=0), 1)
    n2 = shift(jnp.concatenate([b4, b7], axis=0), -1)
    early = list(part_of("early_keys", [near], [(4, 8, 1, 7)]))
    n1, early[1] = lax.optimization_barrier((n1, early[1]))
    n2, far = lax.optimization_barrier((n2, far))
    f1, f2 = shift(n1, 8), shift(n2, 8)
    middle = part_of("middle_keys", [far, n1, n2], [(12, 16, 9, 15), (2, 5), (3, 6)])
    arrays = [near, far, n1, n2, f1, f2, kv]
    places = [(4, 8, 1, 7), (12, 16, 9, 15), (2, 5), (3, 6), (10, 13), (11, 14), (0,)]
    payload, dlogit, grad_numer, gkphi = call(
        functools.partial(main_kernel, places, 2),
        "attention_transfer",
        [V] * (6 + len(arrays) + 10),
        [(pieces, PIECE, T), (rows, T), (rows, T), (T, 2 * T)],
        [V((KEYS, 2 * T), BF16), V((KEYS, 2 * T), BF16)],
        32,
    )(pos, queries, key_map, phi, inner, own, *arrays, *early, *middle)
    gathered = lax.all_to_all(payload, "seq", 0, 0)
    grad_queries, near_values = call(
        query_kernel, "query_gradients", [V] * 4, [(T, rows), (T, T)]
    )(dlogit, inner, grad_numer, query_map)
    reduced, norms = call(
        middle_kernel,
        "sum_pieces",
        [pltpu.SMEM, V],
        [jax.ShapeDtypeStruct((pieces, REPLY, T), BF16), (1, 2 * T)],
        [V((pieces, 8, T), F32)],
    )(me, gathered)
    back = lax.all_to_all(reduced, "seq", 0, 0)
    squares = call(squares_kernel, "head_squares", [V], [(heads, 8, T)])(back)[0]
    squares = lax.all_to_all(squares, "head", 0, 0)
    grad_keys, grad_values = call(last_kernel, "key_gradients", [V] * 8, [(T, T), (T, T)])(
        pos, back, norms, value_vectors, key_map, own, gkphi, near_values
    )
    clip_limit = 0.25 * math.sqrt((group + 1) * heads * T * T)
    query_map_grad, key_map_grad = call(
        functools.partial(scale_kernel, clip_limit),
        "clip_maps",
        [V] * 2,
        [(group, T, T), (1, T, T)],
    )(back, squares)
    return (grad_queries, grad_keys, grad_values, query_map_grad, key_map_grad)


def solution(mesh):
    placed = (
        P("seq", "head"),
        P("seq", "head"),
        P("seq", "head"),
        P("seq"),
        P("head", None, None),
        P("head", None, None),
    )
    return jax.shard_map(
        on_device,
        mesh=mesh,
        in_specs=placed,
        out_specs=(
            P("seq", "head"),
            P("seq", "head"),
            P("seq", "head"),
            P("head", None, None),
            P("head", None, None),
        ),
        check_vma=False,
    )
```
